32 devices in a mesh: dp: 8 (over z, x), tensor: 4 (over y, core).
Axes of the slice: x: 2, y: 2, z: 4, core: 2. Of those that a mesh axis runs over, the one named last changes fastest.
Arguments:
- inputs: bfloat16 [16384, 768], P(('dp', 'tensor')), may hold values from -6 to 6
- layout_cells: int32 [2, 16384], P(None, 'dp'), may hold values from 0 to 31
- page_lengths: int32 [32, 8], P('dp'), may hold values from 1 to 256, 512 in all within a row
- attend_weight: bfloat16 [3, 768, 768], P(None, None, 'tensor'), may hold values from -0.21875 to 0.21875
- attend_shift: bfloat16 [2, 768], P(None, 'tensor'), may hold values from -3 to 3
- merge_weight: bfloat16 [768, 768], P('tensor'), may hold values from -0.875 to 0.875
- merge_shift: bfloat16 [768], replicated, may hold values from -3 to 3
- norm_gains: bfloat16 [2, 768], replicated, may hold values from 0.099609375 to 1.8984375
- norm_shifts: bfloat16 [2, 768], replicated, may hold values from -3 to 3
- expand_weight: bfloat16 [768, 3072], P(None, 'tensor'), may hold values from -0.21875 to 0.21875
- expand_shift: bfloat16 [3072], P('tensor'), may hold values from -3 to 3
- reduce_weight: bfloat16 [3072, 768], P('tensor'), may hold values from -0.109375 to 0.109375
- reduce_shift: bfloat16 [768], replicated, may hold values from -3 to 3
- bias_tables: bfloat16 [2, 12, 32], P(None, 'tensor'), may hold values from -4 to 4
- cotangent: bfloat16 [16384, 768], P(('dp', 'tensor')), may hold values from -6 to 6
Outputs:
- output: bfloat16 [16384, 768], P(('dp', 'tensor'))
- input_grad: bfloat16 [16384, 768], P(('dp', 'tensor'))
- attend_weight_grad: float32 [3, 768, 768], P(None, 'dp', 'tensor')
- attend_shift_grad: float32 [2, 768], P(None, 'tensor')
- merge_weight_grad: float32 [768, 768], P('tensor', 'dp')
- merge_shift_grad: float32 [768], replicated
- norm_gains_grad: float32 [2, 768], replicated
- norm_shifts_grad: float32 [2, 768], replicated
- expand_weight_grad: float32 [768, 3072], P('dp', 'tensor')
- expand_shift_grad: float32 [3072], P('tensor')
- reduce_weight_grad: float32 [3072, 768], P('tensor', 'dp')
- reduce_shift_grad: float32 [768], replicated
- bias_tables_grad: float32 [2, 12, 32], P(None, 'tensor')
The draws below stay inside these ranges and needn't reach their ends.
Inputs may be any that keep to these rules, and one draw needn't show every extreme that they name: `page_lengths`: each row sums to 512; in each row the longest page has exactly 256 tokens.
All inputs are finite; a program needn't handle non-finite values.
Results may differ from the reference program's by a relative error of at most 0.02.
Values may be sent and summed in bfloat16 or wider, within the bound.
A program may use at most 128 MiB of HBM per device.

```python
import math
from functools import partial
import jax
import jax.numpy as jnp
import numpy as np
from jax import lax

D = 768
HEADS = 12
HEAD_DIM = 64
FF = 3072
BUCKETS = 32
WIN = 512
SEGS = 8
WIN_DEV = 4
WINDOWS = 32
TOKENS = 16384
N_DP = 8


def set_ends(drawn, rng, low, largest):
    place = [jax.random.randint(jax.random.fold_in(rng, axis), (), 0, length) for axis, length in enumerate(drawn.shape)]
    widest = drawn.shape.index(max(drawn.shape))
    next_to = place[:widest] + [(place[widest] + 1) % drawn.shape[widest]] + place[widest + 1:]
    return drawn.at[tuple(place)].set(low).at[tuple(next_to)].set(largest)


def block_levels(rng, dims, split, smallest, high):
    def one(dim, blocks):
        heights = jax.random.uniform(jax.random.fold_in(jax.random.fold_in(rng, 6), dim), (blocks,), jnp.float32, smallest / len(split), high / len(split))
        return jnp.repeat(jnp.exp(heights), dims[dim] // blocks).reshape((-1,) + (1,) * (len(dims) - dim - 1))

    factor_of = one(*split[0])
    for cut in split[1:]:
        factor_of = factor_of * one(*cut)
    return factor_of


def split_up(number_of, total, reach, skew):
    portions = [(1 << 20) // math.isqrt(grade ** skew) + 1 for grade in range(2, number_of + 1)]
    rest, given = total - reach - (number_of - 1), [1] * (number_of - 1)
    while rest > 0:
        movable = [i for i in range(number_of - 1) if given[i] < reach]
        pool, budget = sum([portions[i] for i in movable]), rest
        for i in movable:
            extra = min(reach - given[i], max(1, budget * portions[i] // pool), rest)
            given[i] = given[i] + extra
            rest = rest - extra
    return np.array([reach] + given)


def uneven_parts(rng, number_of, total, bound, slope):
    if number_of == 2:
        one = jax.random.randint(rng, (), max(1, total - bound), min(bound, total - 1) + 1)
        return jnp.stack([one, total - one])
    lengths = jnp.asarray(split_up(number_of, total, bound, slope), jnp.int32)
    couples = (number_of - 1) // 2
    giver, receiver = lengths[1:1 + 2 * couples:2], lengths[2:2 + 2 * couples:2]
    slack = jnp.minimum(giver - 1, bound - receiver)
    moved = jax.random.randint(jax.random.fold_in(rng, 1), (couples,), 0, 1 << 20) % (slack + 1)
    lengths = lengths.at[1:1 + 2 * couples:2].set(giver - moved).at[2:2 + 2 * couples:2].set(receiver + moved)
    return lengths[jax.random.permutation(jax.random.fold_in(rng, 2), number_of)]


def noise(rng, extent, scale, bound, split=(), kind=jnp.bfloat16):
    gain = block_levels(rng, extent, split, -0.22, 0.18) if split else 1.0
    array = jax.random.normal(rng, extent, jnp.float32) * scale * gain
    return jnp.minimum(jnp.maximum(array, -bound), bound).astype(kind)


def setup_inputs(seed: int = 0) -> dict:
    splits = jax.random.split(jax.random.key(seed), 16)
    inputs = noise(splits[0], (TOKENS, D), 1.0, 6.0, ((0, 32),))
    layout_cells = set_ends(jax.random.randint(splits[1], (2, TOKENS), 0, BUCKETS), jax.random.fold_in(splits[1], 1), 0, BUCKETS - 1).astype(jnp.int32)
    page_lengths = jax.vmap(lambda own: uneven_parts(own, SEGS, WIN, WIN // 2, 2))(jax.random.split(splits[2], WINDOWS)).reshape((WINDOWS, SEGS)).astype(jnp.int32)
    attend_weight = noise(splits[3], (3, D, D), D ** -0.5, 0.21875, ((2, 4),))
    attend_shift = noise(splits[4], (2, D), 0.5, 3.0, ((1, 4),))
    merge_weight = noise(splits[5], (D, D), (D // 16) ** -0.5, 0.875, ((0, 4),))
    merge_shift = noise(splits[6], (D,), 0.5, 3.0)
    norm_gains = jnp.clip(1.0 + 0.18 * jax.random.normal(splits[7], (2, D), jnp.float32), 0.099609375, 1.8984375).astype(jnp.bfloat16)
    norm_shifts = noise(splits[8], (2, D), 0.5, 3.0)
    expand_weight = noise(splits[9], (D, FF), D ** -0.5, 0.21875, ((1, 4),))
    expand_shift = noise(splits[10], (FF,), 0.5, 3.0, ((0, 4),))
    reduce_weight = noise(splits[11], (FF, D), FF ** -0.5, 0.109375, ((0, 4),))
    reduce_shift = noise(splits[12], (D,), 0.5, 3.0)
    bias_tables = noise(splits[13], (2, HEADS, BUCKETS), 1.0, 4.0, ((1, 4),))
    cotangent = noise(splits[14], (TOKENS, D), 1.0, 6.0, ((0, 32),))
    return {"inputs": inputs, "layout_cells": layout_cells, "page_lengths": page_lengths, "attend_weight": attend_weight, "attend_shift": attend_shift, "merge_weight": merge_weight, "merge_shift": merge_shift, "norm_gains": norm_gains, "norm_shifts": norm_shifts, "expand_weight": expand_weight, "expand_shift": expand_shift, "reduce_weight": reduce_weight, "reduce_shift": reduce_shift, "bias_tables": bias_tables, "cotangent": cotangent}


EPSILON = 1e-05
MASKED = -1000000000.0
HIGHEST = lax.Precision.HIGHEST

@jax.custom_vjp
def low(v):
    return lax.optimization_barrier(v.astype(jnp.bfloat16)).astype(jnp.float32)

@jax.custom_vjp
def low_back(v):
    return v

def low_keep(v):
    return (low(v), None)

def low_pass(kept, grad):
    return (grad,)

def back_keep(v):
    return (v, None)

def back_low(kept, grad):
    return (low(grad),)
low.defvjp(low_keep, low_pass)
low_back.defvjp(back_keep, back_low)

def layer_norm(signal, gain_vec, shift_vec):
    center = signal - lax.optimization_barrier(jnp.mean(signal, axis=-1, keepdims=True))
    spread = lax.optimization_barrier(jnp.mean(center * center, axis=-1, keepdims=True))
    return center * lax.rsqrt(spread + EPSILON) * gain_vec + shift_vec

def window_layout(coords_win, lengths_win):
    window_len = coords_win.shape[1]
    bounds = jnp.cumsum(lengths_win).astype(jnp.int32)
    places = jnp.arange(window_len, dtype=jnp.int32)
    segment = lax.optimization_barrier(jnp.sum((places[:, None] >= bounds[None, :]).astype(jnp.int32), axis=1))
    same_seg = segment[:, None] == segment[None, :]
    offsets = jnp.clip(coords_win[:, :, None] - coords_win[:, None, :] + BUCKETS // 2, 0, BUCKETS - 1)
    return (same_seg, offsets.astype(jnp.int32))

def attend(tables_all, pieces):
    queries, key_rows, value_rows, coords_win, lengths_win = pieces
    same_seg, offsets = window_layout(coords_win, lengths_win)
    raw_scores = jnp.einsum('ihd,jhd->hij', queries, key_rows, precision=HIGHEST) * HEAD_DIM ** (-0.5)
    position = tables_all[0][:, offsets[0]] + tables_all[1][:, offsets[1]]
    scores = low_back(raw_scores + position)
    scores = jnp.where(same_seg[None], scores, MASKED)
    soft_probs = jax.nn.softmax(scores, axis=-1)
    return jnp.einsum('hij,jhd->ihd', low(soft_probs), value_rows, precision=HIGHEST)

def layer(weights_all, inputs, coord_rows, length_rows):
    attend_weight, attend_shift, merge_weight, merge_shift, norm_gains, norm_shifts, expand_weight, expand_shift, reduce_weight, reduce_shift, bias_tables = weights_all
    windows = length_rows.shape[0]
    project = jnp.einsum('td,mde->mte', inputs, attend_weight, precision=HIGHEST)
    triple_shift = jnp.stack([attend_shift[0], jnp.zeros_like(attend_shift[0]), attend_shift[1]])
    packed_rows = low(low_back(project + triple_shift[:, None, :]))
    heads_form = packed_rows.reshape(3, windows, WIN, HEADS, HEAD_DIM)
    context = lax.map(jax.checkpoint(partial(attend, bias_tables)), (heads_form[0], heads_form[1], heads_form[2], coord_rows, length_rows))
    context = low(low_back(context.reshape(windows * WIN, D)))
    attended = low_back(jnp.dot(context, merge_weight, precision=HIGHEST))
    resid_one = inputs + attended + merge_shift
    normed = layer_norm(resid_one, norm_gains[0], norm_shifts[0])
    pre_act = low_back(jnp.dot(low(normed), expand_weight, precision=HIGHEST) + expand_shift)
    activation = low(jax.nn.gelu(pre_act, approximate=False))
    reduced = low_back(jnp.dot(activation, reduce_weight, precision=HIGHEST))
    return layer_norm(normed + reduced + reduce_shift, norm_gains[1], norm_shifts[1])

def reference(inputs, layout_cells, page_lengths, attend_weight, attend_shift, merge_weight, merge_shift, norm_gains, norm_shifts, expand_weight, expand_shift, reduce_weight, reduce_shift, bias_tables, cotangent):
    weights_all = tuple((member.astype(jnp.float32) for member in (attend_weight, attend_shift, merge_weight, merge_shift, norm_gains, norm_shifts, expand_weight, expand_shift, reduce_weight, reduce_shift, bias_tables)))
    group_rows = WIN_DEV * WIN
    input_groups = inputs.astype(jnp.float32).reshape(N_DP, group_rows, D)
    cot_groups = cotangent.astype(jnp.float32).reshape(N_DP, group_rows, D)
    coord_groups = jnp.transpose(layout_cells.reshape(2, N_DP, WIN_DEV, WIN), (1, 2, 0, 3))
    length_groups = page_lengths.reshape(N_DP, WIN_DEV, SEGS)

    def group_step(totals, group_data):
        input_rows, coord_rows, length_rows, cot_rows = group_data

        def forward(params_now, rows_now):
            return layer(params_now, rows_now, coord_rows, length_rows)
        result, backward = jax.vjp(forward, weights_all, input_rows)
        param_grads, row_grads = backward(cot_rows)
        totals = jax.tree.map(jnp.add, totals, param_grads)
        return (totals, (result.astype(jnp.bfloat16), row_grads.astype(jnp.bfloat16)))
    zero_grads = jax.tree.map(jnp.zeros_like, weights_all)
    totals, (outputs, input_grads) = lax.scan(group_step, zero_grads, (input_groups, coord_groups, length_groups, cot_groups))
    return (outputs.reshape(TOKENS, D), input_grads.reshape(TOKENS, D), totals[0], totals[1], totals[2], totals[3], totals[4], totals[5], totals[6], totals[7], totals[8], totals[9], totals[10])
```

```python
import math

import jax
import jax.numpy as jnp
from jax import lax
from jax.experimental import pallas as pl
from jax.experimental.pallas import tpu as pltpu
from jax.sharding import PartitionSpec as P

HEAD_DIM = 64
BUCKETS = 32
EPSILON = 1e-05
MASKED = -1000000000.0
BF = jnp.bfloat16
F32 = jnp.float32
VMEM_LIMIT = 60 * 1024 * 1024


def mm(a, b, da, db):
    return lax.dot_general(a, b, (((da,), (db,)), ((), ())), preferred_element_type=F32)


def nn(a, b):
    return mm(a, b, 1, 0)


def nt(a, b):
    return mm(a, b, 1, 1)


def tn(a, b):
    return mm(a, b, 0, 0)


def iota(shape, dim):
    return lax.broadcasted_iota(jnp.int32, shape, dim)


def page_scalars(pages_ref, half):
    total = jnp.int32(0)
    begin = jnp.int32(0)
    bounds = []
    for k in range(pages_ref.shape[1]):
        length = pages_ref[0, k]
        begin = begin + jnp.where(length == half, total, 0)
        total = total + length
        bounds.append(total)
    return begin, bounds


def page_numbers(places, bounds):
    number = jnp.zeros(places.shape, jnp.int32)
    for bound in bounds:
        number = number + (places >= bound).astype(jnp.int32)
    return number


def half_lanes(which):
    return ((iota((1, 128), 1) // HEAD_DIM) == which).astype(BF)


def norm_stats(signal):
    mean = jnp.mean(signal, axis=1, keepdims=True)
    center = signal - mean
    spread = jnp.mean(center * center, axis=1, keepdims=True)
    scale = lax.rsqrt(spread + EPSILON)
    return center * scale, scale


def norm_back(grad, hat, scale, gain):
    scaled = grad * gain
    return scale * (
        scaled
        - jnp.mean(scaled, axis=1, keepdims=True)
        - hat * jnp.mean(scaled * hat, axis=1, keepdims=True)
    )


def attend_forward_kernel(
    pages_ref, x_ref, cells_ref, aw_ref, shift_ref, pt_ref, mw_ref, ms_ref, gain_ref, nshift_ref,
    xr_ref, hot_ref, q_ref, k_ref, v_ref, p_ref, ctx_ref, nb_ref, hat_ref, scale_ref, acc_ref,
):
    step = pl.program_id(0)
    rows = x_ref.shape[0]
    half = rows // 2
    begin, bounds = page_scalars(pages_ref, half)

    @pl.when(step == 0)
    def _():
        perm = (iota((rows, rows), 1) == ((iota((rows, rows), 0) + begin) & (rows - 1))).astype(BF)
        xr_ref[...] = nn(perm, x_ref[...]).astype(BF)
        bucket = iota((BUCKETS, rows), 0)
        one = (cells_ref[0:1, :] == bucket).astype(BF)
        two = (cells_ref[1:2, :] == bucket).astype(BF)
        hot_ref[...] = nt(perm, jnp.concatenate([one, two, one, two], axis=0)).astype(BF)
        acc_ref[...] = jnp.zeros_like(acc_ref)

    local = shift_ref.shape[2]
    heads = local // HEAD_DIM
    for out_ref in (q_ref, k_ref, v_ref):
        out_ref[0, :, local:] = jnp.zeros((rows, 256 - local), BF)
    queries = (nn(xr_ref[...], aw_ref[0, 0]) + shift_ref[0, 0:1, :].astype(F32)).astype(BF)
    q_ref[0, :, :local] = queries * jnp.asarray(HEAD_DIM ** -0.5, BF)
    k_ref[0, :, :local] = nn(xr_ref[...], aw_ref[0, 1]).astype(BF)
    v_ref[0, :, :local] = (
        nn(xr_ref[...], aw_ref[0, 2]) + shift_ref[0, 1:2, :].astype(F32)
    ).astype(BF)
    left = nn(hot_ref[:, : 2 * BUCKETS], pt_ref[0]).astype(BF)
    col = page_numbers((iota((half, 1), 0) + (half + begin)) & (rows - 1), bounds)
    row = page_numbers((iota((1, half), 1) + (half + begin)) & (rows - 1), bounds)
    same = col == row
    for block in range(2):
        at = slice(block * half, (block + 1) * half)
        for pair in range(2):
            lanes = slice(pair * 128, (pair + 1) * 128)
            key_side = jnp.concatenate([k_ref[0, at, lanes], hot_ref[at, :]], axis=1)
            total = None
            for which in range(min(2, heads - 2 * pair)):
                keep = half_lanes(which)
                query_side = jnp.concatenate(
                    [q_ref[0, at, lanes] * keep, left[at, lanes] * keep], axis=1
                )
                scores = nt(key_side, query_side)
                if block == 1:
                    scores = jnp.where(same, scores, MASKED)
                weights = jnp.exp(scores - jnp.max(scores, axis=0, keepdims=True))
                probs = (weights * (1.0 / jnp.sum(weights, axis=0, keepdims=True))).astype(BF)
                p_ref[0, (2 * pair + which) * 2 + block] = probs
                part = tn(probs, v_ref[0, at, lanes]) * keep.astype(F32)
                total = part if total is None else total + part
            ctx_ref[0, at, lanes] = total.astype(BF)
    acc_ref[...] += nn(ctx_ref[0, :, :local], mw_ref[0])

    @pl.when(step == pl.num_programs(0) - 1)
    def _():
        resid = xr_ref[...].astype(F32) + acc_ref[...] + ms_ref[...].astype(F32)
        hat, scale = norm_stats(resid)
        hat_ref[...] = hat
        scale_ref[...] = scale
        normed = hat * gain_ref[0:1, :].astype(F32) + nshift_ref[0:1, :].astype(F32)
        nb_ref[...] = normed.astype(BF)


def hidden_forward_kernel(
    pages_ref, nb_ref, hat_ref, gain_ref, nshift_ref, ew_ref, es_ref, rw_ref, rs_ref, cot_ref,
    act_ref, slope_ref, out_ref, gtwo_ref, small_ref, acc_ref,
):
    step = pl.program_id(0)
    rows = nb_ref.shape[0]
    pre = nn(nb_ref[...], ew_ref[0]) + es_ref[0].astype(F32)
    gate = 0.5 * (1.0 + lax.erf(pre * (0.5 ** 0.5)))
    act_ref[0] = (pre * gate).astype(BF)
    slope_ref[0] = (
        gate + pre * (jnp.exp(-0.5 * (pre * pre)) * (1.0 / math.sqrt(2.0 * math.pi)))
    ).astype(BF)
    part = nn(act_ref[0], rw_ref[0])

    @pl.when(step == 0)
    def _():
        acc_ref[...] = part

    @pl.when(step > 0)
    def _():
        acc_ref[...] += part

    @pl.when(step == pl.num_programs(0) - 1)
    def _():
        begin, _unused = page_scalars(pages_ref, rows // 2)
        normed = hat_ref[...] * gain_ref[0:1, :].astype(F32) + nshift_ref[0:1, :].astype(F32)
        resid = normed + acc_ref[...] + rs_ref[...].astype(F32)
        hat, scale = norm_stats(resid)
        gain = gain_ref[1:2, :].astype(F32)
        result = (hat * gain + nshift_ref[1:2, :].astype(F32)).astype(BF)
        perm = (iota((rows, rows), 1) == ((iota((rows, rows), 0) + begin) & (rows - 1))).astype(BF)
        out_ref[...] = tn(perm, result).astype(BF)
        cot = nn(perm, cot_ref[...])
        grad = norm_back(cot, hat, scale, gain)
        gtwo_ref[...] = grad
        small_ref[0:1, :] = jnp.sum(cot * hat, axis=0, keepdims=True)
        small_ref[1:2, :] = jnp.sum(cot, axis=0, keepdims=True)
        small_ref[2:3, :] = jnp.sum(grad, axis=0, keepdims=True)
        small_ref[3:8, :] = jnp.zeros((5, small_ref.shape[1]), F32)


def hidden_backward_kernel(
    gtwo_ref, act_ref, slope_ref, rw_ref, ew_ref, nb_ref, hat_ref, scale_ref, gain_ref,
    grw_ref, gew_ref, ges_ref, gone_ref, small_ref, acc_ref, gb_ref,
):
    step = pl.program_id(0)

    @pl.when(step == 0)
    def _():
        gb_ref[...] = gtwo_ref[...].astype(BF)
        acc_ref[...] = gtwo_ref[...]

    grad_pre = (nt(gb_ref[...], rw_ref[0]) * slope_ref[0].astype(F32)).astype(BF)
    ges_ref[0] = jnp.sum(grad_pre.astype(F32), axis=0, keepdims=True)
    grw_ref[0] = tn(gb_ref[...], act_ref[0]).astype(BF)
    gew_ref[0] = tn(nb_ref[...], grad_pre).astype(BF)
    acc_ref[...] += nt(grad_pre, ew_ref[0])

    @pl.when(step == pl.num_programs(0) - 1)
    def _():
        grad = acc_ref[...]
        hat = hat_ref[...]
        gone = norm_back(grad, hat, scale_ref[...], gain_ref[0:1, :].astype(F32))
        gone_ref[...] = gone
        small_ref[0:1, :] = jnp.sum(grad * hat, axis=0, keepdims=True)
        small_ref[1:2, :] = jnp.sum(grad, axis=0, keepdims=True)
        small_ref[2:3, :] = jnp.sum(gone, axis=0, keepdims=True)
        small_ref[3:8, :] = jnp.zeros((5, small_ref.shape[1]), F32)


def attend_backward_kernel(
    pages_ref, gone_ref, mw_ref, ctx_ref, aw_ref, q_ref, k_ref, v_ref, p_ref, xr_ref, hot_ref,
    gmw_ref, gaw_ref, gsh_ref, gpair_ref, gin_ref, acc_ref, gb_ref, gc_ref, dq_ref, dk_ref, dv_ref, e_ref,
):
    step = pl.program_id(0)
    rows = gone_ref.shape[0]
    half = rows // 2
    local = mw_ref.shape[1]
    heads = local // HEAD_DIM

    @pl.when(step == 0)
    def _():
        gb_ref[...] = gone_ref[...].astype(BF)
        acc_ref[...] = gone_ref[...]
        gc_ref[:, local:] = jnp.zeros((rows, 256 - local), BF)

    gc_ref[:, :local] = nt(gb_ref[...], mw_ref[0]).astype(BF)
    gmw_ref[0] = tn(gb_ref[...], ctx_ref[0, :, :local]).astype(BF)
    for block in range(2):
        at = slice(block * half, (block + 1) * half)
        for pair in range(2):
            lanes = slice(pair * 128, (pair + 1) * 128)
            key_side = jnp.concatenate([k_ref[0, at, lanes], hot_ref[at, :]], axis=1)
            sums = None
            for which in range(min(2, heads - 2 * pair)):
                keep = half_lanes(which)
                wide = keep.astype(F32)
                probs = p_ref[0, (2 * pair + which) * 2 + block]
                grad_probs = nt(v_ref[0, at, lanes] * keep, gc_ref[at, lanes])
                soft = probs.astype(F32)
                inner = jnp.sum(soft * grad_probs, axis=0, keepdims=True)
                grad_scores = (soft * (grad_probs - inner)).astype(BF)
                both = tn(grad_scores, key_side)
                parts = (
                    both[:, :128] * wide,
                    both[:, 128:] * wide,
                    nn(grad_scores, q_ref[0, at, lanes]) * wide,
                    nn(probs, gc_ref[at, lanes]) * wide,
                )
                sums = parts if sums is None else tuple(a + b for a, b in zip(sums, parts))
            dq_ref[at, lanes] = (sums[0] * (HEAD_DIM ** -0.5)).astype(BF)
            e_ref[at, lanes] = sums[1].astype(BF)
            dk_ref[at, lanes] = sums[2].astype(BF)
            dv_ref[at, lanes] = sums[3].astype(BF)
    for m, d_ref in enumerate((dq_ref, dk_ref, dv_ref)):
        piece = d_ref[:, :local]
        gaw_ref[0, m] = tn(xr_ref[...], piece).astype(BF)
        acc_ref[...] += nt(piece, aw_ref[0, m])
    gsh_ref[0, 0:1, :] = jnp.sum(dq_ref[:, :local].astype(F32), axis=0, keepdims=True)
    gsh_ref[0, 1:2, :] = jnp.sum(dv_ref[:, :local].astype(F32), axis=0, keepdims=True)
    gpair_ref[0] = tn(hot_ref[:, : 2 * BUCKETS], e_ref[...])

    @pl.when(step == pl.num_programs(0) - 1)
    def _():
        begin, _unused = page_scalars(pages_ref, half)
        perm = (iota((rows, rows), 1) == ((iota((rows, rows), 0) + begin) & (rows - 1))).astype(BF)
        gin_ref[...] = tn(perm, acc_ref[...].astype(BF)).astype(BF)


def whole(shape):
    return pl.BlockSpec(shape, lambda i, *_: (0,) * len(shape))


def slot(shape, order=None):
    pick = order if order is not None else (lambda i: i)
    return pl.BlockSpec((1,) + shape, lambda i, *_: (pick(i),) + (0,) * len(shape))


def late_first(i):
    return 3 - 2 * i + 3 * (i // 2)


def swap(value, axis, size, bit):
    return lax.ppermute(value, axis, [(i, i ^ bit) for i in range(size)])


def gather_slots(shard):
    core = swap(shard, "tensor", 4, 1)
    far = swap(shard, "tensor", 4, 2)
    far_core = swap(far, "tensor", 4, 1)
    return jnp.stack([shard, core, far, far_core])


def reduce_slots(partial_sums, dp):
    add = lambda a, b: (a.astype(F32) + b.astype(F32))
    got = swap(partial_sums[1::2], "tensor", 4, 1)
    two = add(partial_sums[0::2], got).astype(BF)
    got = swap(two[1], "tensor", 4, 2)
    one = add(two[0], got)
    lead = one.shape[:-2]
    rows, cols = one.shape[-2:]
    bits = dp.bit_length() - 1
    one = one.reshape(lead + (2,) * bits + (rows // dp, cols))
    me = lax.axis_index("dp")
    for bit in range(bits):
        axis = one.ndim - 3
        mine = (me >> bit) & 1
        keep = lax.dynamic_index_in_dim(one, mine, axis, keepdims=False)
        send = lax.dynamic_index_in_dim(one, 1 - mine, axis, keepdims=False).astype(BF)
        one = add(keep, swap(send, "dp", dp, 1 << bit))
    return one


def on_device(
    dp,
    inputs,
    layout_cells,
    page_lengths,
    attend_weight,
    attend_shift,
    merge_weight,
    merge_shift,
    norm_gains,
    norm_shifts,
    expand_weight,
    expand_shift,
    reduce_weight,
    reduce_shift,
    bias_tables,
    cotangent,
):
    rows, width = inputs.shape
    local = attend_weight.shape[2]
    heads = bias_tables.shape[1]
    hidden = expand_weight.shape[1]
    me = lax.axis_index("tensor")
    pages = lax.dynamic_slice_in_dim(page_lengths, me, 1, 0)
    cells = lax.dynamic_slice_in_dim(layout_cells, me * rows, rows, 1)

    spot = jnp.arange(BUCKETS, dtype=jnp.int32)
    bucket_of = jnp.clip(spot[:, None] - spot[None, :] + BUCKETS // 2, 0, BUCKETS - 1)
    folding = (bucket_of[:, :, None] == spot[None, None, :]).astype(F32)
    pairs = jnp.einsum("xyb,ahb->ahxy", folding, bias_tables.astype(F32))
    own_pt = jnp.zeros((2, BUCKETS, 4, 2, BUCKETS), F32)
    for a in range(2):
        own_pt = own_pt.at[a, :, :heads, a, :].set(jnp.transpose(pairs[a], (1, 0, 2)))
    own_pt = own_pt.reshape(2 * BUCKETS, 256).astype(BF)

    pt = gather_slots(own_pt)
    shift = gather_slots(attend_shift)
    es = gather_slots(expand_shift.reshape(1, hidden))
    aw = gather_slots(attend_weight)
    mw = gather_slots(merge_weight)
    ew = gather_slots(expand_weight)
    rw = gather_slots(reduce_weight)
    ms = merge_shift.reshape(1, width)
    rs = reduce_shift.reshape(1, width)

    sds = jax.ShapeDtypeStruct
    smem = pl.BlockSpec(memory_space=pltpu.SMEM)
    params = pltpu.CompilerParams(vmem_limit_bytes=VMEM_LIMIT)
    xr, hot, q, k, v, p, ctx, nb, hat, scale = pl.pallas_call(
        attend_forward_kernel,
        grid=(4,),
        in_specs=[
            smem, whole((rows, width)), whole((2, rows)), slot((3, width, local)), slot((2, local)),
            slot((2 * BUCKETS, 256)), slot((local, width)), whole((1, width)), whole((2, width)),
            whole((2, width)),
        ],
        out_specs=[
            whole((rows, width)), whole((rows, 128)), slot((rows, 256)), slot((rows, 256)),
            slot((rows, 256)), slot((2 * heads, rows // 2, rows // 2)), slot((rows, 256)),
            whole((rows, width)), whole((rows, width)), whole((rows, 1)),
        ],
        out_shape=[
            sds((rows, width), BF), sds((rows, 128), BF), sds((4, rows, 256), BF),
            sds((4, rows, 256), BF), sds((4, rows, 256), BF),
            sds((4, 2 * heads, rows // 2, rows // 2), BF), sds((4, rows, 256), BF),
            sds((rows, width), BF), sds((rows, width), F32), sds((rows, 1), F32),
        ],
        scratch_shapes=[pltpu.VMEM((rows, width), F32)],
        compiler_params=params,
    )(pages, inputs, cells, aw, shift, pt, mw, ms, norm_gains, norm_shifts)

    act, slope, output, gtwo, small_two = pl.pallas_call(
        hidden_forward_kernel,
        grid=(4,),
        in_specs=[
            smem, whole((rows, width)), whole((rows, width)), whole((2, width)), whole((2, width)),
            slot((width, hidden)), slot((1, hidden)), slot((hidden, width)), whole((1, width)),
            whole((rows, width)),
        ],
        out_specs=[
            slot((rows, hidden)), slot((rows, hidden)), whole((rows, width)), whole((rows, width)),
            whole((8, width)),
        ],
        out_shape=[
            sds((4, rows, hidden), BF), sds((4, rows, hidden), BF), sds((rows, width), BF),
            sds((rows, width), F32), sds((8, width), F32),
        ],
        scratch_shapes=[pltpu.VMEM((rows, width), F32)],
        compiler_params=params,
    )(pages, nb, hat, norm_gains, norm_shifts, ew, es, rw, rs, cotangent)

    late = late_first
    grw, gew, ges, gone, small_one = pl.pallas_call(
        hidden_backward_kernel,
        grid=(4,),
        in_specs=[
            whole((rows, width)), slot((rows, hidden), late), slot((rows, hidden), late),
            slot((hidden, width), late), slot((width, hidden), late), whole((rows, width)),
            whole((rows, width)), whole((rows, 1)), whole((2, width)),
        ],
        out_specs=[
            slot((width, hidden), late), slot((width, hidden), late), slot((1, hidden), late),
            whole((rows, width)), whole((8, width)),
        ],
        out_shape=[
            sds((4, width, hidden), BF), sds((4, width, hidden), BF), sds((4, 1, hidden), F32),
            sds((rows, width), F32), sds((8, width), F32),
        ],
        scratch_shapes=[pltpu.VMEM((rows, width), F32), pltpu.VMEM((rows, width), BF)],
        compiler_params=params,
    )(gtwo, act, slope, rw, ew, nb, hat, scale, norm_gains)

    gmw, gaw, gsh, gpair, input_grad = pl.pallas_call(
        attend_backward_kernel,
        grid=(4,),
        in_specs=[
            smem, whole((rows, width)), slot((local, width), late), slot((rows, 256), late),
            slot((3, width, local), late), slot((rows, 256), late), slot((rows, 256), late),
            slot((rows, 256), late), slot((2 * heads, rows // 2, rows // 2), late),
            whole((rows, width)), whole((rows, 128)),
        ],
        out_specs=[
            slot((width, local), late), slot((3, width, local), late), slot((2, local), late),
            slot((2 * BUCKETS, 256), late), whole((rows, width)),
        ],
        out_shape=[
            sds((4, width, local), BF), sds((4, 3, width, local), BF), sds((4, 2, local), F32),
            sds((4, 2 * BUCKETS, 256), F32), sds((rows, width), BF),
        ],
        scratch_shapes=[
            pltpu.VMEM((rows, width), F32), pltpu.VMEM((rows, width), BF),
            pltpu.VMEM((rows, 256), BF), pltpu.VMEM((rows, 256), BF), pltpu.VMEM((rows, 256), BF),
            pltpu.VMEM((rows, 256), BF), pltpu.VMEM((rows, 256), BF),
        ],
        compiler_params=params,
    )(pages, gone, mw, ctx, aw, q, k, v, p, xr, hot)

    grad_rw = reduce_slots(grw, dp).T
    grad_ew = reduce_slots(gew, dp)
    grad_mw = reduce_slots(gmw, dp).T
    grad_aw = reduce_slots(gaw, dp)

    split = gpair.reshape(4, 2, BUCKETS, 4, 2, BUCKETS)
    grad_pairs = jnp.stack([split[:, a, :, :heads, a, :] for a in range(2)], axis=1)
    grad_tables = jnp.einsum("raxhy,xyb->rahb", grad_pairs, folding, precision=lax.Precision.HIGHEST)
    spare = -(2 * local + hidden + 2 * heads * BUCKETS) % width
    own = jnp.concatenate(
        [
            gsh.reshape(4, -1),
            ges.reshape(4, -1),
            grad_tables.reshape(4, -1),
            jnp.zeros((4, spare), F32),
        ],
        axis=1,
    ).reshape(4, -1, width)
    shared = jnp.concatenate([small_one[:3], small_two[:3]], axis=0)
    lines = own.shape[1]
    for bit, take in ((1, 2), (2, 1)):
        got = swap(jnp.concatenate([shared, own[1::2].reshape(-1, width)], axis=0), "tensor", 4, bit)
        shared = shared + got[:6]
        own = own[0::2] + got[6:].reshape(take, lines, width)
    both = jnp.concatenate([shared, own[0]], axis=0)
    for bit in range(dp.bit_length() - 1):
        both = both + swap(both, "dp", dp, 1 << bit)
    flat = both[6:].reshape(-1)
    cut = 2 * local + hidden
    return (
        output,
        input_grad,
        grad_aw,
        flat[: 2 * local].reshape(2, local),
        grad_mw,
        both[2],
        jnp.stack([both[0], both[3]]),
        jnp.stack([both[1], both[4]]),
        grad_ew,
        flat[2 * local : cut],
        grad_rw,
        both[5],
        flat[cut : cut + 2 * heads * BUCKETS].reshape(2, heads, BUCKETS),
    )


def solution(mesh):
    in_specs = (
        P(("dp", "tensor"), None),
        P(None, "dp"),
        P("dp", None),
        P(None, None, "tensor"),
        P(None, "tensor"),
        P("tensor", None),
        P(),
        P(),
        P(),
        P(None, "tensor"),
        P("tensor"),
        P("tensor", None),
        P(),
        P(None, "tensor", None),
        P(("dp", "tensor"), None),
    )
    out_specs = (
        P(("dp", "tensor"), None),
        P(("dp", "tensor"), None),
        P(None, "dp", "tensor"),
        P(None, "tensor"),
        P("tensor", "dp"),
        P(),
        P(),
        P(),
        P("dp", "tensor"),
        P("tensor"),
        P("tensor", "dp"),
        P(),
        P(None, "tensor", None),
    )

    def run(*arrays):
        return on_device(mesh.shape["dp"], *arrays)

    return jax.shard_map(
        run, mesh=mesh, in_specs=in_specs, out_specs=out_specs, check_vma=False
    )
```

```python
import math

import jax
import jax.numpy as jnp
from jax import lax
from jax.experimental import pallas as pl
from jax.experimental.pallas import tpu as pltpu
from jax.sharding import PartitionSpec as P

HEAD_DIM = 64
BUCKETS = 32
EPSILON = 1e-05
MASKED = -1000000000.0
BF = jnp.bfloat16
F32 = jnp.float32
VMEM_LIMIT = 60 * 1024 * 1024


def mm(a, b, da, db):
    return lax.dot_general(a, b, (((da,), (db,)), ((), ())), preferred_element_type=F32)


def nn(a, b):
    return mm(a, b, 1, 0)


def nt(a, b):
    return mm(a, b, 1, 1)


def tn(a, b):
    return mm(a, b, 0, 0)


def iota(shape, dim):
    return lax.broadcasted_iota(jnp.int32, shape, dim)


def page_scalars(pages_ref, line, half):
    total = jnp.int32(0)
    begin = jnp.int32(0)
    bounds = []
    for k in range(pages_ref.shape[1]):
        length = pages_ref[line, k]
        begin = begin + jnp.where(length == half, total, 0)
        total = total + length
        bounds.append(total)
    return begin, bounds


def page_numbers(places, bounds):
    number = jnp.zeros(places.shape, jnp.int32)
    for bound in bounds:
        number = number + (places >= bound).astype(jnp.int32)
    return number


def half_lanes(which):
    return ((iota((1, 128), 1) // HEAD_DIM) == which).astype(BF)


def norm_stats(signal):
    mean = jnp.mean(signal, axis=1, keepdims=True)
    center = signal - mean
    spread = jnp.mean(center * center, axis=1, keepdims=True)
    scale = lax.rsqrt(spread + EPSILON)
    return center * scale, scale


def norm_back(grad, hat, scale, gain):
    scaled = grad * gain
    return scale * (
        scaled
        - jnp.mean(scaled, axis=1, keepdims=True)
        - hat * jnp.mean(scaled * hat, axis=1, keepdims=True)
    )


MESH = pl.DeviceIdType.MESH
SMALL_ROWS = 16


class Net:
    def __init__(self, bits):
        t = lax.axis_index("tensor")
        d = lax.axis_index("dp")
        self.t = t
        self.core = {"tensor": t + 1 - 2 * (t % 2)}
        self.y = {"tensor": (t + 2) % 4}
        self.bit = [(d // 2 ** b) % 2 for b in bits]
        self.dp = [{"dp": d + 2 ** b * (1 - 2 * k)} for b, k in zip(bits, self.bit)]


def remote(source, target, sems, index, partner):
    return pltpu.make_async_remote_copy(
        src_ref=source,
        dst_ref=target,
        send_sem=sems.at[0, index],
        recv_sem=sems.at[1, index],
        device_id=partner,
        device_id_type=MESH,
    )


def rows_at(ref, start, count):
    return ref.at[pl.ds(pl.multiple_of(start, 16), count), :]


class Piece:
    def __init__(self, net, number, own, slots, start, count, x_first, sems):
        self.net, self.number, self.own, self.slots = net, number, own, slots
        self.start, self.count, self.x_first = start, count, x_first
        self.y_sems, self.one_sems, self.two_sems, self.core_sems = sems
        self.first, self.second = (0, 1) if x_first else (1, 0)

    def quarter(self, ref, flip):
        net = self.net
        fast = net.bit[self.first]
        if flip:
            fast = 1 - fast
        index = net.bit[self.second] * 2 + fast
        return rows_at(ref, self.start + index * (self.count // 4), self.count // 4)

    def half(self, ref, flip):
        slow = self.net.bit[self.second]
        if flip:
            slow = 1 - slow
        return rows_at(ref, self.start + slow * (self.count // 2), self.count // 2)

    def full(self, ref):
        return rows_at(ref, self.start, self.count)

    def over_y(self):
        return remote(
            self.quarter(self.own, False), self.quarter(self.slots(2), False),
            self.y_sems, self.number, self.net.y,
        )

    def hop_one(self, flip=False):
        here = self.quarter(self.slots(2), flip)
        return remote(here, here, self.one_sems, self.number, self.net.dp[self.first])

    def hop_two(self, flip=False):
        here = self.half(self.slots(2), flip)
        return remote(here, here, self.two_sems, self.number, self.net.dp[self.second])

    def to_core(self):
        return remote(
            self.full(self.slots(2)), self.full(self.slots(3)),
            self.core_sems, self.number, self.net.core,
        )

    def event(self, stage):
        if stage == 0:
            self.over_y().start()
        elif stage == 1:
            self.over_y().wait_recv()
            self.hop_one().start()
        elif stage == 2:
            self.hop_one(True).wait_recv()
            self.hop_two().start()
        elif stage == 3:
            self.hop_two(True).wait_recv()
            self.to_core().start()
        elif stage == 4:
            self.to_core().wait_recv()
        else:
            self.over_y().wait_send()
            self.hop_one().wait_send()
            self.hop_two().wait_send()
            self.to_core().wait_send()


def at_step(index, table):
    for value, actions in table.items():

        @pl.when(index == value)
        def _():
            for action in actions:
                action()


def layer_kernel(
    bits,
    pages_ref, x_ref, cells_ref, shift_ref, es_ref, tables_ref, ms_ref, rs_ref, gain_ref, nshift_ref,
    aw_hbm, mw_hbm, ew_hbm, rw_hbm, cot_hbm,
    out_ref, gin_ref, small_ref, ges_ref, gsh_ref, gpair_ref, grw_hbm, gew_hbm, gat_hbm,
    AW, MW, EW, RW, XR, HOT, Q, K, V, PR, CTX, NB, HAT, SCALE, AS, ACC, GB, GC, DQ, DK, DV, E, DD, SM,
    y_sems, one_sems, two_sems, core_sems, own_sems, small_sems, local_sems,
):
    net = Net(bits)
    rows, width = x_ref.shape
    half = rows // 2
    local = aw_hbm.shape[2]
    heads = local // HEAD_DIM
    hidden = ew_hbm.shape[1]

    barrier = pltpu.get_barrier_semaphore()
    greeted = (net.core, net.y, net.dp[0], net.dp[1])
    for partner in greeted:
        pl.semaphore_signal(barrier, inc=1, device_id=partner, device_id_type=MESH)

    SM[0, 0:2, :local] = shift_ref[...].astype(F32)
    SM[0, 2:3, :] = es_ref[...].astype(F32)
    SM[0, 8 : 8 + 2 * heads, :BUCKETS] = tables_ref[...].astype(F32)

    plan = []
    sems = (y_sems, one_sems, two_sems, core_sems)
    for m in range(3):
        plan.append((aw_hbm.at[m], (lambda s, m=m: AW.at[s, m]), 0, width, m % 2 == 0))
    plan.append((mw_hbm, (lambda s: MW.at[s]), 0, local, False))
    for own, ref, count in ((ew_hbm, EW, width), (rw_hbm, RW, hidden)):
        for part in range(2):
            plan.append(
                (own, (lambda s, ref=ref: ref.at[s]), part * (count // 2), count // 2, part == 0)
            )
    pieces = [Piece(net, n, *entry, sems) for n, entry in enumerate(plan)]
    weights = ((aw_hbm, AW), (mw_hbm, MW), (ew_hbm, EW), (rw_hbm, RW))
    keep_own = [
        pltpu.make_async_copy(own, ref.at[0], local_sems.at[n]) for n, (own, ref) in enumerate(weights)
    ]
    give_own = [remote(own, ref.at[1], own_sems, n, net.core) for n, (own, ref) in enumerate(weights)]
    small_core = remote(SM.at[0], SM.at[1], small_sems, 0, net.core)
    small_y = remote(SM.at[0], SM.at[2], small_sems, 1, net.y)
    small_far = remote(SM.at[2], SM.at[3], small_sems, 2, net.core)
    fetch_cot = pltpu.make_async_copy(cot_hbm, GB, local_sems.at[4])

    keep_own[0].start()
    keep_own[1].start()
    pl.semaphore_wait(barrier, len(greeted))
    small_y.start()
    for piece in pieces[:4]:
        piece.event(0)
    small_core.start()
    for copy in give_own:
        copy.start()
    for piece in pieces[4:]:
        piece.event(0)
    keep_own[2].start()
    keep_own[3].start()
    fetch_cot.start()

    def happen(*pairs):
        return [lambda n=n, s=s: pieces[n].event(s) for n, s in pairs]

    begin, bounds = page_scalars(pages_ref, net.t, half)
    perm = (iota((rows, rows), 1) == ((iota((rows, rows), 0) + begin) & (rows - 1))).astype(BF)
    XR[...] = nn(perm, x_ref[...]).astype(BF)
    bucket = iota((BUCKETS, rows), 0)
    mine = pl.ds(pl.multiple_of(net.t * rows, 128), rows)
    one = (cells_ref[0:1, mine] == bucket).astype(BF)
    two = (cells_ref[1:2, mine] == bucket).astype(BF)
    HOT[...] = nt(perm, jnp.concatenate([one, two, one, two], axis=0)).astype(BF)
    ACC[...] = XR[...].astype(F32) + ms_ref[...].astype(F32)
    for ref in (Q, K, V):
        for s in range(4):
            ref[s, :, local:] = jnp.zeros((rows, 256 - local), BF)
    GC[:, local:] = jnp.zeros((rows, 256 - local), BF)
    DD[:, :local] = jnp.zeros((rows, local), BF)
    col = page_numbers((iota((half, 1), 0) + (half + begin)) & (rows - 1), bounds)
    row = page_numbers((iota((1, half), 1) + (half + begin)) & (rows - 1), bounds)

    spot = iota((BUCKETS, 128), 1)
    spot = jnp.where(spot < 64, spot, spot - 128)
    fold = (iota((BUCKETS, 128), 0) == jnp.clip(BUCKETS // 2 - spot, 0, BUCKETS - 1)).astype(BF)

    keep_own[0].wait()
    keep_own[1].wait()

    def attend(r, _):
        at_step(
            r,
            {
                1: [small_core.wait_recv, give_own[0].wait_recv, give_own[1].wait_recv],
                2: happen((2, 1), (1, 2), (3, 1), (0, 3), (2, 2), (3, 2), (4, 1), (1, 3), (2, 3), (3, 3))
                + [small_far.wait_recv]
                + happen((0, 4), (1, 4), (2, 4), (3, 4)),
            },
        )
        line = nn(SM[r, 8 : 8 + 2 * heads, :BUCKETS].astype(BF), fold)
        lanes_at = iota((BUCKETS, 128), 1)
        tiles = []
        for a in range(2):
            parts = []
            for pair in range(2):
                total = jnp.zeros((BUCKETS, 128), F32)
                for which in range(min(2, heads - 2 * pair)):
                    off = which * HEAD_DIM + a * BUCKETS
                    h = a * heads + 2 * pair + which
                    spread = jnp.broadcast_to(line[h : h + 1, :], (BUCKETS, 128))
                    spread = pltpu.roll(spread, off, axis=1, stride=1, stride_axis=0)
                    inside = (lanes_at >= off) & (lanes_at < off + BUCKETS)
                    total = jnp.where(inside, spread, total)
                parts.append(total.astype(BF))
            tiles.append(jnp.concatenate(parts, axis=1))
        pairs = jnp.concatenate(tiles, axis=0)
        left = nn(HOT[:, : 2 * BUCKETS], pairs).astype(BF)

        queries = (nn(XR[...], AW[r, 0]) + SM[r, 0:1, :local]).astype(BF)
        Q[r, :, :local] = queries * jnp.asarray(HEAD_DIM ** -0.5, BF)
        K[r, :, :local] = nn(XR[...], AW[r, 1]).astype(BF)
        V[r, :, :local] = (nn(XR[...], AW[r, 2]) + SM[r, 1:2, :local]).astype(BF)
        at_step(r, {1: happen((0, 1), (1, 1)) + [small_y.wait_recv, small_far.start]})
        same = col == row
        for block in range(2):
            at = slice(block * half, (block + 1) * half)
            if block == 1:
                at_step(r, {1: happen((0, 2)), 2: happen((5, 1)), 3: happen((7, 1), (5, 2))})
            for pair in range(2):
                lanes = slice(pair * 128, (pair + 1) * 128)
                key_side = jnp.concatenate([K[r, at, lanes], HOT[at, :]], axis=1)
                total = None
                for which in range(min(2, heads - 2 * pair)):
                    keep = half_lanes(which)
                    query_side = jnp.concatenate(
                        [Q[r, at, lanes] * keep, left[at, lanes] * keep], axis=1
                    )
                    scores = nt(key_side, query_side)
                    if block == 1:
                        scores = jnp.where(same, scores, MASKED)
                    weights = jnp.exp(scores - jnp.max(scores, axis=0, keepdims=True))
                    probs = (weights * (1.0 / jnp.sum(weights, axis=0, keepdims=True))).astype(BF)
                    PR[r, (2 * pair + which) * 2 + block] = probs
                    part = tn(probs, V[r, at, lanes]) * keep.astype(F32)
                    total = part if total is None else total + part
                CTX[r, at, lanes] = total.astype(BF)
        at_step(r, {2: happen((4, 2), (6, 1)), 3: happen((4, 3), (6, 2))})
        ACC[...] += nn(CTX[r, :, :local], MW[r])
        return 0

    lax.fori_loop(0, 4, attend, 0)

    hat, scale = norm_stats(ACC[...])
    HAT[...] = hat
    SCALE[...] = scale
    normed = hat * gain_ref[0:1, :].astype(F32) + nshift_ref[0:1, :].astype(F32)
    NB[...] = normed.astype(BF)
    ACC[...] = normed + rs_ref[...].astype(F32)
    keep_own[2].wait()
    keep_own[3].wait()

    def feed(r, _):
        at_step(
            r,
            {
                0: happen((7, 2)),
                1: [give_own[2].wait_recv, give_own[3].wait_recv] + happen((5, 3)),
                2: happen((6, 3), (7, 3), (4, 4), (5, 4), (6, 4), (7, 4)),
            },
        )
        pre = nn(NB[...], EW[r]) + SM[r, 2:3, :]
        gate = 0.5 * (1.0 + lax.erf(pre * (0.5 ** 0.5)))
        AS[r, :rows] = (pre * gate).astype(BF)
        AS[r, rows:] = (
            gate + pre * (jnp.exp(-0.5 * (pre * pre)) * (1.0 / math.sqrt(2.0 * math.pi)))
        ).astype(BF)
        ACC[...] += nn(AS[r, :rows], RW[r])
        return 0

    lax.fori_loop(0, 4, feed, 0)

    fetch_cot.wait()
    hat, scale = norm_stats(ACC[...])
    gain = gain_ref[1:2, :].astype(F32)
    result = (hat * gain + nshift_ref[1:2, :].astype(F32)).astype(BF)
    perm = (iota((rows, rows), 1) == ((iota((rows, rows), 0) + begin) & (rows - 1))).astype(BF)
    out_ref[...] = tn(perm, result).astype(BF)
    cot = nn(perm, GB[...])
    grad = norm_back(cot, hat, scale, gain)
    ACC[...] = grad
    GB[...] = grad.astype(BF)
    small_ref[3:4, :] = jnp.sum(cot * hat, axis=0, keepdims=True)
    small_ref[4:5, :] = jnp.sum(cot, axis=0, keepdims=True)
    small_ref[5:6, :] = jnp.sum(grad, axis=0, keepdims=True)
    small_ref[6:8, :] = jnp.zeros((2, width), F32)

    for piece in pieces[4:]:
        piece.event(5)

    def feed_back(i, _):
        r = 3 - i
        grad_pre = (nt(GB[...], RW[r]) * AS[r, rows:].astype(F32)).astype(BF)
        RW[r] = tn(GB[...], AS[r, :rows]).astype(BF)
        ges_ref[r] = jnp.sum(grad_pre.astype(F32), axis=0, keepdims=True)
        ACC[...] += nt(grad_pre, EW[r])
        EW[r] = tn(NB[...], grad_pre).astype(BF)
        pltpu.make_async_copy(RW.at[r], grw_hbm.at[r], local_sems.at[5 + r]).start()
        pltpu.make_async_copy(EW.at[r], gew_hbm.at[r], local_sems.at[9 + r]).start()
        return 0

    lax.fori_loop(0, 4, feed_back, 0)

    grad = ACC[...]
    hat = HAT[...]
    gone = norm_back(grad, hat, SCALE[...], gain_ref[0:1, :].astype(F32))
    ACC[...] = gone
    GB[...] = gone.astype(BF)
    small_ref[0:1, :] = jnp.sum(grad * hat, axis=0, keepdims=True)
    small_ref[1:2, :] = jnp.sum(grad, axis=0, keepdims=True)
    small_ref[2:3, :] = jnp.sum(gone, axis=0, keepdims=True)

    def attend_back(i, _):
        r = 3 - i
        GC[:, :local] = nt(GB[...], MW[r]).astype(BF)
        for block in range(2):
            at = slice(block * half, (block + 1) * half)
            for pair in range(2):
                lanes = slice(pair * 128, (pair + 1) * 128)
                key_side = jnp.concatenate([K[r, at, lanes], HOT[at, :]], axis=1)
                sums = None
                for which in range(min(2, heads - 2 * pair)):
                    keep = half_lanes(which)
                    wide = keep.astype(F32)
                    probs = PR[r, (2 * pair + which) * 2 + block]
                    grad_probs = nt(V[r, at, lanes] * keep, GC[at, lanes])
                    soft = probs.astype(F32)
                    inner = jnp.sum(soft * grad_probs, axis=0, keepdims=True)
                    grad_scores = (soft * (grad_probs - inner)).astype(BF)
                    both = tn(grad_scores, key_side)
                    parts = (
                        both[:, :128] * wide,
                        both[:, 128:] * wide,
                        nn(grad_scores, Q[r, at, lanes]) * wide,
                        nn(probs, GC[at, lanes]) * wide,
                    )
                    sums = parts if sums is None else tuple(a + b for a, b in zip(sums, parts))
                DQ[at, lanes] = (sums[0] * (HEAD_DIM ** -0.5)).astype(BF)
                E[at, lanes] = sums[1].astype(BF)
                DK[at, lanes] = sums[2].astype(BF)
                DV[at, lanes] = sums[3].astype(BF)
        for m, ref in enumerate((DQ, DK, DV)):
            DD[:, (m + 1) * local : (m + 2) * local] = ref[:, :local]
            ACC[...] += nt(ref[:, :local], AW[r, m])
        weight_grad = tn(XR[...], DD[...])
        AS[r, :width, 256:] = weight_grad[:, 256:].astype(BF)
        AS[r, :width, :256] = (weight_grad[:, :256] + tn(GB[...], CTX[r])).astype(BF)
        gsh_ref[r, 0:1, :] = jnp.sum(DQ[:, :local].astype(F32), axis=0, keepdims=True)
        gsh_ref[r, 1:2, :] = jnp.sum(DV[:, :local].astype(F32), axis=0, keepdims=True)
        gpair_ref[r] = tn(HOT[:, : 2 * BUCKETS], E[...])
        pltpu.make_async_copy(AS.at[r, :width], gat_hbm.at[r], local_sems.at[13 + r]).start()
        return 0

    lax.fori_loop(0, 4, attend_back, 0)

    perm = (iota((rows, rows), 1) == ((iota((rows, rows), 0) + begin) & (rows - 1))).astype(BF)
    gin_ref[...] = tn(perm, ACC[...].astype(BF)).astype(BF)

    for r in range(4):
        pltpu.make_async_copy(RW.at[r], grw_hbm.at[r], local_sems.at[5 + r]).wait()
        pltpu.make_async_copy(EW.at[r], gew_hbm.at[r], local_sems.at[9 + r]).wait()
        pltpu.make_async_copy(AS.at[r, :width], gat_hbm.at[r], local_sems.at[13 + r]).wait()
    for piece in pieces[:4]:
        piece.event(5)
    for copy in give_own + [small_core, small_y, small_far]:
        copy.wait_send()


def swap(value, axis, size, bit):
    return lax.ppermute(value, axis, [(i, i ^ bit) for i in range(size)])


def reduce_slots(partial_sums, dp):
    add = lambda a, b: (a.astype(F32) + b.astype(F32))
    got = swap(partial_sums[1::2], "tensor", 4, 1)
    two = add(partial_sums[0::2], got).astype(BF)
    got = swap(two[1], "tensor", 4, 2)
    one = add(two[0], got)
    lead = one.shape[:-2]
    rows, cols = one.shape[-2:]
    bits = dp.bit_length() - 1
    one = one.reshape(lead + (2,) * bits + (rows // dp, cols))
    me = lax.axis_index("dp")
    for bit in range(bits):
        axis = one.ndim - 3
        mine = (me >> bit) & 1
        keep = lax.dynamic_index_in_dim(one, mine, axis, keepdims=False)
        send = lax.dynamic_index_in_dim(one, 1 - mine, axis, keepdims=False).astype(BF)
        one = add(keep, swap(send, "dp", dp, 1 << bit))
    return one


def on_device(
    dp,
    inputs,
    layout_cells,
    page_lengths,
    attend_weight,
    attend_shift,
    merge_weight,
    merge_shift,
    norm_gains,
    norm_shifts,
    expand_weight,
    expand_shift,
    reduce_weight,
    reduce_shift,
    bias_tables,
    cotangent,
):
    rows, width = inputs.shape
    half = rows // 2
    local = attend_weight.shape[2]
    heads = bias_tables.shape[1]
    hidden = expand_weight.shape[1]
    top = dp.bit_length() - 1
    bits = (top - 3, top - 2, top - 1)

    sds = jax.ShapeDtypeStruct
    smem = pl.BlockSpec(memory_space=pltpu.SMEM)
    vmem = pl.BlockSpec(memory_space=pltpu.VMEM)
    hbm = pl.BlockSpec(memory_space=pl.ANY)

    def kernel(*refs):
        return layer_kernel(bits, *refs)

    dma = pltpu.SemaphoreType.DMA
    output, input_grad, small, ges, gsh, gpair, grw, gew, gat = pl.pallas_call(
        kernel,
        in_specs=[smem] + [vmem] * 9 + [hbm] * 5,
        out_specs=[vmem] * 6 + [hbm] * 3,
        out_shape=[
            sds((rows, width), BF), sds((rows, width), BF), sds((8, width), F32),
            sds((4, 1, hidden), F32), sds((4, 2, local), F32), sds((4, 2 * BUCKETS, 256), F32),
            sds((4, width, hidden), BF), sds((4, width, hidden), BF), sds((4, width, 4 * local), BF),
        ],
        scratch_shapes=[
            pltpu.VMEM((4, 3, width, local), BF),
            pltpu.VMEM((4, local, width), BF),
            pltpu.VMEM((4, width, hidden), BF),
            pltpu.VMEM((4, hidden, width), BF),
            pltpu.VMEM((rows, width), BF),
            pltpu.VMEM((rows, 128), BF),
            pltpu.VMEM((4, rows, 256), BF),
            pltpu.VMEM((4, rows, 256), BF),
            pltpu.VMEM((4, rows, 256), BF),
            pltpu.VMEM((4, 2 * heads, half, half), BF),
            pltpu.VMEM((4, rows, 256), BF),
            pltpu.VMEM((rows, width), BF),
            pltpu.VMEM((rows, width), F32),
            pltpu.VMEM((rows, 1), F32),
            pltpu.VMEM((4, 2 * rows, hidden), BF),
            pltpu.VMEM((rows, width), F32),
            pltpu.VMEM((rows, width), BF),
            pltpu.VMEM((rows, 256), BF),
            pltpu.VMEM((rows, 256), BF),
            pltpu.VMEM((rows, 256), BF),
            pltpu.VMEM((rows, 256), BF),
            pltpu.VMEM((rows, 256), BF),
            pltpu.VMEM((rows, 4 * local), BF),
            pltpu.VMEM((4, SMALL_ROWS, hidden), F32),
            dma((2, 8)), dma((2, 8)), dma((2, 8)), dma((2, 8)), dma((2, 4)), dma((2, 3)), dma((17,)),
        ],
        compiler_params=pltpu.CompilerParams(
            collective_id=0, has_side_effects=True, vmem_limit_bytes=VMEM_LIMIT
        ),
    )(
        page_lengths, inputs, layout_cells, attend_shift, expand_shift.reshape(1, hidden),
        bias_tables.reshape(2 * heads, BUCKETS), merge_shift.reshape(1, width),
        reduce_shift.reshape(1, width), norm_gains, norm_shifts,
        attend_weight, merge_weight, expand_weight, reduce_weight, cotangent,
    )

    grad_rw = reduce_slots(grw, dp).T
    grad_ew = reduce_slots(gew, dp)
    grad_at = reduce_slots(gat, dp)
    grad_mw = grad_at[:, :local].T
    grad_aw = jnp.transpose(grad_at[:, local:].reshape(-1, 3, local), (1, 0, 2))

    spot = jnp.arange(BUCKETS, dtype=jnp.int32)
    bucket_of = jnp.clip(spot[:, None] - spot[None, :] + BUCKETS // 2, 0, BUCKETS - 1)
    folding = (bucket_of[:, :, None] == spot[None, None, :]).astype(F32)
    split = gpair.reshape(4, 2, BUCKETS, 4, 2, BUCKETS)
    grad_pairs = jnp.stack([split[:, a, :, :heads, a, :] for a in range(2)], axis=1)
    grad_tables = jnp.einsum("raxhy,xyb->rahb", grad_pairs, folding, precision=lax.Precision.HIGHEST)
    spare = -(2 * local + hidden + 2 * heads * BUCKETS) % width
    own = jnp.concatenate(
        [
            gsh.reshape(4, -1),
            ges.reshape(4, -1),
            grad_tables.reshape(4, -1),
            jnp.zeros((4, spare), F32),
        ],
        axis=1,
    ).reshape(4, -1, width)
    shared = small[:6]
    lines = own.shape[1]
    for bit, take in ((1, 2), (2, 1)):
        got = swap(jnp.concatenate([shared, own[1::2].reshape(-1, width)], axis=0), "tensor", 4, bit)
        shared = shared + got[:6]
        own = own[0::2] + got[6:].reshape(take, lines, width)
    both = jnp.concatenate([shared, own[0]], axis=0)
    for bit in range(dp.bit_length() - 1):
        both = both + swap(both, "dp", dp, 1 << bit)
    flat = both[6:].reshape(-1)
    cut = 2 * local + hidden
    return (
        output,
        input_grad,
        grad_aw,
        flat[: 2 * local].reshape(2, local),
        grad_mw,
        both[2],
        jnp.stack([both[0], both[3]]),
        jnp.stack([both[1], both[4]]),
        grad_ew,
        flat[2 * local : cut],
        grad_rw,
        both[5],
        flat[cut : cut + 2 * heads * BUCKETS].reshape(2, heads, BUCKETS),
    )


def solution(mesh):
    in_specs = (
        P(("dp", "tensor"), None),
        P(None, "dp"),
        P("dp", None),
        P(None, None, "tensor"),
        P(None, "tensor"),
        P("tensor", None),
        P(),
        P(),
        P(),
        P(None, "tensor"),
        P("tensor"),
        P("tensor", None),
        P(),
        P(None, "tensor", None),
        P(("dp", "tensor"), None),
    )
    out_specs = (
        P(("dp", "tensor"), None),
        P(("dp", "tensor"), None),
        P(None, "dp", "tensor"),
        P(None, "tensor"),
        P("tensor", "dp"),
        P(),
        P(),
        P(),
        P("dp", "tensor"),
        P("tensor"),
        P("tensor", "dp"),
        P(),
        P(None, "tensor", None),
    )

    def run(*arrays):
        return on_device(mesh.shape["dp"], *arrays)

    return jax.shard_map(
        run, mesh=mesh, in_specs=in_specs, out_specs=out_specs, check_vma=False
    )
```

```python
import math

import jax
import jax.numpy as jnp
from jax import lax
from jax.experimental import pallas as pl
from jax.experimental.pallas import tpu as pltpu
from jax.sharding import PartitionSpec as P

HEAD_DIM = 64
BUCKETS = 32
EPSILON = 1e-05
MASKED = -1000000000.0
BF = jnp.bfloat16
F32 = jnp.float32
VMEM_LIMIT = 60 * 1024 * 1024


def mm(a, b, da, db):
    return lax.dot_general(a, b, (((da,), (db,)), ((), ())), preferred_element_type=F32)


def nn(a, b):
    return mm(a, b, 1, 0)


def nt(a, b):
    return mm(a, b, 1, 1)


def tn(a, b):
    return mm(a, b, 0, 0)


def iota(shape, dim):
    return lax.broadcasted_iota(jnp.int32, shape, dim)


def page_scalars(pages_ref, line, half):
    total = jnp.int32(0)
    begin = jnp.int32(0)
    bounds = []
    for k in range(pages_ref.shape[1]):
        length = pages_ref[line, k]
        begin = begin + jnp.where(length == half, total, 0)
        total = total + length
        bounds.append(total)
    return begin, bounds


def page_numbers(places, bounds):
    number = jnp.zeros(places.shape, jnp.int32)
    for bound in bounds:
        number = number + (places >= bound).astype(jnp.int32)
    return number


def half_lanes(which):
    return ((iota((1, 128), 1) // HEAD_DIM) == which).astype(BF)


def norm_stats(signal):
    mean = jnp.mean(signal, axis=1, keepdims=True)
    center = signal - mean
    spread = jnp.mean(center * center, axis=1, keepdims=True)
    scale = lax.rsqrt(spread + EPSILON)
    return center * scale, scale


def norm_back(grad, hat, scale, gain):
    scaled = grad * gain
    return scale * (
        scaled
        - jnp.mean(scaled, axis=1, keepdims=True)
        - hat * jnp.mean(scaled * hat, axis=1, keepdims=True)
    )


MESH = pl.DeviceIdType.MESH
SMALL_ROWS = 16


class Net:
    def __init__(self, bits):
        t = lax.axis_index("tensor")
        d = lax.axis_index("dp")
        self.t = t
        self.core = {"tensor": t + 1 - 2 * (t % 2)}
        self.y = {"tensor": (t + 2) % 4}
        self.bit = [(d // 2 ** b) % 2 for b in bits]
        self.dp = [{"dp": d + 2 ** b * (1 - 2 * k)} for b, k in zip(bits, self.bit)]


def remote(source, target, sems, index, partner):
    return pltpu.make_async_remote_copy(
        src_ref=source,
        dst_ref=target,
        send_sem=sems.at[0, index],
        recv_sem=sems.at[1, index],
        device_id=partner,
        device_id_type=MESH,
    )


def rows_at(ref, start, count):
    return ref.at[pl.ds(pl.multiple_of(start, 16), count), :]


class Piece:
    def __init__(self, net, number, own, slots, start, count, x_first, sems):
        self.net, self.number, self.own, self.slots = net, number, own, slots
        self.start, self.count, self.x_first = start, count, x_first
        self.y_sems, self.one_sems, self.two_sems, self.core_sems = sems
        self.first, self.second = (0, 1) if x_first else (1, 0)

    def quarter(self, ref, flip):
        net = self.net
        fast = net.bit[self.first]
        if flip:
            fast = 1 - fast
        index = net.bit[self.second] * 2 + fast
        return rows_at(ref, self.start + index * (self.count // 4), self.count // 4)

    def half(self, ref, flip):
        slow = self.net.bit[self.second]
        if flip:
            slow = 1 - slow
        return rows_at(ref, self.start + slow * (self.count // 2), self.count // 2)

    def full(self, ref):
        return rows_at(ref, self.start, self.count)

    def over_y(self):
        return remote(
            self.quarter(self.own, False), self.quarter(self.slots(2), False),
            self.y_sems, self.number, self.net.y,
        )

    def hop_one(self, flip=False):
        here = self.quarter(self.slots(2), flip)
        return remote(here, here, self.one_sems, self.number, self.net.dp[self.first])

    def hop_two(self, flip=False):
        here = self.half(self.slots(2), flip)
        return remote(here, here, self.two_sems, self.number, self.net.dp[self.second])

    def to_core(self):
        return remote(
            self.full(self.slots(2)), self.full(self.slots(3)),
            self.core_sems, self.number, self.net.core,
        )

    def event(self, stage):
        if stage == 0:
            self.over_y().start()
        elif stage == 1:
            self.over_y().wait_recv()
            self.hop_one().start()
        elif stage == 2:
            self.hop_one(True).wait_recv()
            self.hop_two().start()
        elif stage == 3:
            self.hop_two(True).wait_recv()
            self.to_core().start()
        elif stage == 4:
            self.to_core().wait_recv()
        else:
            self.over_y().wait_send()
            self.hop_one().wait_send()
            self.hop_two().wait_send()
            self.to_core().wait_send()


CHUNK = 256
SHARED = 9
ORDERS = (
    (("y", 0, 1, 2), (0, "y", 1, 2), (1, "y", 0, 2)),
    (("y", 0, 1, 2), (0, "y", 1, 2), (1, 0, "y", 2)),
    (("y", 0, 1, 2), (0, "y", 1, 2), (1, 0, "y", 2)),
)


class Stage:
    def __init__(self, net, axis, slot, fixed, values, room, index, sems, block):
        self.net, self.axis, self.slot, self.fixed, self.values = net, axis, slot, dict(fixed), values
        self.room, self.index, self.sems, self.block = room, index, sems, block
        self.kept = slot if axis != "y" else 0
        self.partner = net.y if axis == "y" else net.dp[axis]

    def runs(self, bits):
        low = 0
        while low < 3 and low not in bits:
            low += 1
        starts = [0]
        for k in range(low, 3):
            choice = [bits[k]] if k in bits else [0, 1]
            starts = [start + value * (2 ** k * self.block) for start in starts for value in choice]
        return [(start, 2 ** low * self.block) for start in starts]

    def theirs(self):
        bits = dict(self.fixed)
        if self.axis != "y":
            bits[self.axis] = 1 - self.net.bit[self.axis]
        return self.runs(bits)

    def ours(self):
        bits = dict(self.fixed)
        if self.axis != "y":
            bits[self.axis] = self.net.bit[self.axis]
        return self.runs(bits)

    def send(self):
        at = 0
        for start, count in self.theirs():
            remote(
                self.values(self.slot, start, count), self.room(at, count),
                self.sems, self.index, self.partner,
            ).start()
            at += count

    def all_of_it(self):
        total = sum(count for _, count in self.ours())
        return remote(self.room(0, total), self.room(0, total), self.sems, self.index, self.partner)

    def take(self):
        self.all_of_it().wait_recv()
        at = 0
        for start, count in self.ours():
            here = self.values(self.kept, start, count)
            here[...] = here[...] + self.room(at, count)[...]
            at += count

    def sent(self):
        self.all_of_it().wait_send()


def chunk_stages(net, unit, chunk, slots, got, sems, first, block):
    lanes = pl.ds(chunk * CHUNK, CHUNK)

    def values(slot, start, count):
        return slots(slot).at[pl.ds(pl.multiple_of(start, 32), count), lanes]

    stages, fixed, live, at = {}, {}, (2, 0), 0
    for axis in ORDERS[unit][chunk]:
        exchanges = (2,) if axis == "y" else live
        for slot in exchanges:
            count = (8 * block) >> (len(fixed) + (axis != "y"))
            room = lambda start, rows, at=at: got.at[pl.ds(at + start, rows), :]
            stages[(axis, slot)] = Stage(
                net, axis, slot, fixed, values, room, first + len(stages), sems, block
            )
            at += count
        if axis == "y":
            live = (0,)
        else:
            fixed[axis] = net.bit[axis]
    return stages


def at_step(index, table):
    for value, actions in table.items():

        @pl.when(index == value)
        def _():
            for action in actions:
                action()


def layer_kernel(
    bits,
    pages_ref, x_ref, cells_ref, shift_ref, es_ref, tables_ref, ms_ref, rs_ref, gain_ref, nshift_ref,
    aw_hbm, mw_hbm, ew_hbm, rw_hbm, cot_hbm,
    out_ref, gin_ref, gaw_ref, gmw_ref, gew_ref, grw_ref, both_ref,
    AW, MW, EW, RW, XR, HOT, BACK, Q, K, V, PR, CTX, NB, HAT, SCALE, AS, ACC, GB, GC, DQ, DK, DV, E, DD, SM,
    FROM_CORE, FROM, SUMS, SUMS_CORE, SUMS_FAR,
    y_sems, one_sems, two_sems, core_sems, own_sems, small_sems, local_sems,
    unit_sems, stage_sems, total_sems,
):
    net = Net(bits)
    rows, width = x_ref.shape
    half = rows // 2
    local = aw_hbm.shape[1]
    heads = local // HEAD_DIM
    hidden = ew_hbm.shape[1]

    barrier = pltpu.get_barrier_semaphore()
    greeted = (net.core, net.y, net.dp[0], net.dp[1], net.dp[2])
    for partner in greeted:
        pl.semaphore_signal(barrier, inc=1, device_id=partner, device_id_type=MESH)

    SM[0, 0:2, :local] = shift_ref[...].astype(F32)
    SM[0, 2:3, :] = es_ref[...].reshape(1, hidden).astype(F32)
    for h in range(heads):
        SM[0, 8 + 2 * h : 10 + 2 * h, :BUCKETS] = tables_ref[h].astype(F32)

    plan = []
    sems = (y_sems, one_sems, two_sems, core_sems)
    for m in range(3):
        plan.append((aw_hbm.at[m], (lambda s, m=m: AW.at[s, m]), 0, local, m % 2 == 0))
    plan.append((mw_hbm, (lambda s: MW.at[s]), 0, local, False))
    for own, ref, count in ((ew_hbm, EW, width), (rw_hbm, RW, hidden)):
        for part in range(2):
            plan.append(
                (own, (lambda s, ref=ref: ref.at[s]), part * (count // 2), count // 2, part == 0)
            )
    pieces = [Piece(net, n, *entry, sems) for n, entry in enumerate(plan)]
    weights = ((aw_hbm, AW), (mw_hbm, MW), (ew_hbm, EW), (rw_hbm, RW))
    keep_own = [
        pltpu.make_async_copy(own, ref.at[0], local_sems.at[n]) for n, (own, ref) in enumerate(weights)
    ]
    give_own = [remote(own, ref.at[1], own_sems, n, net.core) for n, (own, ref) in enumerate(weights)]
    small_core = remote(SM.at[0], SM.at[1], small_sems, 0, net.core)
    small_y = remote(SM.at[0], SM.at[2], small_sems, 1, net.y)
    small_far = remote(SM.at[2], SM.at[3], small_sems, 2, net.core)
    fetch_cot = pltpu.make_async_copy(cot_hbm, GB, local_sems.at[4])

    keep_own[0].start()
    keep_own[1].start()
    pl.semaphore_wait(barrier, len(greeted))
    small_y.start()
    for piece in pieces[:4]:
        piece.event(0)
    small_core.start()
    for copy in give_own:
        copy.start()
    for piece in pieces[4:]:
        piece.event(0)
    keep_own[2].start()
    keep_own[3].start()
    fetch_cot.start()

    block = width // 8
    units = (
        (lambda slot: RW.at[slot]),
        (lambda slot: EW.at[slot]),
        (lambda slot: AS.at[slot, pl.ds(0, width), :]),
    )
    flows, first = {}, 0
    for unit in range(3):
        for chunk in range(3):
            stages = chunk_stages(
                net, unit, chunk, units[unit], FROM.at[unit * 3 + chunk], stage_sems, first, block
            )
            flows[unit, chunk] = stages
            first += len(stages)

    def to_core(unit, slot):
        return remote(
            units[unit](slot), FROM_CORE.at[unit, slot // 2], unit_sems, unit * 2 + slot // 2, net.core
        )

    def add_core(unit, slot):
        to_core(unit, slot + 1).wait_recv()
        here = units[unit](slot)
        here[...] = here[...] + FROM_CORE[unit, slot // 2]

    def send(unit, chunk, axis, slot=0):
        return flows[unit, chunk][axis, 2 if axis == "y" else slot].send

    def take(unit, chunk, axis, slot=0):
        return flows[unit, chunk][axis, 2 if axis == "y" else slot].take

    def open_far(unit):
        return [
            lambda: add_core(unit, 2),
            send(unit, 0, "y"), send(unit, 1, 0, 2), send(unit, 2, 1, 2),
        ]

    def open_near(unit):
        return [lambda: add_core(unit, 0), send(unit, 1, 0, 0), send(unit, 2, 1, 0)]

    def happen(*pairs):
        return [lambda n=n, s=s: pieces[n].event(s) for n, s in pairs]

    begin, bounds = page_scalars(pages_ref, net.t, half)
    perm = (iota((rows, rows), 1) == ((iota((rows, rows), 0) + begin) & (rows - 1))).astype(BF)
    XR[...] = nn(perm, x_ref[...]).astype(BF)
    bucket = iota((BUCKETS, rows), 0)
    mine = pl.ds(pl.multiple_of(net.t * rows, 128), rows)
    one = (cells_ref[0:1, mine] == bucket).astype(BF)
    two = (cells_ref[1:2, mine] == bucket).astype(BF)
    HOT[...] = nt(perm, jnp.concatenate([one, two, one, two], axis=0)).astype(BF)
    one = (cells_ref[0:1, mine] == BUCKETS - 1 - bucket).astype(BF)
    two = (cells_ref[1:2, mine] == BUCKETS - 1 - bucket).astype(BF)
    BACK[...] = nt(perm, jnp.concatenate([one, two], axis=0)).astype(BF)
    ACC[...] = XR[...].astype(F32) + ms_ref[...].reshape(1, width).astype(F32)
    for ref in (Q, K, V):
        for s in range(4):
            ref[s, :, local:] = jnp.zeros((rows, 256 - local), BF)
    GC[:, local:] = jnp.zeros((rows, 256 - local), BF)
    DD[:, :local] = jnp.zeros((rows, local), BF)
    col = page_numbers((iota((half, 1), 0) + (half + begin)) & (rows - 1), bounds)
    row = page_numbers((iota((1, half), 1) + (half + begin)) & (rows - 1), bounds)

    spot = iota((BUCKETS, 128), 1)
    spot = jnp.where(spot < 64, spot, spot - 128)
    fold = (iota((BUCKETS, 128), 0) == jnp.clip(BUCKETS // 2 - spot, 0, BUCKETS - 1)).astype(BF)

    fold_f32 = fold.astype(F32)

    keep_own[0].wait()
    keep_own[1].wait()

    def attend(r, _):
        at_step(
            r,
            {
                1: [small_core.wait_recv, give_own[0].wait_recv, give_own[1].wait_recv],
                2: happen((2, 1), (1, 2), (3, 1), (0, 3), (2, 2), (3, 2), (4, 1), (1, 3), (2, 3), (3, 3))
                + [small_far.wait_recv]
                + happen((0, 4), (1, 4), (2, 4), (3, 4)),
            },
        )
        line = nn(SM[r, 8 : 8 + 2 * heads, :BUCKETS].astype(BF), fold)
        lanes_at = iota((BUCKETS, 128), 1)
        tiles = []
        for a in range(2):
            parts = []
            for pair in range(2):
                total = jnp.zeros((BUCKETS, 128), F32)
                for which in range(min(2, heads - 2 * pair)):
                    off = which * HEAD_DIM + a * BUCKETS
                    h = (2 * pair + which) * 2 + a
                    spread = jnp.broadcast_to(line[h : h + 1, :], (BUCKETS, 128))
                    spread = pltpu.roll(spread, off, axis=1, stride=1, stride_axis=0)
                    inside = (lanes_at >= off) & (lanes_at < off + BUCKETS)
                    total = jnp.where(inside, spread, total)
                parts.append(total.astype(BF))
            tiles.append(jnp.concatenate(parts, axis=1))
        pairs = jnp.concatenate(tiles, axis=0)
        left = nn(HOT[:, : 2 * BUCKETS], pairs).astype(BF)

        queries = (nt(XR[...], AW[r, 0]) + SM[r, 0:1, :local]).astype(BF)
        Q[r, :, :local] = queries * jnp.asarray(HEAD_DIM ** -0.5, BF)
        K[r, :, :local] = nt(XR[...], AW[r, 1]).astype(BF)
        V[r, :, :local] = (nt(XR[...], AW[r, 2]) + SM[r, 1:2, :local]).astype(BF)
        at_step(r, {1: happen((0, 1), (1, 1)) + [small_y.wait_recv, small_far.start]})
        same = col == row
        for block in range(2):
            at = slice(block * half, (block + 1) * half)
            if block == 1:
                at_step(r, {1: happen((0, 2)), 2: happen((5, 1)), 3: happen((7, 1), (5, 2))})
            for pair in range(2):
                lanes = slice(pair * 128, (pair + 1) * 128)
                key_side = jnp.concatenate([K[r, at, lanes], HOT[at, :]], axis=1)
                total = None
                for which in range(min(2, heads - 2 * pair)):
                    keep = half_lanes(which)
                    query_side = jnp.concatenate(
                        [Q[r, at, lanes] * keep, left[at, lanes] * keep], axis=1
                    )
                    scores = nt(key_side, query_side)
                    if block == 1:
                        scores = jnp.where(same, scores, MASKED)
                    weights = jnp.exp(scores - jnp.max(scores, axis=0, keepdims=True))
                    probs = (weights * (1.0 / jnp.sum(weights, axis=0, keepdims=True))).astype(BF)
                    PR[r, (2 * pair + which) * 2 + block] = probs
                    part = tn(probs, V[r, at, lanes]) * keep.astype(F32)
                    total = part if total is None else total + part
                CTX[r, at, lanes] = total.astype(BF)
        at_step(r, {2: happen((4, 2), (6, 1)), 3: happen((4, 3), (6, 2))})
        ACC[...] += nn(CTX[r, :, :local], MW[r])
        return 0

    lax.fori_loop(0, 4, attend, 0)

    hat, scale = norm_stats(ACC[...])
    HAT[...] = hat
    SCALE[...] = scale
    normed = hat * gain_ref[0:1, :].astype(F32) + nshift_ref[0:1, :].astype(F32)
    NB[...] = normed.astype(BF)
    ACC[...] = normed + rs_ref[...].reshape(1, width).astype(F32)
    keep_own[2].wait()
    keep_own[3].wait()

    def feed(r, _):
        at_step(
            r,
            {
                0: happen((7, 2)),
                1: [give_own[2].wait_recv, give_own[3].wait_recv] + happen((5, 3)),
                2: happen((6, 3), (7, 3), (4, 4), (5, 4), (6, 4), (7, 4)),
            },
        )
        pre = nn(NB[...], EW[r]) + SM[r, 2:3, :]
        gate = 0.5 * (1.0 + lax.erf(pre * (0.5 ** 0.5)))
        AS[r, :rows] = (pre * gate).astype(BF)
        AS[r, rows:] = (
            gate + pre * (jnp.exp(-0.5 * (pre * pre)) * (1.0 / math.sqrt(2.0 * math.pi)))
        ).astype(BF)
        ACC[...] += nn(AS[r, :rows], RW[r])
        return 0

    lax.fori_loop(0, 4, feed, 0)

    fetch_cot.wait()
    hat, scale = norm_stats(ACC[...])
    gain = gain_ref[1:2, :].astype(F32)
    result = (hat * gain + nshift_ref[1:2, :].astype(F32)).astype(BF)
    perm = (iota((rows, rows), 1) == ((iota((rows, rows), 0) + begin) & (rows - 1))).astype(BF)
    out_ref[...] = tn(perm, result).astype(BF)
    cot = nn(perm, GB[...])
    grad = norm_back(cot, hat, scale, gain)
    ACC[...] = grad
    GB[...] = grad.astype(BF)
    shared_two = (
        jnp.sum(cot * hat, axis=0, keepdims=True),
        jnp.sum(cot, axis=0, keepdims=True),
        jnp.sum(grad, axis=0, keepdims=True),
    )
    for n, line in enumerate(shared_two):
        SUMS[0, SHARED + 3 + n : SHARED + 4 + n, :] = line

    for piece in pieces[4:]:
        piece.event(5)

    def feed_back(i, _):
        r = 3 - i
        grad_pre = (nt(GB[...], RW[r]) * AS[r, rows:].astype(F32)).astype(BF)
        RW[r] = tn(GB[...], AS[r, :rows]).astype(BF)
        at_step(
            r,
            {
                3: [to_core(0, 3).start],
                2: open_far(0),
                1: [to_core(0, 1).start],
                0: open_near(0),
            },
        )
        SUMS[r, 0:1, :] = jnp.sum(grad_pre.astype(F32), axis=0, keepdims=True)
        ACC[...] += nt(grad_pre, EW[r])
        EW[r] = tn(NB[...], grad_pre).astype(BF)
        at_step(
            r,
            {
                3: [to_core(1, 3).start],
                2: open_far(1),
                1: [to_core(1, 1).start],
                0: open_near(1),
            },
        )
        return 0

    lax.fori_loop(0, 4, feed_back, 0)

    grad = ACC[...]
    hat = HAT[...]
    gone = norm_back(grad, hat, SCALE[...], gain_ref[0:1, :].astype(F32))
    ACC[...] = gone
    GB[...] = gone.astype(BF)
    shared_one = (
        jnp.sum(grad * hat, axis=0, keepdims=True),
        jnp.sum(grad, axis=0, keepdims=True),
        jnp.sum(gone, axis=0, keepdims=True),
    )
    for n, line in enumerate(shared_one):
        SUMS[0, SHARED + n : SHARED + 1 + n, :] = line

    for action in (
        take(0, 0, "y"), send(0, 0, 0),
        take(0, 1, 0, 2), send(0, 1, "y"),
        take(0, 2, 1, 2), send(0, 2, "y"),
    ):
        action()

    def attend_back(i, _):
        r = 3 - i

        def early():
            at_step(
                r,
                {
                    3: [
                        take(0, 1, 0, 0), take(0, 2, 1, 0),
                        take(1, 1, 0, 2), send(1, 1, "y"),
                        take(1, 2, 1, 2), send(1, 2, 0, 2),
                    ],
                    2: [take(1, 1, 0, 0), take(1, 2, 1, 0), send(1, 2, 0, 0)],
                    1: [take(0, 2, "y"), send(0, 2, 0), take(1, 2, 0, 2), send(1, 2, "y")],
                    0: [
                        take(1, 1, "y"), send(1, 1, 1), take(1, 2, 0, 0),
                        take(0, 2, 0), send(0, 2, 2),
                    ],
                },
            )

        def late():
            at_step(
                r,
                {
                    3: [to_core(2, 3).start, take(1, 0, "y"), send(1, 0, 0)],
                    2: open_far(2)
                    + [take(0, 0, 0), send(0, 0, 1), take(0, 1, "y"), send(0, 1, 1)],
                    1: [
                        to_core(2, 1).start,
                        take(1, 0, 0), send(1, 0, 1),
                        take(0, 0, 1), send(0, 0, 2), take(0, 1, 1), send(0, 1, 2),
                    ],
                    0: open_near(2)
                    + [take(1, 2, "y"), send(1, 2, 2), take(1, 0, 1), send(1, 0, 2)]
                    + [take(1, 1, 1), send(1, 1, 2)],
                },
            )

        GC[:, :local] = nt(GB[...], MW[r]).astype(BF)
        for block in range(2):
            at = slice(block * half, (block + 1) * half)
            for pair in range(2):
                lanes = slice(pair * 128, (pair + 1) * 128)
                key_side = jnp.concatenate([K[r, at, lanes], HOT[at, :]], axis=1)
                sums = None
                for which in range(min(2, heads - 2 * pair)):
                    keep = half_lanes(which)
                    wide = keep.astype(F32)
                    probs = PR[r, (2 * pair + which) * 2 + block]
                    grad_probs = nt(V[r, at, lanes] * keep, GC[at, lanes])
                    soft = probs.astype(F32)
                    inner = jnp.sum(soft * grad_probs, axis=0, keepdims=True)
                    grad_scores = (soft * (grad_probs - inner)).astype(BF)
                    both = tn(grad_scores, key_side)
                    parts = (
                        both[:, :128] * wide,
                        both[:, 128:] * wide,
                        nn(grad_scores, Q[r, at, lanes]) * wide,
                        nn(probs, GC[at, lanes]) * wide,
                    )
                    sums = parts if sums is None else tuple(a + b for a, b in zip(sums, parts))
                DQ[at, lanes] = (sums[0] * (HEAD_DIM ** -0.5)).astype(BF)
                E[at, lanes] = sums[1].astype(BF)
                DK[at, lanes] = sums[2].astype(BF)
                DV[at, lanes] = sums[3].astype(BF)
            if block == 0:
                early()
        for m, ref in enumerate((DQ, DK, DV)):
            DD[:, (m + 1) * local : (m + 2) * local] = ref[:, :local]
            ACC[...] += nn(ref[:, :local], AW[r, m])
        weight_grad = tn(XR[...], DD[...])
        AS[r, :width, 256:] = weight_grad[:, 256:].astype(BF)
        AS[r, :width, :256] = (weight_grad[:, :256] + tn(GB[...], CTX[r])).astype(BF)
        late()
        SUMS[r, 1:2, :local] = jnp.sum(DQ[:, :local].astype(F32), axis=0, keepdims=True)
        SUMS[r, 2:3, :local] = jnp.sum(DV[:, :local].astype(F32), axis=0, keepdims=True)
        grad_pairs = tn(BACK[...], E[...])
        lanes_at = iota((BUCKETS, 128), 1)
        for h in range(heads):
            for a in range(2):
                off = (h % 2) * HEAD_DIM + a * BUCKETS
                part = grad_pairs[a * BUCKETS : (a + 1) * BUCKETS, (h // 2) * 128 : (h // 2 + 1) * 128]
                part = jnp.where((lanes_at >= off) & (lanes_at < off + BUCKETS), part, 0.0)
                part = pltpu.roll(part, (129 - BUCKETS - off) % 128, axis=1, stride=1, stride_axis=0)
                SUMS[r, 3 + 2 * h + a : 4 + 2 * h + a, :128] = jnp.sum(part, axis=0, keepdims=True)
        return 0

    SUMS[1, SHARED : SHARED + 6, :] = SUMS[0, SHARED : SHARED + 6, :]
    lax.fori_loop(0, 4, attend_back, 0)

    sums_core = [
        remote(SUMS.at[2 * n + 1], SUMS_CORE.at[n], total_sems, n, net.core) for n in range(2)
    ]
    sums_far = [
        remote(SUMS.at[2 - 2 * (n > 0)], SUMS_FAR.at[n], total_sems, 2 + n, partner)
        for n, partner in enumerate([net.y] + net.dp)
    ]
    for copy in sums_core:
        copy.start()
    perm = (iota((rows, rows), 1) == ((iota((rows, rows), 0) + begin) & (rows - 1))).astype(BF)
    gin_ref[...] = tn(perm, ACC[...].astype(BF)).astype(BF)
    take(2, 1, 0, 2)()
    send(2, 1, "y")()
    take(2, 2, 1, 2)()
    send(2, 2, 0, 2)()
    for n, copy in enumerate(sums_core):
        copy.wait_recv()
        SUMS[2 * n] = SUMS[2 * n] + SUMS_CORE[n]
    SUMS[2, SHARED : SHARED + 6, :] = SUMS[0, SHARED : SHARED + 6, :]
    sums_far[0].start()
    take(2, 2, 1, 0)()
    send(2, 2, 0, 0)()
    take(2, 0, "y")()
    send(2, 0, 0)()
    take(2, 1, 0, 0)()

    def finish(unit, chunk, out_ref):
        stage = flows[unit, chunk][2, 0]
        stage.all_of_it().wait_recv()
        (start, count), = stage.ours()
        here = stage.values(0, start, count)
        return here[...].astype(F32) + stage.room(0, count)[...].astype(F32)

    def lanes_of(chunk):
        return slice(chunk * CHUNK, (chunk + 1) * CHUNK)

    for chunk in range(3):
        grw_ref[:, lanes_of(chunk)] = finish(0, chunk, grw_ref)
    sums_far[0].wait_recv()
    SUMS[0] = SUMS[0] + SUMS_FAR[0]
    sums_far[1].start()
    take(2, 2, 0, 2)()
    send(2, 2, "y")()
    take(2, 1, "y")()
    send(2, 1, 1)()
    for chunk in range(3):
        gew_ref[:, lanes_of(chunk)] = finish(1, chunk, gew_ref)
    sums_far[1].wait()
    SUMS[0] = SUMS[0] + SUMS_FAR[1]
    sums_far[2].start()
    take(2, 2, 0, 0)()
    take(2, 0, 0)()
    send(2, 0, 1)()
    take(2, 2, "y")()
    send(2, 2, 2)()
    sums_far[2].wait()
    SUMS[0] = SUMS[0] + SUMS_FAR[2]
    sums_far[3].start()
    take(2, 1, 1)()
    send(2, 1, 2)()
    take(2, 0, 1)()
    send(2, 0, 2)()
    mixed = jnp.concatenate(
        [finish(2, chunk, None) for chunk in (0, 1, 2)], axis=1
    )
    gmw_ref[...] = jnp.transpose(mixed[:, :256])[:local, :]
    for m in range(3):
        gaw_ref[m] = mixed[:, (m + 1) * local : (m + 2) * local]
    sums_far[3].wait()
    both_ref[...] = SUMS[0] + SUMS_FAR[3]
    for row in range(2 * heads):
        both_ref[3 + row : 4 + row, :BUCKETS] = lax.dot_general(
            both_ref[3 + row : 4 + row, :128], fold_f32, (((1,), (1,)), ((), ())),
            precision=lax.Precision.HIGHEST, preferred_element_type=F32,
        )

    for stages in flows.values():
        for stage in stages.values():
            stage.sent()
    for unit in range(3):
        for slot in (1, 3):
            to_core(unit, slot).wait_send()
    for copy in sums_core + sums_far[:1]:
        copy.wait_send()
    for piece in pieces[:4]:
        piece.event(5)
    for copy in give_own + [small_core, small_y, small_far]:
        copy.wait_send()


def swap(value, axis, size, bit):
    return lax.ppermute(value, axis, [(i, i ^ bit) for i in range(size)])


def finish_rows(value, dp, bits_done):
    me = lax.axis_index("dp")
    left = dp.bit_length() - 1 - bits_done
    rows, cols = value.shape
    value = value.reshape((2,) * left + (rows >> left, cols))
    for bit in range(left):
        axis = value.ndim - 3
        mine = (me >> bit) & 1
        keep = lax.dynamic_index_in_dim(value, mine, axis, keepdims=False)
        send = lax.dynamic_index_in_dim(value, 1 - mine, axis, keepdims=False)
        value = keep + swap(send, "dp", dp, 1 << bit)
    return value


def on_device(
    dp,
    inputs,
    layout_cells,
    page_lengths,
    attend_weight,
    attend_shift,
    merge_weight,
    merge_shift,
    norm_gains,
    norm_shifts,
    expand_weight,
    expand_shift,
    reduce_weight,
    reduce_shift,
    bias_tables,
    cotangent,
):
    rows, width = inputs.shape
    half = rows // 2
    local = attend_weight.shape[2]
    heads = bias_tables.shape[1]
    hidden = expand_weight.shape[1]
    top = dp.bit_length() - 1
    bits = (top - 3, top - 2, top - 1)

    sds = jax.ShapeDtypeStruct
    smem = pl.BlockSpec(memory_space=pltpu.SMEM)
    vmem = pl.BlockSpec(memory_space=pltpu.VMEM)
    hbm = pl.BlockSpec(memory_space=pl.ANY)

    def kernel(*refs):
        return layer_kernel(bits, *refs)

    dma = pltpu.SemaphoreType.DMA
    count = sum(len(order) for orders in ORDERS for order in orders) + sum(
        order.index("y") for orders in ORDERS for order in orders
    )
    block = width // 8
    output, input_grad, gaw, gmw, gew, grw, both = pl.pallas_call(
        kernel,
        in_specs=[smem] + [vmem] * 9 + [hbm] * 5,
        out_specs=[vmem] * 7,
        out_shape=[
            sds((rows, width), BF), sds((rows, width), BF), sds((3, block, local), F32),
            sds((local, block), F32), sds((block, hidden), F32), sds((block, hidden), F32),
            sds((SMALL_ROWS, width), F32),
        ],
        scratch_shapes=[
            pltpu.VMEM((4, 3, local, width), BF),
            pltpu.VMEM((4, local, width), BF),
            pltpu.VMEM((4, width, hidden), BF),
            pltpu.VMEM((4, hidden, width), BF),
            pltpu.VMEM((rows, width), BF),
            pltpu.VMEM((rows, 128), BF),
            pltpu.VMEM((rows, 2 * BUCKETS), BF),
            pltpu.VMEM((4, rows, 256), BF),
            pltpu.VMEM((4, rows, 256), BF),
            pltpu.VMEM((4, rows, 256), BF),
            pltpu.VMEM((4, 2 * heads, half, half), BF),
            pltpu.VMEM((4, rows, 256), BF),
            pltpu.VMEM((rows, width), BF),
            pltpu.VMEM((rows, width), F32),
            pltpu.VMEM((rows, 1), F32),
            pltpu.VMEM((4, 2 * rows, hidden), BF),
            pltpu.VMEM((rows, width), F32),
            pltpu.VMEM((rows, width), BF),
            pltpu.VMEM((rows, 256), BF),
            pltpu.VMEM((rows, 256), BF),
            pltpu.VMEM((rows, 256), BF),
            pltpu.VMEM((rows, 256), BF),
            pltpu.VMEM((rows, 256), BF),
            pltpu.VMEM((rows, 4 * local), BF),
            pltpu.VMEM((4, SMALL_ROWS, hidden), F32),
            pltpu.VMEM((3, 2, width, hidden), BF),
            pltpu.VMEM((9, 15 * block, CHUNK), BF),
            pltpu.VMEM((4, SMALL_ROWS, width), F32),
            pltpu.VMEM((2, SMALL_ROWS, width), F32),
            pltpu.VMEM((4, SMALL_ROWS, width), F32),
            dma((2, 8)), dma((2, 8)), dma((2, 8)), dma((2, 8)), dma((2, 4)), dma((2, 3)), dma((5,)),
            dma((2, 6)), dma((2, count)), dma((2, 6)),
        ],
        compiler_params=pltpu.CompilerParams(
            collective_id=0, has_side_effects=True, vmem_limit_bytes=VMEM_LIMIT
        ),
    )(
        page_lengths, inputs, layout_cells, attend_shift, expand_shift,
        jnp.transpose(bias_tables, (1, 0, 2)), merge_shift, reduce_shift, norm_gains, norm_shifts,
        jnp.transpose(attend_weight, (0, 2, 1)), merge_weight, expand_weight, reduce_weight, cotangent,
    )

    if top > 3:
        grw = finish_rows(grw, dp, 3)
        gew = finish_rows(gew, dp, 3)
        gmw = finish_rows(gmw.T, dp, 3).T
        gaw = jnp.stack([finish_rows(gaw[m], dp, 3) for m in range(3)])
        for bit in range(top - 3):
            both = both + swap(both, "dp", dp, 1 << bit)
    first = SHARED
    tables = both[3 : 3 + 2 * heads, :BUCKETS].reshape(heads, 2, BUCKETS)
    return (
        output,
        input_grad,
        gaw,
        both[1:3, :local],
        gmw,
        both[first + 2],
        jnp.stack([both[first], both[first + 3]]),
        jnp.stack([both[first + 1], both[first + 4]]),
        gew,
        both[0],
        grw.T,
        both[first + 5],
        jnp.transpose(tables, (1, 0, 2)),
    )


def solution(mesh):
    in_specs = (
        P(("dp", "tensor"), None),
        P(None, "dp"),
        P("dp", None),
        P(None, None, "tensor"),
        P(None, "tensor"),
        P("tensor", None),
        P(),
        P(),
        P(),
        P(None, "tensor"),
        P("tensor"),
        P("tensor", None),
        P(),
        P(None, "tensor", None),
        P(("dp", "tensor"), None),
    )
    out_specs = (
        P(("dp", "tensor"), None),
        P(("dp", "tensor"), None),
        P(None, "dp", "tensor"),
        P(None, "tensor"),
        P("tensor", "dp"),
        P(),
        P(),
        P(),
        P("dp", "tensor"),
        P("tensor"),
        P("tensor", "dp"),
        P(),
        P(None, "tensor", None),
    )

    def run(*arrays):
        return on_device(mesh.shape["dp"], *arrays)

    return jax.shard_map(
        run, mesh=mesh, in_specs=in_specs, out_specs=out_specs, check_vma=False
    )
```

```python
import math

import jax
import jax.numpy as jnp
from jax import lax
from jax.experimental import pallas as pl
from jax.experimental.pallas import tpu as pltpu
from jax.sharding import PartitionSpec as P

HEAD_DIM = 64
BUCKETS = 32
EPSILON = 1e-05
MASKED = -1000000000.0
BF = jnp.bfloat16
F32 = jnp.float32
VMEM_LIMIT = 60 * 1024 * 1024
PIECES = (
    ("aw0", 0, 192, (0, 1)),
    ("aw1", 0, 192, (1, 0)),
    ("aw2", 0, 192, (1,)),
    ("mw", 0, 192, (1, 0)),
    ("ew", 0, 384, (0, 1)),
    ("ew", 384, 384, (1, 0)),
    ("rw", 0, 384, (0, 1)),
    ("rw", 384, 384, ()),
)
CHUNKS = (
    (
        (0, 256, ("y", 0, 1, 2)),
        (256, 256, (0, "y", 1, 2)),
        (512, 256, (1, "y", 0, 2)),
    ),
    (
        (0, 256, ("y", 0, 1, 2)),
        (256, 256, (0, "y", 1, 2)),
        (512, 256, (1, 0, "y", 2)),
    ),
    (
        (0, 256, ("y", 0, 1, 2)),
        (256, 256, (0, "y", 1, 2)),
        (512, 256, (1, 0, "y", 2)),
    ),
)
PLAN = {
    ("start", 0, 0): (
        ("gs", 0, 0),
        ("gs", 1, 0),
        ("gs", 2, 0),
        ("gs", 3, 0),
        ("gs", 4, 0),
        ("gs", 5, 0),
        ("gs", 6, 0),
        ("gs", 7, 0),
    ),
    ("att", 1, 0): (
        ("gt", 0, 1),
        ("gs", 0, 1),
        ("gt", 1, 1),
        ("gs", 1, 1),
    ),
    ("att", 2, 0): (
        ("gt", 3, 1),
        ("gs", 3, 1),
        ("gt", 0, 2),
        ("gs", 0, 2),
        ("gt", 1, 2),
        ("gs", 1, 2),
        ("gt", 2, 1),
        ("gs", 2, 1),
        ("gt", 3, 2),
        ("gs", 3, 2),
        ("gt", 4, 1),
        ("gs", 4, 1),
        ("gt", 1, 3),
        ("gs", 1, 3),
        ("gt", 1, 4),
        ("gt", 5, 1),
        ("gs", 5, 1),
        ("gt", 0, 3),
        ("gs", 0, 3),
        ("gt", 2, 2),
    ),
    ("att", 2, 1): (
        ("gs", 2, 2),
    ),
    ("att", 2, 3): (
        ("gt", 0, 4),
        ("gt", 6, 1),
        ("gs", 6, 1),
        ("gt", 3, 3),
    ),
    ("att", 3, 0): (
        ("gs", 3, 3),
        ("gt", 4, 2),
        ("gs", 4, 2),
        ("gt", 2, 3),
    ),
    ("att", 3, 1): (
        ("gt", 5, 2),
        ("gs", 5, 2),
    ),
    ("att", 3, 3): (
        ("gt", 3, 4),
    ),
    ("feed", 0, 1): (
        ("gt", 6, 2),
        ("gs", 6, 2),
    ),
    ("feed", 1, 1): (
        ("gt", 4, 3),
        ("gs", 4, 3),
    ),
    ("feed", 2, 0): (
        ("gt", 7, 1),
        ("gs", 7, 1),
        ("gt", 5, 3),
    ),
    ("feed", 2, 1): (
        ("gs", 5, 3),
        ("gt", 4, 4),
        ("gt", 7, 2),
        ("gt", 6, 3),
    ),
    ("feed", 3, 0): (
        ("gs", 6, 3),
        ("gt", 5, 4),
    ),
    ("feed", 3, 1): (
        ("gt", 6, 4),
    ),
    ("fa", 3, 1): (
        ("cs", 0, 3),
    ),
    ("fa", 1, 1): (
        ("cs", 0, 1),
    ),
    ("fa", 0, 0): (
        ("ct", 0, 2),
        ("s", 0, 0, "y", 2),
        ("s", 0, 1, 0, 2),
        ("s", 0, 2, 1, 2),
    ),
    ("fb", 3, 1): (
        ("cs", 1, 3),
        ("ct", 0, 0),
        ("s", 0, 1, 0, 0),
        ("s", 0, 2, 1, 0),
    ),
    ("fb", 1, 0): (
        ("ct", 1, 2),
        ("s", 1, 0, "y", 2),
        ("s", 1, 1, 0, 2),
        ("s", 1, 2, 1, 2),
    ),
    ("fb", 1, 1): (
        ("cs", 1, 1),
        ("t", 0, 1, 0, 2),
        ("s", 0, 1, "y", 2),
        ("t", 0, 2, 1, 2),
        ("s", 0, 2, "y", 2),
    ),
    ("lnb", 0, 0): (
        ("ct", 1, 0),
        ("s", 1, 1, 0, 0),
        ("s", 1, 2, 1, 0),
    ),
    ("ab", 3, 0): (
        ("t", 0, 0, "y", 2),
        ("s", 0, 0, 0, 0),
        ("t", 0, 1, 0, 0),
        ("t", 0, 2, 1, 0),
    ),
    ("ab", 3, 2): (
        ("t", 1, 1, 0, 2),
        ("s", 1, 1, "y", 2),
        ("t", 1, 2, 1, 2),
        ("s", 1, 2, 0, 2),
    ),
    ("ab", 3, 3): (
        ("cs", 2, 3),
    ),
    ("ab", 2, 1): (
        ("t", 1, 2, 1, 0),
        ("s", 1, 2, 0, 0),
    ),
    ("ab", 2, 2): (
        ("t", 0, 1, "y", 2),
        ("s", 0, 1, 1, 0),
    ),
    ("ab", 2, 3): (
        ("ct", 2, 2),
        ("s", 2, 0, "y", 2),
        ("s", 2, 1, 0, 2),
        ("s", 2, 2, 1, 2),
    ),
    ("ab", 1, 0): (
        ("t", 1, 1, 0, 0),
    ),
    ("ab", 1, 1): (
        ("t", 0, 0, 0, 0),
        ("s", 0, 0, 1, 0),
    ),
    ("ab", 1, 2): (
        ("t", 0, 1, 1, 0),
        ("s", 0, 1, 2, 0),
        ("t", 1, 0, "y", 2),
        ("s", 1, 0, 0, 0),
    ),
    ("ab", 1, 3): (
        ("cs", 2, 1),
        ("t", 1, 2, 0, 2),
        ("s", 1, 2, "y", 2),
    ),
    ("ab", 0, 0): (
        ("t", 1, 2, 0, 0),
    ),
    ("ab", 0, 1): (
        ("t", 0, 2, "y", 2),
        ("s", 0, 2, 0, 0),
    ),
    ("ab", 0, 2): (
        ("t", 0, 0, 1, 0),
        ("s", 0, 0, 2, 0),
    ),
    ("ab", 0, 3): (
        ("ms", 0),
        ("ct", 2, 0),
        ("s", 2, 1, 0, 0),
        ("s", 2, 2, 1, 0),
        ("t", 2, 2, 1, 2),
        ("s", 2, 2, 0, 2),
    ),
    ("end", 0, 0): (
        ("t", 0, 1, 2, 0),
        ("t", 1, 1, "y", 2),
        ("s", 1, 1, 1, 0),
        ("t", 2, 1, 0, 2),
        ("s", 2, 1, "y", 2),
        ("mt", 0),
        ("ms", 1),
        ("t", 0, 0, 2, 0),
        ("t", 1, 0, 0, 0),
        ("s", 1, 0, 1, 0),
        ("t", 1, 2, "y", 2),
        ("s", 1, 2, 2, 0),
        ("t", 0, 2, 0, 0),
        ("s", 0, 2, 2, 0),
        ("t", 1, 1, 1, 0),
        ("s", 1, 1, 2, 0),
        ("t", 2, 2, 1, 0),
        ("s", 2, 2, 0, 0),
        ("t", 2, 2, 0, 2),
        ("s", 2, 2, "y", 2),
        ("t", 2, 1, 0, 0),
        ("t", 1, 0, 1, 0),
        ("s", 1, 0, 2, 0),
        ("t", 1, 2, 2, 0),
        ("t", 2, 0, "y", 2),
        ("s", 2, 0, 0, 0),
        ("t", 2, 2, 0, 0),
        ("t", 2, 1, "y", 2),
        ("s", 2, 1, 1, 0),
        ("mt", 1),
        ("ms", 2),
        ("t", 0, 2, 2, 0),
        ("t", 1, 1, 2, 0),
        ("t", 2, 2, "y", 2),
        ("s", 2, 2, 2, 0),
        ("t", 1, 0, 2, 0),
        ("mt", 2),
        ("ms", 3),
        ("t", 2, 1, 1, 0),
        ("s", 2, 1, 2, 0),
        ("t", 2, 0, 0, 0),
        ("s", 2, 0, 1, 0),
        ("t", 2, 2, 2, 0),
        ("mt", 3),
        ("ms", 4),
        ("t", 2, 1, 2, 0),
        ("t", 2, 0, 1, 0),
        ("s", 2, 0, 2, 0),
        ("mt", 4),
        ("t", 2, 0, 2, 0),
    ),
}


def mm(a, b, da, db):
    return lax.dot_general(a, b, (((da,), (db,)), ((), ())), preferred_element_type=F32)


def nn(a, b):
    return mm(a, b, 1, 0)


def nt(a, b):
    return mm(a, b, 1, 1)


def tn(a, b):
    return mm(a, b, 0, 0)


def iota(shape, dim):
    return lax.broadcasted_iota(jnp.int32, shape, dim)


def page_scalars(pages_ref, line, half):
    total = jnp.int32(0)
    begin = jnp.int32(0)
    bounds = []
    for k in range(pages_ref.shape[1]):
        length = pages_ref[line, k]
        begin = begin + jnp.where(length == half, total, 0)
        total = total + length
        bounds.append(total)
    return begin, bounds


def page_numbers(places, bounds):
    number = jnp.zeros(places.shape, jnp.int32)
    for bound in bounds:
        number = number + (places >= bound).astype(jnp.int32)
    return number


def half_lanes(which):
    return ((iota((1, 128), 1) // HEAD_DIM) == which).astype(BF)


def norm_stats(signal):
    mean = jnp.mean(signal, axis=1, keepdims=True)
    center = signal - mean
    spread = jnp.mean(center * center, axis=1, keepdims=True)
    scale = lax.rsqrt(spread + EPSILON)
    return center * scale, scale


def norm_back(grad, hat, scale, gain):
    scaled = grad * gain
    return scale * (
        scaled
        - jnp.mean(scaled, axis=1, keepdims=True)
        - hat * jnp.mean(scaled * hat, axis=1, keepdims=True)
    )


MESH = pl.DeviceIdType.MESH
SMALL_ROWS = 16


class Net:
    def __init__(self, bits):
        t = lax.axis_index("tensor")
        d = lax.axis_index("dp")
        self.t = t
        self.core = {"tensor": t + 1 - 2 * (t % 2)}
        self.y = {"tensor": (t + 2) % 4}
        self.bit = [(d // 2 ** b) % 2 for b in bits]
        self.dp = [{"dp": d + 2 ** b * (1 - 2 * k)} for b, k in zip(bits, self.bit)]


def remote(source, target, sems, index, partner):
    return pltpu.make_async_remote_copy(
        src_ref=source,
        dst_ref=target,
        send_sem=sems.at[0, index],
        recv_sem=sems.at[1, index],
        device_id=partner,
        device_id_type=MESH,
    )


def rows_at(ref, start, count):
    return ref.at[pl.ds(pl.multiple_of(start, 16), count), :]


class Piece:
    def __init__(self, net, own, slots, start, count, axes, sems, first):
        self.net, self.own, self.slots, self.start, self.count = net, own, slots, start, count
        self.axes, self.sems, self.first = axes, sems, first

    def region(self, hop, flip):
        index, weight = 0, 1
        for axis in self.axes[hop - 1 :]:
            bit = self.net.bit[axis]
            index = index + weight * ((1 - bit) if flip and weight == 1 else bit)
            weight *= 2
        rows = self.count // weight
        return self.start + index * rows, rows

    def hop(self, number, arriving=False):
        if number == len(self.axes) + 1:
            here = rows_at(self.slots(2), self.start, self.count)
            there, partner = rows_at(self.slots(3), self.start, self.count), self.net.core
        elif number == 0:
            start, rows = self.region(1, False)
            here, partner = rows_at(self.own, start, rows), self.net.y
            there = rows_at(self.slots(2), start, rows)
        else:
            here = there = rows_at(self.slots(2), *self.region(number, arriving))
            partner = self.net.dp[self.axes[number - 1]]
        return remote(here, there, self.sems, self.first + number, partner)

    def sent(self):
        for number in range(len(self.axes) + 2):
            self.hop(number).wait_send()


SHARED = 9
class Stage:
    def __init__(self, net, axis, slot, fixed, values, room, index, sems, block):
        self.net, self.axis, self.slot, self.fixed, self.values = net, axis, slot, dict(fixed), values
        self.room, self.index, self.sems, self.block = room, index, sems, block
        self.kept = slot if axis != "y" else 0
        self.partner = net.y if axis == "y" else net.dp[axis]

    def runs(self, bits):
        low = 0
        while low < 3 and low not in bits:
            low += 1
        starts = [0]
        for k in range(low, 3):
            choice = [bits[k]] if k in bits else [0, 1]
            starts = [start + value * (2 ** k * self.block) for start in starts for value in choice]
        return [(start, 2 ** low * self.block) for start in starts]

    def theirs(self):
        bits = dict(self.fixed)
        if self.axis != "y":
            bits[self.axis] = 1 - self.net.bit[self.axis]
        return self.runs(bits)

    def ours(self):
        bits = dict(self.fixed)
        if self.axis != "y":
            bits[self.axis] = self.net.bit[self.axis]
        return self.runs(bits)

    def send(self):
        at = 0
        for start, count in self.theirs():
            remote(
                self.values(self.slot, start, count), self.room(at, count),
                self.sems, self.index, self.partner,
            ).start()
            at += count

    def all_of_it(self):
        total = sum(count for _, count in self.ours())
        return remote(self.room(0, total), self.room(0, total), self.sems, self.index, self.partner)

    def take(self):
        self.all_of_it().wait_recv()
        at = 0
        for start, count in self.ours():
            here = self.values(self.kept, start, count)
            here[...] = here[...] + self.room(at, count)[...]
            at += count

    def sent(self):
        self.all_of_it().wait_send()


def chunk_stages(net, order, lanes, slots, got, sems, first, block):
    def values(slot, start, count):
        return slots(slot).at[pl.ds(pl.multiple_of(start, 32), count), lanes]

    stages, fixed, live, at = {}, {}, (2, 0), 0
    for axis in order:
        exchanges = (2,) if axis == "y" else live
        for slot in exchanges:
            count = (8 * block) >> (len(fixed) + (axis != "y"))
            room = lambda start, rows, at=at: got.at[pl.ds(at + start, rows), lanes]
            stages[(axis, slot)] = Stage(
                net, axis, slot, fixed, values, room, first + len(stages), sems, block
            )
            at += count
        if axis == "y":
            live = (0,)
        else:
            fixed[axis] = net.bit[axis]
    return stages


def layer_kernel(
    bits,
    pages_ref, x_ref, cells_ref, shift_ref, es_ref, tables_ref, ms_ref, rs_ref, gain_ref, nshift_ref,
    aw_hbm, mw_hbm, ew_hbm, rw_hbm, cot_hbm,
    out_ref, gin_ref, gaw_ref, gmw_ref, gew_ref, grw_ref, both_ref,
    AW, MW, EW, RW, XR, HOT, BACK, Q, K, V, PR, CTX, NB, HAT, SCALE, AS, ACC, GB, GC, DQ, DK, DV, E, DD, SM,
    FROM_CORE, FROM, MIX, SUMS, SUMS_CORE, SUMS_FAR,
    in_sems, own_sems, small_sems, local_sems,
    unit_sems, stage_sems, total_sems,
):
    net = Net(bits)
    rows, width = x_ref.shape
    half = rows // 2
    local = aw_hbm.shape[1]
    heads = local // HEAD_DIM
    hidden = ew_hbm.shape[1]

    barrier = pltpu.get_barrier_semaphore()
    greeted = (net.core, net.y, net.dp[0], net.dp[1], net.dp[2])
    for partner in greeted:
        pl.semaphore_signal(barrier, inc=1, device_id=partner, device_id_type=MESH)

    SM[0, 0:2, :local] = shift_ref[...].astype(F32)
    SM[0, 2:3, :] = es_ref[...].reshape(1, hidden).astype(F32)
    for h in range(heads):
        SM[0, 8 + 2 * h : 10 + 2 * h, :BUCKETS] = tables_ref[h].astype(F32)

    whole_of = {
        "aw0": (aw_hbm.at[0], lambda s: AW.at[s, 0]),
        "aw1": (aw_hbm.at[1], lambda s: AW.at[s, 1]),
        "aw2": (aw_hbm.at[2], lambda s: AW.at[s, 2]),
        "mw": (mw_hbm, lambda s: MW.at[s]),
        "ew": (ew_hbm, lambda s: EW.at[s]),
        "rw": (rw_hbm, lambda s: RW.at[s]),
    }
    pieces = [
        Piece(net, *whole_of[name], start, count, axes, in_sems, 4 * n)
        for n, (name, start, count, axes) in enumerate(PIECES)
    ]
    weights = ((aw_hbm, AW), (mw_hbm, MW), (ew_hbm, EW), (rw_hbm, RW))
    keep_own = [
        pltpu.make_async_copy(own, ref.at[0], local_sems.at[n]) for n, (own, ref) in enumerate(weights)
    ]
    give_own = [remote(own, ref.at[1], own_sems, n, net.core) for n, (own, ref) in enumerate(weights)]
    small_core = remote(SM.at[0], SM.at[1], small_sems, 0, net.core)
    small_y = remote(SM.at[0], SM.at[2], small_sems, 1, net.y)
    small_far = remote(SM.at[2], SM.at[3], small_sems, 2, net.core)
    fetch_cot = pltpu.make_async_copy(cot_hbm, GB, local_sems.at[4])

    keep_own[0].start()
    keep_own[1].start()
    pl.semaphore_wait(barrier, len(greeted))
    block = width // 8
    units = (
        (lambda slot: RW.at[slot]),
        (lambda slot: EW.at[slot]),
        (lambda slot: AS.at[slot, pl.ds(0, width), :]),
    )
    flows, first = {}, 0
    for unit, chunks in enumerate(CHUNKS):
        for chunk, (lane, lanes, order) in enumerate(chunks):
            stages = chunk_stages(
                net, order, pl.ds(lane, lanes), units[unit], FROM.at[unit], stage_sems, first, block
            )
            flows[unit, chunk] = stages
            first += len(stages)

    def to_core(unit, slot):
        return remote(
            units[unit](slot), FROM_CORE.at[unit, slot // 2], unit_sems, unit * 2 + slot // 2, net.core
        )

    def add_core(unit, slot):
        to_core(unit, slot + 1).wait_recv()
        here = units[unit](slot)
        here[...] = here[...] + FROM_CORE[unit, slot // 2]

    sums_core = [
        remote(SUMS.at[2 * n + 1], SUMS_CORE.at[n], total_sems, n, net.core) for n in range(2)
    ]
    sums_far = [
        remote(SUMS.at[2 - 2 * (n > 0)], SUMS_FAR.at[n], total_sems, 2 + n, partner)
        for n, partner in enumerate([net.y] + net.dp)
    ]
    shared = slice(SHARED, SHARED + 6)

    def send_totals(k):
        if k == 0:
            for copy in sums_core:
                copy.start()
        else:
            sums_far[k - 1].start()

    def take_totals(k):
        if k == 0:
            for n, copy in enumerate(sums_core):
                copy.wait_recv()
                SUMS[2 * n] = SUMS[2 * n] + SUMS_CORE[n]
            SUMS[2, shared, :] = SUMS[0, shared, :]
        else:
            sums_far[k - 1].wait_recv()
            if k > 1:
                sums_far[k - 1].wait_send()
            SUMS[0] = SUMS[0] + SUMS_FAR[k - 1]

    results = (grw_ref, gew_ref, MIX)

    def take(unit, chunk, axis, slot):
        stages = flows[unit, chunk]
        stage = stages[axis, slot]
        if stage is not list(stages.values())[-1]:
            stage.take()
            return
        stage.all_of_it().wait_recv()
        (start, count), = stage.ours()
        lane, lanes, _ = CHUNKS[unit][chunk]
        mine = stage.values(0, start, count)[...].astype(F32)
        results[unit][:, lane : lane + lanes] = mine + stage.room(0, count)[...].astype(F32)

    def act(kind, *what):
        if kind == "gs":
            pieces[what[0]].hop(what[1]).start()
        elif kind == "gt":
            pieces[what[0]].hop(what[1] - 1, True).wait_recv()
        elif kind == "cs":
            to_core(*what).start()
        elif kind == "ct":
            add_core(*what)
        elif kind == "s":
            flows[what[0], what[1]][what[2], what[3]].send()
        elif kind == "t":
            take(*what)
        elif kind == "ms":
            send_totals(*what)
        else:
            take_totals(*what)

    def do(actions):
        for action in actions:
            act(*action)

    def at(phase, point, index=None, before=None):
        if index is None:
            do(PLAN.get((phase, 0, point), ()))
            return
        for r in range(4):
            first = (before or {}).get(r, ())
            actions = PLAN.get((phase, r, point), ())
            if first or actions:

                @pl.when(index == r)
                def _():
                    for wait in first:
                        wait()
                    do(actions)

    small_y.start()
    at("start", 0)
    small_core.start()
    for copy in give_own:
        copy.start()
    keep_own[2].start()
    keep_own[3].start()
    fetch_cot.start()

    begin, bounds = page_scalars(pages_ref, net.t, half)
    perm = (iota((rows, rows), 1) == ((iota((rows, rows), 0) + begin) & (rows - 1))).astype(BF)
    XR[...] = nn(perm, x_ref[...]).astype(BF)
    bucket = iota((BUCKETS, rows), 0)
    mine = pl.ds(pl.multiple_of(net.t * rows, 128), rows)
    one = (cells_ref[0:1, mine] == bucket).astype(BF)
    two = (cells_ref[1:2, mine] == bucket).astype(BF)
    HOT[...] = nt(perm, jnp.concatenate([one, two, one, two], axis=0)).astype(BF)
    one = (cells_ref[0:1, mine] == BUCKETS - 1 - bucket).astype(BF)
    two = (cells_ref[1:2, mine] == BUCKETS - 1 - bucket).astype(BF)
    BACK[...] = nt(perm, jnp.concatenate([one, two], axis=0)).astype(BF)
    ACC[...] = XR[...].astype(F32) + ms_ref[...].reshape(1, width).astype(F32)
    for ref in (Q, K, V):
        for s in range(4):
            ref[s, :, local:] = jnp.zeros((rows, 256 - local), BF)
    GC[:, local:] = jnp.zeros((rows, 256 - local), BF)
    DD[:, :local] = jnp.zeros((rows, local), BF)
    col = page_numbers((iota((half, 1), 0) + (half + begin)) & (rows - 1), bounds)
    row = page_numbers((iota((1, half), 1) + (half + begin)) & (rows - 1), bounds)

    spot = iota((BUCKETS, 128), 1)
    spot = jnp.where(spot < 64, spot, spot - 128)
    fold = (iota((BUCKETS, 128), 0) == jnp.clip(BUCKETS // 2 - spot, 0, BUCKETS - 1)).astype(BF)

    fold_f32 = fold.astype(F32)

    keep_own[0].wait()
    keep_own[1].wait()

    def attend(r, _):
        at(
            "att", 0, r,
            {
                1: [small_core.wait_recv, give_own[0].wait_recv, give_own[1].wait_recv],
                2: [small_y.wait_recv, small_far.start],
                3: [small_far.wait_recv],
            },
        )
        line = nn(SM[r, 8 : 8 + 2 * heads, :BUCKETS].astype(BF), fold)
        lanes_at = iota((BUCKETS, 128), 1)
        tiles = []
        for a in range(2):
            parts = []
            for pair in range(2):
                total = jnp.zeros((BUCKETS, 128), F32)
                for which in range(min(2, heads - 2 * pair)):
                    off = which * HEAD_DIM + a * BUCKETS
                    h = (2 * pair + which) * 2 + a
                    spread = jnp.broadcast_to(line[h : h + 1, :], (BUCKETS, 128))
                    spread = pltpu.roll(spread, off, axis=1, stride=1, stride_axis=0)
                    inside = (lanes_at >= off) & (lanes_at < off + BUCKETS)
                    total = jnp.where(inside, spread, total)
                parts.append(total.astype(BF))
            tiles.append(jnp.concatenate(parts, axis=1))
        pairs = jnp.concatenate(tiles, axis=0)
        left = nn(HOT[:, : 2 * BUCKETS], pairs).astype(BF)

        queries = (nt(XR[...], AW[r, 0]) + SM[r, 0:1, :local]).astype(BF)
        Q[r, :, :local] = queries * jnp.asarray(HEAD_DIM ** -0.5, BF)
        K[r, :, :local] = nt(XR[...], AW[r, 1]).astype(BF)
        V[r, :, :local] = (nt(XR[...], AW[r, 2]) + SM[r, 1:2, :local]).astype(BF)
        at("att", 1, r)
        same = col == row
        for block in range(2):
            span = slice(block * half, (block + 1) * half)
            if block == 1:
                at("att", 2, r)
            for pair in range(2):
                lanes = slice(pair * 128, (pair + 1) * 128)
                key_side = jnp.concatenate([K[r, span, lanes], HOT[span, :]], axis=1)
                total = None
                for which in range(min(2, heads - 2 * pair)):
                    keep = half_lanes(which)
                    query_side = jnp.concatenate(
                        [Q[r, span, lanes] * keep, left[span, lanes] * keep], axis=1
                    )
                    scores = nt(key_side, query_side)
                    if block == 1:
                        scores = jnp.where(same, scores, MASKED)
                    weights = jnp.exp(scores - jnp.max(scores, axis=0, keepdims=True))
                    probs = (weights * (1.0 / jnp.sum(weights, axis=0, keepdims=True))).astype(BF)
                    PR[r, (2 * pair + which) * 2 + block] = probs
                    part = tn(probs, V[r, span, lanes]) * keep.astype(F32)
                    total = part if total is None else total + part
                CTX[r, span, lanes] = total.astype(BF)
        at("att", 3, r)
        ACC[...] += nn(CTX[r, :, :local], MW[r])
        return 0

    lax.fori_loop(0, 4, attend, 0)

    hat, scale = norm_stats(ACC[...])
    HAT[...] = hat
    SCALE[...] = scale
    normed = hat * gain_ref[0:1, :].astype(F32) + nshift_ref[0:1, :].astype(F32)
    NB[...] = normed.astype(BF)
    ACC[...] = normed + rs_ref[...].reshape(1, width).astype(F32)
    keep_own[2].wait()
    keep_own[3].wait()

    def feed(r, _):
        at("feed", 0, r, {1: [give_own[2].wait_recv, give_own[3].wait_recv]})
        pre = nn(NB[...], EW[r]) + SM[r, 2:3, :]
        gate = 0.5 * (1.0 + lax.erf(pre * (0.5 ** 0.5)))
        AS[r, :rows] = (pre * gate).astype(BF)
        AS[r, rows:] = (
            gate + pre * (jnp.exp(-0.5 * (pre * pre)) * (1.0 / math.sqrt(2.0 * math.pi)))
        ).astype(BF)
        at("feed", 1, r)
        ACC[...] += nn(AS[r, :rows], RW[r])
        return 0

    lax.fori_loop(0, 4, feed, 0)

    fetch_cot.wait()
    hat, scale = norm_stats(ACC[...])
    gain = gain_ref[1:2, :].astype(F32)
    result = (hat * gain + nshift_ref[1:2, :].astype(F32)).astype(BF)
    perm = (iota((rows, rows), 1) == ((iota((rows, rows), 0) + begin) & (rows - 1))).astype(BF)
    out_ref[...] = result
    cot = nn(perm, GB[...])
    grad = norm_back(cot, hat, scale, gain)
    ACC[...] = grad
    GB[...] = grad.astype(BF)
    shared_two = (
        jnp.sum(cot * hat, axis=0, keepdims=True),
        jnp.sum(cot, axis=0, keepdims=True),
        jnp.sum(grad, axis=0, keepdims=True),
    )
    for n, line in enumerate(shared_two):
        SUMS[0, SHARED + 3 + n : SHARED + 4 + n, :] = line

    for (name, *_), piece in zip(PIECES, pieces):
        if name in ("ew", "rw"):
            piece.sent()

    def reduce_back(i, _):
        r = 3 - i
        grad_pre = (nt(GB[...], RW[r]) * AS[r, rows:].astype(F32)).astype(BF)
        AS[r, rows:] = grad_pre
        SUMS[r, 0:1, :] = jnp.sum(grad_pre.astype(F32), axis=0, keepdims=True)
        at("fa", 0, r)
        RW[r] = tn(GB[...], AS[r, :rows]).astype(BF)
        at("fa", 1, r)
        return 0

    lax.fori_loop(0, 4, reduce_back, 0)

    def expand_back(i, _):
        r = 3 - i
        ACC[...] += nt(AS[r, rows:], EW[r])
        at("fb", 0, r)
        EW[r] = tn(NB[...], AS[r, rows:]).astype(BF)
        at("fb", 1, r)
        return 0

    lax.fori_loop(0, 4, expand_back, 0)

    grad = ACC[...]
    hat = HAT[...]
    gone = norm_back(grad, hat, SCALE[...], gain_ref[0:1, :].astype(F32))
    ACC[...] = gone
    GB[...] = gone.astype(BF)
    shared_one = (
        jnp.sum(grad * hat, axis=0, keepdims=True),
        jnp.sum(grad, axis=0, keepdims=True),
        jnp.sum(gone, axis=0, keepdims=True),
    )
    for n, line in enumerate(shared_one):
        SUMS[0, SHARED + n : SHARED + 1 + n, :] = line

    at("lnb", 0)

    def attend_back(i, _):
        r = 3 - i

        GC[:, :local] = nt(GB[...], MW[r]).astype(BF)
        at("ab", 0, r)
        for block in range(2):
            span = slice(block * half, (block + 1) * half)
            for pair in range(2):
                lanes = slice(pair * 128, (pair + 1) * 128)
                key_side = jnp.concatenate([K[r, span, lanes], HOT[span, :]], axis=1)
                sums = None
                for which in range(min(2, heads - 2 * pair)):
                    keep = half_lanes(which)
                    wide = keep.astype(F32)
                    probs = PR[r, (2 * pair + which) * 2 + block]
                    grad_probs = nt(V[r, span, lanes] * keep, GC[span, lanes])
                    soft = probs.astype(F32)
                    inner = jnp.sum(soft * grad_probs, axis=0, keepdims=True)
                    grad_scores = (soft * (grad_probs - inner)).astype(BF)
                    both = tn(grad_scores, key_side)
                    parts = (
                        both[:, :128] * wide,
                        both[:, 128:] * wide,
                        nn(grad_scores, Q[r, span, lanes]) * wide,
                        nn(probs, GC[span, lanes]) * wide,
                    )
                    sums = parts if sums is None else tuple(a + b for a, b in zip(sums, parts))
                DQ[span, lanes] = (sums[0] * (HEAD_DIM ** -0.5)).astype(BF)
                E[span, lanes] = sums[1].astype(BF)
                DK[span, lanes] = sums[2].astype(BF)
                DV[span, lanes] = sums[3].astype(BF)
            at("ab", 1 + block, r)
        for m, ref in enumerate((DQ, DK, DV)):
            DD[:, (m + 1) * local : (m + 2) * local] = ref[:, :local]
            ACC[...] += nn(ref[:, :local], AW[r, m])
        weight_grad = tn(XR[...], DD[...])
        AS[r, :width, 256:] = weight_grad[:, 256:].astype(BF)
        AS[r, :width, :256] = (weight_grad[:, :256] + tn(GB[...], CTX[r])).astype(BF)
        SUMS[r, 1:2, :local] = jnp.sum(DQ[:, :local].astype(F32), axis=0, keepdims=True)
        SUMS[r, 2:3, :local] = jnp.sum(DV[:, :local].astype(F32), axis=0, keepdims=True)
        grad_pairs = tn(BACK[...], E[...])
        lanes_at = iota((BUCKETS, 128), 1)
        for h in range(heads):
            for a in range(2):
                off = (h % 2) * HEAD_DIM + a * BUCKETS
                part = grad_pairs[a * BUCKETS : (a + 1) * BUCKETS, (h // 2) * 128 : (h // 2 + 1) * 128]
                part = jnp.where((lanes_at >= off) & (lanes_at < off + BUCKETS), part, 0.0)
                part = pltpu.roll(part, (129 - BUCKETS - off) % 128, axis=1, stride=1, stride_axis=0)
                SUMS[r, 3 + 2 * h + a : 4 + 2 * h + a, :128] = jnp.sum(part, axis=0, keepdims=True)
        at("ab", 3, r)
        return 0

    SUMS[1, shared, :] = SUMS[0, shared, :]
    lax.fori_loop(0, 4, attend_back, 0)

    at("fin", 0)
    perm = (iota((rows, rows), 1) == ((iota((rows, rows), 0) + begin) & (rows - 1))).astype(BF)
    gin_ref[...] = tn(perm, ACC[...].astype(BF)).astype(BF)
    out_ref[...] = tn(perm, out_ref[...]).astype(BF)
    at("end", 0)
    gmw_ref[...] = jnp.transpose(MIX[:, :256])[:local, :]
    for m in range(3):
        gaw_ref[m] = MIX[:, (m + 1) * local : (m + 2) * local]
    both_ref[...] = SUMS[0]
    for row in range(2 * heads):
        both_ref[3 + row : 4 + row, :BUCKETS] = lax.dot_general(
            both_ref[3 + row : 4 + row, :128], fold_f32, (((1,), (1,)), ((), ())),
            precision=lax.Precision.HIGHEST, preferred_element_type=F32,
        )

    for stages in flows.values():
        for stage in stages.values():
            stage.sent()
    for unit in range(3):
        for slot in (1, 3):
            to_core(unit, slot).wait_send()
    for copy in sums_core + sums_far[:1]:
        copy.wait_send()
    for (name, *_), piece in zip(PIECES, pieces):
        if name not in ("ew", "rw"):
            piece.sent()
    for copy in give_own + [small_core, small_y, small_far]:
        copy.wait_send()


def swap(value, axis, size, bit):
    return lax.ppermute(value, axis, [(i, i ^ bit) for i in range(size)])


def finish_rows(value, dp, bits_done):
    me = lax.axis_index("dp")
    left = dp.bit_length() - 1 - bits_done
    rows, cols = value.shape
    value = value.reshape((2,) * left + (rows >> left, cols))
    for bit in range(left):
        axis = value.ndim - 3
        mine = (me >> bit) & 1
        keep = lax.dynamic_index_in_dim(value, mine, axis, keepdims=False)
        send = lax.dynamic_index_in_dim(value, 1 - mine, axis, keepdims=False)
        value = keep + swap(send, "dp", dp, 1 << bit)
    return value


def on_device(
    dp,
    inputs,
    layout_cells,
    page_lengths,
    attend_weight,
    attend_shift,
    merge_weight,
    merge_shift,
    norm_gains,
    norm_shifts,
    expand_weight,
    expand_shift,
    reduce_weight,
    reduce_shift,
    bias_tables,
    cotangent,
):
    rows, width = inputs.shape
    half = rows // 2
    local = attend_weight.shape[2]
    heads = bias_tables.shape[1]
    hidden = expand_weight.shape[1]
    top = dp.bit_length() - 1
    bits = (top - 3, top - 2, top - 1)

    sds = jax.ShapeDtypeStruct
    smem = pl.BlockSpec(memory_space=pltpu.SMEM)
    vmem = pl.BlockSpec(memory_space=pltpu.VMEM)
    hbm = pl.BlockSpec(memory_space=pl.ANY)

    def kernel(*refs):
        return layer_kernel(bits, *refs)

    dma = pltpu.SemaphoreType.DMA
    count = sum(len(order) + order.index("y") for chunks in CHUNKS for _, _, order in chunks)
    block = width // 8
    output, input_grad, gaw, gmw, gew, grw, both = pl.pallas_call(
        kernel,
        in_specs=[smem] + [vmem] * 9 + [hbm] * 5,
        out_specs=[vmem] * 7,
        out_shape=[
            sds((rows, width), BF), sds((rows, width), BF), sds((3, block, local), F32),
            sds((local, block), F32), sds((block, hidden), F32), sds((block, hidden), F32),
            sds((SMALL_ROWS, width), F32),
        ],
        scratch_shapes=[
            pltpu.VMEM((4, 3, local, width), BF),
            pltpu.VMEM((4, local, width), BF),
            pltpu.VMEM((4, width, hidden), BF),
            pltpu.VMEM((4, hidden, width), BF),
            pltpu.VMEM((rows, width), BF),
            pltpu.VMEM((rows, 128), BF),
            pltpu.VMEM((rows, 2 * BUCKETS), BF),
            pltpu.VMEM((4, rows, 256), BF),
            pltpu.VMEM((4, rows, 256), BF),
            pltpu.VMEM((4, rows, 256), BF),
            pltpu.VMEM((4, 2 * heads, half, half), BF),
            pltpu.VMEM((4, rows, 256), BF),
            pltpu.VMEM((rows, width), BF),
            pltpu.VMEM((rows, width), F32),
            pltpu.VMEM((rows, 1), F32),
            pltpu.VMEM((4, 2 * rows, hidden), BF),
            pltpu.VMEM((rows, width), F32),
            pltpu.VMEM((rows, width), BF),
            pltpu.VMEM((rows, 256), BF),
            pltpu.VMEM((rows, 256), BF),
            pltpu.VMEM((rows, 256), BF),
            pltpu.VMEM((rows, 256), BF),
            pltpu.VMEM((rows, 256), BF),
            pltpu.VMEM((rows, 4 * local), BF),
            pltpu.VMEM((4, SMALL_ROWS, hidden), F32),
            pltpu.VMEM((3, 2, width, hidden), BF),
            pltpu.VMEM((3, 15 * block, hidden), BF),
            pltpu.VMEM((block, width), F32),
            pltpu.VMEM((4, SMALL_ROWS, width), F32),
            pltpu.VMEM((2, SMALL_ROWS, width), F32),
            pltpu.VMEM((4, SMALL_ROWS, width), F32),
            dma((2, 4 * len(PIECES))), dma((2, 4)), dma((2, 3)), dma((5,)),
            dma((2, 6)), dma((2, count)), dma((2, 6)),
        ],
        compiler_params=pltpu.CompilerParams(
            collective_id=0, has_side_effects=True, vmem_limit_bytes=VMEM_LIMIT
        ),
    )(
        page_lengths, inputs, layout_cells, attend_shift, expand_shift,
        jnp.transpose(bias_tables, (1, 0, 2)), merge_shift, reduce_shift, norm_gains, norm_shifts,
        jnp.transpose(attend_weight, (0, 2, 1)), merge_weight, expand_weight, reduce_weight, cotangent,
    )

    if top > 3:
        grw = finish_rows(grw, dp, 3)
        gew = finish_rows(gew, dp, 3)
        gmw = finish_rows(gmw.T, dp, 3).T
        gaw = jnp.stack([finish_rows(gaw[m], dp, 3) for m in range(3)])
        for bit in range(top - 3):
            both = both + swap(both, "dp", dp, 1 << bit)
    first = SHARED
    tables = both[3 : 3 + 2 * heads, :BUCKETS].reshape(heads, 2, BUCKETS)
    return (
        output,
        input_grad,
        gaw,
        both[1:3, :local],
        gmw,
        both[first + 2],
        jnp.stack([both[first], both[first + 3]]),
        jnp.stack([both[first + 1], both[first + 4]]),
        gew,
        both[0],
        grw.T,
        both[first + 5],
        jnp.transpose(tables, (1, 0, 2)),
    )


def solution(mesh):
    in_specs = (
        P(("dp", "tensor"), None),
        P(None, "dp"),
        P("dp", None),
        P(None, None, "tensor"),
        P(None, "tensor"),
        P("tensor", None),
        P(),
        P(),
        P(),
        P(None, "tensor"),
        P("tensor"),
        P("tensor", None),
        P(),
        P(None, "tensor", None),
        P(("dp", "tensor"), None),
    )
    out_specs = (
        P(("dp", "tensor"), None),
        P(("dp", "tensor"), None),
        P(None, "dp", "tensor"),
        P(None, "tensor"),
        P("tensor", "dp"),
        P(),
        P(),
        P(),
        P("dp", "tensor"),
        P("tensor"),
        P("tensor", "dp"),
        P(),
        P(None, "tensor", None),
    )

    def run(*arrays):
        return on_device(mesh.shape["dp"], *arrays)

    return jax.shard_map(
        run, mesh=mesh, in_specs=in_specs, out_specs=out_specs, check_vma=False
    )
```

```python
import math

import jax
import jax.numpy as jnp
from jax import lax
from jax.experimental import pallas as pl
from jax.experimental.pallas import tpu as pltpu
from jax.sharding import PartitionSpec as P

HEAD_DIM = 64
BUCKETS = 32
EPSILON = 1e-05
MASKED = -1000000000.0
BF = jnp.bfloat16
F32 = jnp.float32
VMEM_LIMIT = 60 * 1024 * 1024
PIECES = (
    ("ew", 0, 192, (1, 0)),
    ("ew", 192, 192, (1, 0)),
    ("rw", 0, 192, (1, 0)),
    ("aw0", 0, 192, (0, 1)),
    ("rw", 192, 192, ()),
    ("aw1", 0, 192, (1, 0)),
    ("ew", 384, 192, ()),
    ("aw2", 0, 192, (0, 1)),
    ("mw", 0, 192, (0,)),
    ("rw", 384, 192, (1, 0)),
    ("ew", 576, 192, (1,)),
    ("rw", 576, 192, (0, 1)),
)
CHUNKS = (
    (
        (0, 256, ("y", 0, 1, 2)),
        (256, 256, (0, "y", 1, 2)),
        (512, 128, (1, "y", 0, 2)),
        (640, 128, (1, 0, 2, "y")),
    ),
    (
        (0, 128, ("y", 2, 0, 1)),
        (128, 256, (0, "y", 1, 2)),
        (384, 384, (1, 0, "y", 2)),
    ),
    (
        (0, 256, ("y", 0, 1, 2)),
        (256, 256, (0, "y", 1, 2)),
        (512, 256, (1, 0, "y", 2)),
    ),
)
PLAN = {
    ("start", 0, 0): (
        ("gs", 0, 0),
        ("gs", 3, 0),
        ("gs", 5, 0),
    ),
    ("att", 0, 2): (
        ("gs", 7, 0),
    ),
    ("att", 1, 0): (
        ("gs", 8, 0),
        ("gs", 9, 0),
        ("gs", 11, 0),
        ("gt", 0, 1),
        ("gs", 0, 1),
        ("gt", 3, 1),
        ("gs", 3, 1),
    ),
    ("att", 1, 2): (
        ("gs", 1, 0),
        ("gs", 2, 0),
        ("gs", 10, 0),
    ),
    ("att", 1, 3): (
        ("gt", 5, 1),
        ("gs", 5, 1),
    ),
    ("att", 2, 0): (
        ("gs", 4, 0),
        ("gs", 6, 0),
        ("gt", 7, 1),
        ("gs", 7, 1),
        ("gt", 0, 2),
        ("gs", 0, 2),
        ("gt", 3, 2),
        ("gs", 3, 2),
        ("gt", 9, 1),
        ("gs", 9, 1),
        ("gt", 5, 2),
        ("gs", 5, 2),
        ("gt", 8, 1),
        ("gs", 8, 1),
        ("gt", 11, 1),
        ("gs", 11, 1),
        ("gt", 7, 2),
        ("gs", 7, 2),
        ("gt", 1, 1),
        ("gs", 1, 1),
        ("gt", 9, 2),
        ("gs", 9, 2),
        ("gt", 2, 1),
        ("gs", 2, 1),
        ("gt", 3, 3),
        ("gs", 3, 3),
        ("gt", 0, 3),
        ("gs", 0, 3),
        ("gt", 3, 4),
        ("gt", 0, 4),
        ("gt", 7, 3),
        ("gs", 7, 3),
        ("gt", 5, 3),
    ),
    ("att", 2, 1): (
        ("gs", 5, 3),
        ("gt", 7, 4),
    ),
    ("att", 2, 3): (
        ("gt", 1, 2),
        ("gs", 1, 2),
        ("gt", 2, 2),
        ("gs", 2, 2),
        ("gt", 5, 4),
        ("gt", 8, 2),
        ("gs", 8, 2),
        ("gt", 10, 1),
        ("gs", 10, 1),
    ),
    ("att", 3, 1): (
        ("gt", 8, 3),
        ("gt", 11, 2),
        ("gs", 11, 2),
    ),
    ("feed", 0, 0): (
        ("gt", 4, 1),
        ("gs", 4, 1),
        ("gt", 9, 3),
        ("gs", 9, 3),
    ),
    ("feed", 1, 0): (
        ("gt", 4, 2),
        ("gt", 9, 4),
        ("gt", 10, 2),
        ("gs", 10, 2),
    ),
    ("feed", 1, 1): (
        ("gt", 1, 3),
        ("gs", 1, 3),
        ("gt", 2, 3),
        ("gs", 2, 3),
        ("gt", 6, 1),
        ("gs", 6, 1),
        ("gt", 10, 3),
        ("gt", 11, 3),
        ("gs", 11, 3),
    ),
    ("feed", 3, 0): (
        ("gt", 1, 4),
        ("gt", 2, 4),
        ("gt", 6, 2),
        ("gt", 11, 4),
    ),
    ("fa", 3, 1): (
        ("cs", 0, 3),
    ),
    ("fa", 1, 0): (
        ("ct", 0, 2),
        ("s", 0, 0, "y", 2),
        ("s", 0, 3, 1, 2),
        ("s", 0, 1, 0, 2),
        ("s", 0, 2, 1, 2),
    ),
    ("fa", 1, 1): (
        ("cs", 0, 1),
    ),
    ("fb", 3, 0): (
        ("ct", 0, 0),
        ("s", 0, 3, 1, 0),
        ("s", 0, 1, 0, 0),
        ("s", 0, 2, 1, 0),
    ),
    ("fb", 3, 1): (
        ("cs", 1, 3),
    ),
    ("fb", 1, 0): (
        ("ct", 1, 2),
        ("s", 1, 1, 0, 2),
        ("s", 1, 0, "y", 2),
        ("s", 1, 2, 1, 2),
        ("t", 0, 3, 1, 2),
        ("s", 0, 3, 0, 2),
        ("t", 0, 1, 0, 2),
        ("s", 0, 1, "y", 2),
        ("t", 0, 2, 1, 2),
        ("s", 0, 2, "y", 2),
    ),
    ("fb", 1, 1): (
        ("cs", 1, 1),
    ),
    ("fb", 0, 1): (
        ("t", 0, 0, "y", 2),
        ("s", 0, 0, 0, 0),
        ("t", 0, 3, 1, 0),
        ("s", 0, 3, 0, 0),
        ("ct", 1, 0),
        ("s", 1, 1, 0, 0),
        ("s", 1, 2, 1, 0),
        ("t", 0, 1, 0, 0),
        ("t", 0, 2, 1, 0),
    ),
    ("lnb", 0, 0): (
        ("t", 0, 3, 0, 2),
        ("s", 0, 3, 2, 2),
    ),
    ("ab", 3, 3): (
        ("cs", 2, 3),
        ("t", 1, 1, 0, 2),
        ("s", 1, 1, "y", 2),
    ),
    ("ab", 2, 1): (
        ("t", 0, 3, 0, 0),
        ("s", 0, 3, 2, 0),
        ("t", 0, 1, "y", 2),
        ("s", 0, 1, 1, 0),
        ("t", 1, 0, "y", 2),
        ("s", 1, 0, 2, 0),
        ("t", 0, 3, 2, 2),
        ("s", 0, 3, "y", 2),
        ("t", 1, 2, 1, 2),
        ("s", 1, 2, 0, 2),
    ),
    ("ab", 2, 2): (
        ("t", 0, 2, "y", 2),
        ("s", 0, 2, 0, 0),
    ),
    ("ab", 2, 3): (
        ("ct", 2, 2),
        ("s", 2, 1, 0, 2),
        ("s", 2, 2, 1, 2),
        ("s", 2, 0, "y", 2),
        ("t", 0, 0, 0, 0),
        ("s", 0, 0, 1, 0),
    ),
    ("ab", 1, 1): (
        ("t", 0, 3, 2, 0),
        ("t", 0, 3, "y", 2),
        ("t", 1, 2, 1, 0),
        ("s", 1, 2, 0, 0),
    ),
    ("ab", 1, 2): (
        ("t", 1, 1, 0, 0),
        ("t", 1, 1, "y", 2),
        ("s", 1, 1, 1, 0),
    ),
    ("ab", 1, 3): (
        ("cs", 2, 1),
        ("t", 0, 1, 1, 0),
        ("s", 0, 1, 2, 0),
    ),
    ("ab", 0, 0): (
        ("t", 0, 2, 0, 0),
        ("s", 0, 2, 2, 0),
        ("t", 1, 0, 2, 0),
        ("s", 1, 0, 0, 0),
    ),
    ("ab", 0, 1): (
        ("t", 1, 2, 0, 2),
        ("s", 1, 2, "y", 2),
    ),
    ("ab", 0, 3): (
        ("ms", 0),
        ("ct", 2, 0),
        ("s", 2, 1, 0, 0),
        ("s", 2, 2, 1, 0),
        ("t", 0, 0, 1, 0),
        ("s", 0, 0, 2, 0),
    ),
    ("end", 0, 0): (
        ("mt", 0),
        ("ms", 1),
        ("t", 2, 0, "y", 2),
        ("s", 2, 0, 0, 0),
        ("t", 1, 2, 0, 0),
        ("t", 2, 2, 1, 2),
        ("s", 2, 2, 0, 2),
        ("t", 2, 1, 0, 2),
        ("s", 2, 1, "y", 2),
        ("t", 1, 1, 1, 0),
        ("s", 1, 1, 2, 0),
        ("t", 1, 2, "y", 2),
        ("s", 1, 2, 2, 0),
        ("t", 1, 0, 0, 0),
        ("s", 1, 0, 1, 0),
        ("t", 0, 2, 2, 0),
        ("t", 0, 1, 2, 0),
        ("mt", 1),
        ("ms", 2),
        ("t", 0, 0, 2, 0),
        ("t", 1, 1, 2, 0),
        ("t", 2, 1, 0, 0),
        ("t", 2, 1, "y", 2),
        ("s", 2, 1, 1, 0),
        ("t", 2, 2, 1, 0),
        ("s", 2, 2, 0, 0),
        ("t", 2, 0, 0, 0),
        ("s", 2, 0, 1, 0),
        ("t", 1, 2, 2, 0),
        ("t", 1, 0, 1, 0),
        ("t", 2, 2, 0, 2),
        ("s", 2, 2, "y", 2),
        ("mt", 2),
        ("ms", 3),
        ("t", 2, 1, 1, 0),
        ("s", 2, 1, 2, 0),
        ("t", 2, 2, 0, 0),
        ("t", 2, 0, 1, 0),
        ("s", 2, 0, 2, 0),
        ("t", 2, 2, "y", 2),
        ("s", 2, 2, 2, 0),
        ("mt", 3),
        ("ms", 4),
        ("t", 2, 1, 2, 0),
        ("t", 2, 0, 2, 0),
        ("t", 2, 2, 2, 0),
        ("mt", 4),
    ),
}


def mm(a, b, da, db):
    return lax.dot_general(a, b, (((da,), (db,)), ((), ())), preferred_element_type=F32)


def nn(a, b):
    return mm(a, b, 1, 0)


def nt(a, b):
    return mm(a, b, 1, 1)


def tn(a, b):
    return mm(a, b, 0, 0)


def iota(shape, dim):
    return lax.broadcasted_iota(jnp.int32, shape, dim)


def page_scalars(pages_ref, line, half):
    total = jnp.int32(0)
    begin = jnp.int32(0)
    bounds = []
    for k in range(pages_ref.shape[1]):
        length = pages_ref[line, k]
        begin = begin + jnp.where(length == half, total, 0)
        total = total + length
        bounds.append(total)
    return begin, bounds


def page_numbers(places, bounds):
    number = jnp.zeros(places.shape, jnp.int32)
    for bound in bounds:
        number = number + (places >= bound).astype(jnp.int32)
    return number


def half_lanes(which):
    return ((iota((1, 128), 1) // HEAD_DIM) == which).astype(BF)


def norm_stats(signal):
    mean = jnp.mean(signal, axis=1, keepdims=True)
    center = signal - mean
    spread = jnp.mean(center * center, axis=1, keepdims=True)
    scale = lax.rsqrt(spread + EPSILON)
    return center * scale, scale


def norm_back(grad, hat, scale, gain):
    scaled = grad * gain
    return scale * (
        scaled
        - jnp.mean(scaled, axis=1, keepdims=True)
        - hat * jnp.mean(scaled * hat, axis=1, keepdims=True)
    )


MESH = pl.DeviceIdType.MESH
SMALL_ROWS = 16


class Net:
    def __init__(self, bits):
        t = lax.axis_index("tensor")
        d = lax.axis_index("dp")
        self.t = t
        self.core = {"tensor": t + 1 - 2 * (t % 2)}
        self.y = {"tensor": (t + 2) % 4}
        self.bit = [(d // 2 ** b) % 2 for b in bits]
        self.dp = [{"dp": d + 2 ** b * (1 - 2 * k)} for b, k in zip(bits, self.bit)]


def remote(source, target, sems, index, partner):
    return pltpu.make_async_remote_copy(
        src_ref=source,
        dst_ref=target,
        send_sem=sems.at[0, index],
        recv_sem=sems.at[1, index],
        device_id=partner,
        device_id_type=MESH,
    )


def rows_at(ref, start, count):
    return ref.at[pl.ds(pl.multiple_of(start, 16), count), :]


class Piece:
    def __init__(self, net, own, slots, start, count, axes, sems, first):
        self.net, self.own, self.slots, self.start, self.count = net, own, slots, start, count
        self.axes, self.sems, self.first = axes, sems, first

    def region(self, hop, flip):
        index, weight = 0, 1
        for axis in self.axes[hop - 1 :]:
            bit = self.net.bit[axis]
            index = index + weight * ((1 - bit) if flip and weight == 1 else bit)
            weight *= 2
        rows = self.count // weight
        return self.start + index * rows, rows

    def hop(self, number, arriving=False):
        if number == len(self.axes) + 1:
            here = rows_at(self.slots(2), self.start, self.count)
            there, partner = rows_at(self.slots(3), self.start, self.count), self.net.core
        elif number == 0:
            start, rows = self.region(1, False)
            here, partner = rows_at(self.own, start, rows), self.net.y
            there = rows_at(self.slots(2), start, rows)
        else:
            here = there = rows_at(self.slots(2), *self.region(number, arriving))
            partner = self.net.dp[self.axes[number - 1]]
        return remote(here, there, self.sems, self.first + number, partner)

    def sent(self):
        for number in range(len(self.axes) + 2):
            self.hop(number).wait_send()


SHARED = 9
class Stage:
    def __init__(self, net, axis, slot, fixed, values, room, index, sems, block):
        self.net, self.axis, self.slot, self.fixed, self.values = net, axis, slot, dict(fixed), values
        self.room, self.index, self.sems, self.block = room, index, sems, block
        self.kept = slot if axis != "y" else 0
        self.partner = net.y if axis == "y" else net.dp[axis]

    def runs(self, bits):
        low = 0
        while low < 3 and low not in bits:
            low += 1
        starts = [0]
        for k in range(low, 3):
            choice = [bits[k]] if k in bits else [0, 1]
            starts = [start + value * (2 ** k * self.block) for start in starts for value in choice]
        return [(start, 2 ** low * self.block) for start in starts]

    def theirs(self):
        bits = dict(self.fixed)
        if self.axis != "y":
            bits[self.axis] = 1 - self.net.bit[self.axis]
        return self.runs(bits)

    def ours(self):
        bits = dict(self.fixed)
        if self.axis != "y":
            bits[self.axis] = self.net.bit[self.axis]
        return self.runs(bits)

    def send(self):
        at = 0
        for start, count in self.theirs():
            remote(
                self.values(self.slot, start, count), self.room(at, count),
                self.sems, self.index, self.partner,
            ).start()
            at += count

    def all_of_it(self):
        total = sum(count for _, count in self.ours())
        return remote(self.room(0, total), self.room(0, total), self.sems, self.index, self.partner)

    def take(self):
        self.all_of_it().wait_recv()
        at = 0
        for start, count in self.ours():
            here = self.values(self.kept, start, count)
            here[...] = here[...] + self.room(at, count)[...]
            at += count

    def sent(self):
        self.all_of_it().wait_send()


def chunk_stages(net, order, lanes, slots, got, sems, first, block):
    def values(slot, start, count):
        return slots(slot).at[pl.ds(pl.multiple_of(start, 32), count), lanes]

    stages, fixed, live, at = {}, {}, (2, 0), 0
    for axis in order:
        exchanges = (2,) if axis == "y" else live
        for slot in exchanges:
            count = (8 * block) >> (len(fixed) + (axis != "y"))
            room = lambda start, rows, at=at: got.at[pl.ds(at + start, rows), lanes]
            stages[(axis, slot)] = Stage(
                net, axis, slot, fixed, values, room, first + len(stages), sems, block
            )
            at += count
        if axis == "y":
            live = (0,)
        else:
            fixed[axis] = net.bit[axis]
    return stages


def layer_kernel(
    bits,
    pages_ref, x_ref, cells_ref, shift_ref, es_ref, tables_ref, ms_ref, rs_ref, gain_ref, nshift_ref,
    aw_hbm, mw_hbm, ew_hbm, rw_hbm, cot_hbm,
    out_ref, gin_ref, gaw_ref, gmw_ref, gew_ref, grw_ref, both_ref,
    AW, MW, EW, RW, XR, HOT, BACK, Q, K, V, PR, CTX, NB, HAT, SCALE, AS, ACC, GB, GC, DQ, DK, DV, E, DD, SM,
    FROM_CORE, FROM, MIX, SUMS, SUMS_CORE, SUMS_FAR,
    in_sems, own_sems, small_sems, local_sems,
    unit_sems, stage_sems, total_sems,
):
    net = Net(bits)
    rows, width = x_ref.shape
    half = rows // 2
    local = aw_hbm.shape[1]
    heads = local // HEAD_DIM
    hidden = ew_hbm.shape[1]

    barrier = pltpu.get_barrier_semaphore()
    greeted = (net.core, net.y, net.dp[0], net.dp[1], net.dp[2])
    for partner in greeted:
        pl.semaphore_signal(barrier, inc=1, device_id=partner, device_id_type=MESH)

    SM[0, 0:2, :local] = shift_ref[...].astype(F32)
    SM[0, 2:3, :] = es_ref[...].reshape(1, hidden).astype(F32)
    for h in range(heads):
        SM[0, 8 + 2 * h : 10 + 2 * h, :BUCKETS] = tables_ref[h].astype(F32)

    whole_of = {
        "aw0": (aw_hbm.at[0], lambda s: AW.at[s, 0]),
        "aw1": (aw_hbm.at[1], lambda s: AW.at[s, 1]),
        "aw2": (aw_hbm.at[2], lambda s: AW.at[s, 2]),
        "mw": (mw_hbm, lambda s: MW.at[s]),
        "ew": (ew_hbm, lambda s: EW.at[s]),
        "rw": (rw_hbm, lambda s: RW.at[s]),
    }
    pieces = [
        Piece(net, *whole_of[name], start, count, axes, in_sems, 4 * n)
        for n, (name, start, count, axes) in enumerate(PIECES)
    ]
    weights = ((aw_hbm, AW), (mw_hbm, MW), (ew_hbm, EW), (rw_hbm, RW))
    keep_own = [
        pltpu.make_async_copy(own, ref.at[0], local_sems.at[n]) for n, (own, ref) in enumerate(weights)
    ]
    give_own = [remote(own, ref.at[1], own_sems, n, net.core) for n, (own, ref) in enumerate(weights)]
    small_core = remote(SM.at[0], SM.at[1], small_sems, 0, net.core)
    small_y = remote(SM.at[0], SM.at[2], small_sems, 1, net.y)
    small_far = remote(SM.at[2], SM.at[3], small_sems, 2, net.core)
    fetch_cot = pltpu.make_async_copy(cot_hbm, GB, local_sems.at[4])

    keep_own[0].start()
    keep_own[1].start()
    pl.semaphore_wait(barrier, len(greeted))
    block = width // 8
    units = (
        (lambda slot: RW.at[slot]),
        (lambda slot: EW.at[slot]),
        (lambda slot: AS.at[slot, pl.ds(0, width), :]),
    )
    flows, first = {}, 0
    for unit, chunks in enumerate(CHUNKS):
        for chunk, (lane, lanes, order) in enumerate(chunks):
            stages = chunk_stages(
                net, order, pl.ds(lane, lanes), units[unit], FROM.at[unit], stage_sems, first, block
            )
            flows[unit, chunk] = stages
            first += len(stages)

    def to_core(unit, slot):
        return remote(
            units[unit](slot), FROM_CORE.at[unit, slot // 2], unit_sems, unit * 2 + slot // 2, net.core
        )

    def add_core(unit, slot):
        to_core(unit, slot + 1).wait_recv()
        here = units[unit](slot)
        here[...] = here[...] + FROM_CORE[unit, slot // 2]

    sums_core = [
        remote(SUMS.at[2 * n + 1], SUMS_CORE.at[n], total_sems, n, net.core) for n in range(2)
    ]
    sums_far = [
        remote(SUMS.at[2 - 2 * (n > 0)], SUMS_FAR.at[n], total_sems, 2 + n, partner)
        for n, partner in enumerate([net.y] + net.dp)
    ]
    shared = slice(SHARED, SHARED + 6)

    def send_totals(k):
        if k == 0:
            for copy in sums_core:
                copy.start()
        else:
            sums_far[k - 1].start()

    def take_totals(k):
        if k == 0:
            for n, copy in enumerate(sums_core):
                copy.wait_recv()
                SUMS[2 * n] = SUMS[2 * n] + SUMS_CORE[n]
            SUMS[2, shared, :] = SUMS[0, shared, :]
        else:
            sums_far[k - 1].wait_recv()
            if k > 1:
                sums_far[k - 1].wait_send()
            SUMS[0] = SUMS[0] + SUMS_FAR[k - 1]

    results = (grw_ref, gew_ref, MIX)

    def take(unit, chunk, axis, slot):
        stages = flows[unit, chunk]
        stage = stages[axis, slot]
        if stage is not list(stages.values())[-1]:
            stage.take()
            return
        stage.all_of_it().wait_recv()
        (start, count), = stage.ours()
        lane, lanes, _ = CHUNKS[unit][chunk]
        mine = stage.values(0, start, count)[...].astype(F32)
        results[unit][:, lane : lane + lanes] = mine + stage.room(0, count)[...].astype(F32)

    def act(kind, *what):
        if kind == "gs":
            pieces[what[0]].hop(what[1]).start()
        elif kind == "gt":
            pieces[what[0]].hop(what[1] - 1, True).wait_recv()
        elif kind == "cs":
            to_core(*what).start()
        elif kind == "ct":
            add_core(*what)
        elif kind == "s":
            flows[what[0], what[1]][what[2], what[3]].send()
        elif kind == "t":
            take(*what)
        elif kind == "ms":
            send_totals(*what)
        else:
            take_totals(*what)

    def do(actions):
        for action in actions:
            act(*action)

    def at(phase, point, index=None, before=None):
        if index is None:
            do(PLAN.get((phase, 0, point), ()))
            return
        for r in range(4):
            first = (before or {}).get(r, ())
            actions = PLAN.get((phase, r, point), ())
            if first or actions:

                @pl.when(index == r)
                def _():
                    for wait in first:
                        wait()
                    do(actions)

    small_y.start()
    at("start", 0)
    small_core.start()
    for copy in give_own:
        copy.start()
    keep_own[2].start()
    keep_own[3].start()
    fetch_cot.start()

    begin, bounds = page_scalars(pages_ref, net.t, half)
    perm = (iota((rows, rows), 1) == ((iota((rows, rows), 0) + begin) & (rows - 1))).astype(BF)
    XR[...] = nn(perm, x_ref[...]).astype(BF)
    bucket = iota((BUCKETS, rows), 0)
    mine = pl.ds(pl.multiple_of(net.t * rows, 128), rows)
    one = (cells_ref[0:1, mine] == bucket).astype(BF)
    two = (cells_ref[1:2, mine] == bucket).astype(BF)
    HOT[...] = nt(perm, jnp.concatenate([one, two, one, two], axis=0)).astype(BF)
    one = (cells_ref[0:1, mine] == BUCKETS - 1 - bucket).astype(BF)
    two = (cells_ref[1:2, mine] == BUCKETS - 1 - bucket).astype(BF)
    BACK[...] = nt(perm, jnp.concatenate([one, two], axis=0)).astype(BF)
    ACC[...] = XR[...].astype(F32) + ms_ref[...].reshape(1, width).astype(F32)
    for ref in (Q, K, V):
        for s in range(4):
            ref[s, :, local:] = jnp.zeros((rows, 256 - local), BF)
    GC[:, local:] = jnp.zeros((rows, 256 - local), BF)
    DD[:, :local] = jnp.zeros((rows, local), BF)
    col = page_numbers((iota((half, 1), 0) + (half + begin)) & (rows - 1), bounds)
    row = page_numbers((iota((1, half), 1) + (half + begin)) & (rows - 1), bounds)

    spot = iota((BUCKETS, 128), 1)
    spot = jnp.where(spot < 64, spot, spot - 128)
    fold = (iota((BUCKETS, 128), 0) == jnp.clip(BUCKETS // 2 - spot, 0, BUCKETS - 1)).astype(BF)

    fold_f32 = fold.astype(F32)

    keep_own[0].wait()
    keep_own[1].wait()

    def attend(r, _):
        at(
            "att", 0, r,
            {
                1: [small_core.wait_recv, give_own[0].wait_recv, give_own[1].wait_recv],
                2: [small_y.wait_recv, small_far.start],
                3: [small_far.wait_recv],
            },
        )
        line = nn(SM[r, 8 : 8 + 2 * heads, :BUCKETS].astype(BF), fold)
        lanes_at = iota((BUCKETS, 128), 1)
        tiles = []
        for a in range(2):
            parts = []
            for pair in range(2):
                total = jnp.zeros((BUCKETS, 128), F32)
                for which in range(min(2, heads - 2 * pair)):
                    off = which * HEAD_DIM + a * BUCKETS
                    h = (2 * pair + which) * 2 + a
                    spread = jnp.broadcast_to(line[h : h + 1, :], (BUCKETS, 128))
                    spread = pltpu.roll(spread, off, axis=1, stride=1, stride_axis=0)
                    inside = (lanes_at >= off) & (lanes_at < off + BUCKETS)
                    total = jnp.where(inside, spread, total)
                parts.append(total.astype(BF))
            tiles.append(jnp.concatenate(parts, axis=1))
        pairs = jnp.concatenate(tiles, axis=0)
        left = nn(HOT[:, : 2 * BUCKETS], pairs).astype(BF)

        queries = (nt(XR[...], AW[r, 0]) + SM[r, 0:1, :local]).astype(BF)
        Q[r, :, :local] = queries * jnp.asarray(HEAD_DIM ** -0.5, BF)
        K[r, :, :local] = nt(XR[...], AW[r, 1]).astype(BF)
        V[r, :, :local] = (nt(XR[...], AW[r, 2]) + SM[r, 1:2, :local]).astype(BF)
        at("att", 1, r)
        same = col == row
        for block in range(2):
            span = slice(block * half, (block + 1) * half)
            if block == 1:
                at("att", 2, r)
            for pair in range(2):
                lanes = slice(pair * 128, (pair + 1) * 128)
                key_side = jnp.concatenate([K[r, span, lanes], HOT[span, :]], axis=1)
                total = None
                for which in range(min(2, heads - 2 * pair)):
                    keep = half_lanes(which)
                    query_side = jnp.concatenate(
                        [Q[r, span, lanes] * keep, left[span, lanes] * keep], axis=1
                    )
                    scores = nt(key_side, query_side)
                    if block == 1:
                        scores = jnp.where(same, scores, MASKED)
                    weights = jnp.exp(scores - jnp.max(scores, axis=0, keepdims=True))
                    probs = (weights * (1.0 / jnp.sum(weights, axis=0, keepdims=True))).astype(BF)
                    PR[r, (2 * pair + which) * 2 + block] = probs
                    part = tn(probs, V[r, span, lanes]) * keep.astype(F32)
                    total = part if total is None else total + part
                CTX[r, span, lanes] = total.astype(BF)
        at("att", 3, r)
        ACC[...] += nn(CTX[r, :, :local], MW[r])
        return 0

    lax.fori_loop(0, 4, attend, 0)

    hat, scale = norm_stats(ACC[...])
    HAT[...] = hat
    SCALE[...] = scale
    normed = hat * gain_ref[0:1, :].astype(F32) + nshift_ref[0:1, :].astype(F32)
    NB[...] = normed.astype(BF)
    ACC[...] = normed + rs_ref[...].reshape(1, width).astype(F32)
    keep_own[2].wait()
    keep_own[3].wait()

    def feed(r, _):
        at("feed", 0, r, {1: [give_own[2].wait_recv, give_own[3].wait_recv]})
        pre = nn(NB[...], EW[r]) + SM[r, 2:3, :]
        gate = 0.5 * (1.0 + lax.erf(pre * (0.5 ** 0.5)))
        AS[r, :rows] = (pre * gate).astype(BF)
        AS[r, rows:] = (
            gate + pre * (jnp.exp(-0.5 * (pre * pre)) * (1.0 / math.sqrt(2.0 * math.pi)))
        ).astype(BF)
        at("feed", 1, r)
        ACC[...] += nn(AS[r, :rows], RW[r])
        return 0

    lax.fori_loop(0, 4, feed, 0)

    fetch_cot.wait()
    hat, scale = norm_stats(ACC[...])
    gain = gain_ref[1:2, :].astype(F32)
    result = (hat * gain + nshift_ref[1:2, :].astype(F32)).astype(BF)
    perm = (iota((rows, rows), 1) == ((iota((rows, rows), 0) + begin) & (rows - 1))).astype(BF)
    out_ref[...] = result
    cot = nn(perm, GB[...])
    grad = norm_back(cot, hat, scale, gain)
    ACC[...] = grad
    GB[...] = grad.astype(BF)
    shared_two = (
        jnp.sum(cot * hat, axis=0, keepdims=True),
        jnp.sum(cot, axis=0, keepdims=True),
        jnp.sum(grad, axis=0, keepdims=True),
    )
    for n, line in enumerate(shared_two):
        SUMS[0, SHARED + 3 + n : SHARED + 4 + n, :] = line

    for (name, *_), piece in zip(PIECES, pieces):
        if name in ("ew", "rw"):
            piece.sent()

    def reduce_back(i, _):
        r = 3 - i
        grad_pre = (nt(GB[...], RW[r]) * AS[r, rows:].astype(F32)).astype(BF)
        AS[r, rows:] = grad_pre
        SUMS[r, 0:1, :] = jnp.sum(grad_pre.astype(F32), axis=0, keepdims=True)
        at("fa", 0, r)
        RW[r] = tn(GB[...], AS[r, :rows]).astype(BF)
        at("fa", 1, r)
        return 0

    lax.fori_loop(0, 4, reduce_back, 0)

    def expand_back(i, _):
        r = 3 - i
        ACC[...] += nt(AS[r, rows:], EW[r])
        at("fb", 0, r)
        EW[r] = tn(NB[...], AS[r, rows:]).astype(BF)
        at("fb", 1, r)
        return 0

    lax.fori_loop(0, 4, expand_back, 0)

    grad = ACC[...]
    hat = HAT[...]
    gone = norm_back(grad, hat, SCALE[...], gain_ref[0:1, :].astype(F32))
    ACC[...] = gone
    GB[...] = gone.astype(BF)
    shared_one = (
        jnp.sum(grad * hat, axis=0, keepdims=True),
        jnp.sum(grad, axis=0, keepdims=True),
        jnp.sum(gone, axis=0, keepdims=True),
    )
    for n, line in enumerate(shared_one):
        SUMS[0, SHARED + n : SHARED + 1 + n, :] = line

    at("lnb", 0)

    def attend_back(i, _):
        r = 3 - i

        GC[:, :local] = nt(GB[...], MW[r]).astype(BF)
        at("ab", 0, r)
        for block in range(2):
            span = slice(block * half, (block + 1) * half)
            for pair in range(2):
                lanes = slice(pair * 128, (pair + 1) * 128)
                key_side = jnp.concatenate([K[r, span, lanes], HOT[span, :]], axis=1)
                sums = None
                for which in range(min(2, heads - 2 * pair)):
                    keep = half_lanes(which)
                    wide = keep.astype(F32)
                    probs = PR[r, (2 * pair + which) * 2 + block]
                    grad_probs = nt(V[r, span, lanes] * keep, GC[span, lanes])
                    soft = probs.astype(F32)
                    inner = jnp.sum(soft * grad_probs, axis=0, keepdims=True)
                    grad_scores = (soft * (grad_probs - inner)).astype(BF)
                    both = tn(grad_scores, key_side)
                    parts = (
                        both[:, :128] * wide,
                        both[:, 128:] * wide,
                        nn(grad_scores, Q[r, span, lanes]) * wide,
                        nn(probs, GC[span, lanes]) * wide,
                    )
                    sums = parts if sums is None else tuple(a + b for a, b in zip(sums, parts))
                DQ[span, lanes] = (sums[0] * (HEAD_DIM ** -0.5)).astype(BF)
                E[span, lanes] = sums[1].astype(BF)
                DK[span, lanes] = sums[2].astype(BF)
                DV[span, lanes] = sums[3].astype(BF)
            at("ab", 1 + block, r)
        for m, ref in enumerate((DQ, DK, DV)):
            DD[:, (m + 1) * local : (m + 2) * local] = ref[:, :local]
            ACC[...] += nn(ref[:, :local], AW[r, m])
        weight_grad = tn(XR[...], DD[...])
        AS[r, :width, 256:] = weight_grad[:, 256:].astype(BF)
        AS[r, :width, :256] = (weight_grad[:, :256] + tn(GB[...], CTX[r])).astype(BF)
        SUMS[r, 1:2, :local] = jnp.sum(DQ[:, :local].astype(F32), axis=0, keepdims=True)
        SUMS[r, 2:3, :local] = jnp.sum(DV[:, :local].astype(F32), axis=0, keepdims=True)
        grad_pairs = tn(BACK[...], E[...])
        lanes_at = iota((BUCKETS, 128), 1)
        for h in range(heads):
            for a in range(2):
                off = (h % 2) * HEAD_DIM + a * BUCKETS
                part = grad_pairs[a * BUCKETS : (a + 1) * BUCKETS, (h // 2) * 128 : (h // 2 + 1) * 128]
                part = jnp.where((lanes_at >= off) & (lanes_at < off + BUCKETS), part, 0.0)
                part = pltpu.roll(part, (129 - BUCKETS - off) % 128, axis=1, stride=1, stride_axis=0)
                SUMS[r, 3 + 2 * h + a : 4 + 2 * h + a, :128] = jnp.sum(part, axis=0, keepdims=True)
        at("ab", 3, r)
        return 0

    SUMS[1, shared, :] = SUMS[0, shared, :]
    lax.fori_loop(0, 4, attend_back, 0)

    at("fin", 0)
    perm = (iota((rows, rows), 1) == ((iota((rows, rows), 0) + begin) & (rows - 1))).astype(BF)
    gin_ref[...] = tn(perm, ACC[...].astype(BF)).astype(BF)
    out_ref[...] = tn(perm, out_ref[...]).astype(BF)
    at("end", 0)
    gmw_ref[...] = jnp.transpose(MIX[:, :256])[:local, :]
    for m in range(3):
        gaw_ref[m] = MIX[:, (m + 1) * local : (m + 2) * local]
    both_ref[...] = SUMS[0]
    for row in range(2 * heads):
        both_ref[3 + row : 4 + row, :BUCKETS] = lax.dot_general(
            both_ref[3 + row : 4 + row, :128], fold_f32, (((1,), (1,)), ((), ())),
            precision=lax.Precision.HIGHEST, preferred_element_type=F32,
        )

    for stages in flows.values():
        for stage in stages.values():
            stage.sent()
    for unit in range(3):
        for slot in (1, 3):
            to_core(unit, slot).wait_send()
    for copy in sums_core + sums_far[:1]:
        copy.wait_send()
    for (name, *_), piece in zip(PIECES, pieces):
        if name not in ("ew", "rw"):
            piece.sent()
    for copy in give_own + [small_core, small_y, small_far]:
        copy.wait_send()


def swap(value, axis, size, bit):
    return lax.ppermute(value, axis, [(i, i ^ bit) for i in range(size)])


def finish_rows(value, dp, bits_done):
    me = lax.axis_index("dp")
    left = dp.bit_length() - 1 - bits_done
    rows, cols = value.shape
    value = value.reshape((2,) * left + (rows >> left, cols))
    for bit in range(left):
        axis = value.ndim - 3
        mine = (me >> bit) & 1
        keep = lax.dynamic_index_in_dim(value, mine, axis, keepdims=False)
        send = lax.dynamic_index_in_dim(value, 1 - mine, axis, keepdims=False)
        value = keep + swap(send, "dp", dp, 1 << bit)
    return value


def finish_kernel(*refs):
    sources, both, targets, small = refs[:6], refs[6], refs[7:13], refs[13:20]
    for source, target in zip(sources, targets):
        target[...] = source[...]
    shifts, merge, gains, norm_shift, expand, reduced, tables = small
    shifts[...] = both[1:3, : shifts.shape[1]]
    for target, row in ((merge, SHARED + 2), (expand, 0), (reduced, SHARED + 5)):
        target[...] = both[row : row + 1, :].reshape(target.shape)
    for target, row in ((gains, SHARED), (norm_shift, SHARED + 1)):
        target[0:1, :] = both[row : row + 1, :]
        target[1:2, :] = both[row + 3 : row + 4, :]
    for h in range(tables.shape[0]):
        tables[h] = both[3 + 2 * h : 5 + 2 * h, :BUCKETS]


def on_device(
    dp,
    inputs,
    layout_cells,
    page_lengths,
    attend_weight,
    attend_shift,
    merge_weight,
    merge_shift,
    norm_gains,
    norm_shifts,
    expand_weight,
    expand_shift,
    reduce_weight,
    reduce_shift,
    bias_tables,
    cotangent,
):
    rows, width = inputs.shape
    half = rows // 2
    local = attend_weight.shape[2]
    heads = bias_tables.shape[1]
    hidden = expand_weight.shape[1]
    top = dp.bit_length() - 1
    bits = (top - 3, top - 2, top - 1)

    sds = jax.ShapeDtypeStruct
    smem = pl.BlockSpec(memory_space=pltpu.SMEM)
    vmem = pl.BlockSpec(memory_space=pltpu.VMEM)
    hbm = pl.BlockSpec(memory_space=pl.ANY)

    def kernel(*refs):
        return layer_kernel(bits, *refs)

    dma = pltpu.SemaphoreType.DMA
    count = sum(len(order) + order.index("y") for chunks in CHUNKS for _, _, order in chunks)
    block = width // 8
    output, input_grad, gaw, gmw, gew, grw, both = pl.pallas_call(
        kernel,
        in_specs=[smem] + [vmem] * 9 + [hbm] * 5,
        out_specs=[vmem] * 7,
        out_shape=[
            sds((rows, width), BF), sds((rows, width), BF), sds((3, block, local), F32),
            sds((local, block), F32), sds((block, hidden), F32), sds((block, hidden), F32),
            sds((SMALL_ROWS, width), F32),
        ],
        scratch_shapes=[
            pltpu.VMEM((4, 3, local, width), BF),
            pltpu.VMEM((4, local, width), BF),
            pltpu.VMEM((4, width, hidden), BF),
            pltpu.VMEM((4, hidden, width), BF),
            pltpu.VMEM((rows, width), BF),
            pltpu.VMEM((rows, 128), BF),
            pltpu.VMEM((rows, 2 * BUCKETS), BF),
            pltpu.VMEM((4, rows, 256), BF),
            pltpu.VMEM((4, rows, 256), BF),
            pltpu.VMEM((4, rows, 256), BF),
            pltpu.VMEM((4, 2 * heads, half, half), BF),
            pltpu.VMEM((4, rows, 256), BF),
            pltpu.VMEM((rows, width), BF),
            pltpu.VMEM((rows, width), F32),
            pltpu.VMEM((rows, 1), F32),
            pltpu.VMEM((4, 2 * rows, hidden), BF),
            pltpu.VMEM((rows, width), F32),
            pltpu.VMEM((rows, width), BF),
            pltpu.VMEM((rows, 256), BF),
            pltpu.VMEM((rows, 256), BF),
            pltpu.VMEM((rows, 256), BF),
            pltpu.VMEM((rows, 256), BF),
            pltpu.VMEM((rows, 256), BF),
            pltpu.VMEM((rows, 4 * local), BF),
            pltpu.VMEM((4, SMALL_ROWS, hidden), F32),
            pltpu.VMEM((3, 2, width, hidden), BF),
            pltpu.VMEM((3, 15 * block, hidden), BF),
            pltpu.VMEM((block, width), F32),
            pltpu.VMEM((4, SMALL_ROWS, width), F32),
            pltpu.VMEM((2, SMALL_ROWS, width), F32),
            pltpu.VMEM((4, SMALL_ROWS, width), F32),
            dma((2, 4 * len(PIECES))), dma((2, 4)), dma((2, 3)), dma((5,)),
            dma((2, 6)), dma((2, count)), dma((2, 6)),
        ],
        compiler_params=pltpu.CompilerParams(
            collective_id=0, has_side_effects=True, vmem_limit_bytes=VMEM_LIMIT
        ),
    )(
        page_lengths, inputs, layout_cells, attend_shift, expand_shift,
        jnp.transpose(bias_tables, (1, 0, 2)), merge_shift, reduce_shift, norm_gains, norm_shifts,
        jnp.transpose(attend_weight, (0, 2, 1)), merge_weight, expand_weight, reduce_weight, cotangent,
    )

    if top > 3:
        grw = finish_rows(grw, dp, 3)
        gew = finish_rows(gew, dp, 3)
        gmw = finish_rows(gmw.T, dp, 3).T
        gaw = jnp.stack([finish_rows(gaw[m], dp, 3) for m in range(3)])
        for bit in range(top - 3):
            both = both + swap(both, "dp", dp, 1 << bit)
    big = (output, input_grad, gaw, gmw, gew, grw)
    done = pl.pallas_call(
        finish_kernel,
        in_specs=[vmem] * 7,
        out_specs=[vmem] * 13,
        out_shape=[sds(a.shape, a.dtype) for a in big]
        + [
            sds((2, local), F32), sds((width,), F32), sds((2, width), F32), sds((2, width), F32),
            sds((hidden,), F32), sds((width,), F32), sds((heads, 2, BUCKETS), F32),
        ],
    )(*big, both)
    output, input_grad, gaw, gmw, gew, grw, shifts, merge, gains, norm_shift, expand, reduced, tables = done
    return (
        output, input_grad, gaw, shifts, gmw, merge, gains, norm_shift, gew, expand, grw.T, reduced,
        jnp.transpose(tables, (1, 0, 2)),
    )


def solution(mesh):
    in_specs = (
        P(("dp", "tensor"), None),
        P(None, "dp"),
        P("dp", None),
        P(None, None, "tensor"),
        P(None, "tensor"),
        P("tensor", None),
        P(),
        P(),
        P(),
        P(None, "tensor"),
        P("tensor"),
        P("tensor", None),
        P(),
        P(None, "tensor", None),
        P(("dp", "tensor"), None),
    )
    out_specs = (
        P(("dp", "tensor"), None),
        P(("dp", "tensor"), None),
        P(None, "dp", "tensor"),
        P(None, "tensor"),
        P("tensor", "dp"),
        P(),
        P(),
        P(),
        P("dp", "tensor"),
        P("tensor"),
        P("tensor", "dp"),
        P(),
        P(None, "tensor", None),
    )

    def run(*arrays):
        return on_device(mesh.shape["dp"], *arrays)

    return jax.shard_map(
        run, mesh=mesh, in_specs=in_specs, out_specs=out_specs, check_vma=False
    )
```

```python
import math

import jax
import jax.numpy as jnp
from jax import lax
from jax.experimental import pallas as pl
from jax.experimental.pallas import tpu as pltpu
from jax.sharding import PartitionSpec as P

HEAD_DIM = 64
BUCKETS = 32
EPSILON = 1e-05
MASKED = -1000000000.0
BF = jnp.bfloat16
F32 = jnp.float32
VMEM_LIMIT = 60 * 1024 * 1024
PIECES = (
    ("ew", 0, 192, (1, 0)),
    ("ew", 192, 192, (1, 0)),
    ("rw", 0, 192, (1, 0)),
    ("aw0", 0, 192, (0, 1)),
    ("rw", 192, 192, ()),
    ("aw1", 0, 192, (1, 0)),
    ("ew", 384, 192, ()),
    ("aw2", 0, 192, (0, 1)),
    ("mw", 0, 192, (0,)),
    ("rw", 384, 192, (1, 0)),
    ("ew", 576, 192, (1,)),
    ("rw", 576, 192, (0, 1)),
)
CHUNKS = (
    (
        (0, 256, ("y", 0, 1, 2)),
        (256, 256, (0, "y", 1, 2)),
        (512, 128, (1, "y", 0, 2)),
        (640, 128, (1, 0, 2, "y")),
    ),
    (
        (0, 128, ("y", 2, 0, 1)),
        (128, 256, (0, "y", 1, 2)),
        (384, 384, (1, 0, "y", 2)),
    ),
    (
        (0, 256, ("y", 0, 1, 2)),
        (256, 256, (0, "y", 1, 2)),
        (512, 256, (1, 0, "y", 2)),
    ),
)
PLAN = {
    ("start", 0, 0): (
        ("gs", 0, 0),
        ("gs", 3, 0),
        ("gs", 5, 0),
    ),
    ("att", 0, 2): (
        ("gs", 7, 0),
    ),
    ("att", 1, 0): (
        ("gs", 8, 0),
        ("gs", 9, 0),
        ("gs", 11, 0),
        ("gt", 0, 1),
        ("gs", 0, 1),
        ("gt", 3, 1),
        ("gs", 3, 1),
    ),
    ("att", 1, 2): (
        ("gs", 1, 0),
        ("gs", 2, 0),
        ("gs", 10, 0),
    ),
    ("att", 1, 3): (
        ("gt", 5, 1),
        ("gs", 5, 1),
    ),
    ("att", 2, 0): (
        ("gs", 4, 0),
        ("gs", 6, 0),
        ("gt", 7, 1),
        ("gs", 7, 1),
        ("gt", 0, 2),
        ("gs", 0, 2),
        ("gt", 3, 2),
        ("gs", 3, 2),
        ("gt", 9, 1),
        ("gs", 9, 1),
        ("gt", 5, 2),
        ("gs", 5, 2),
        ("gt", 8, 1),
        ("gs", 8, 1),
        ("gt", 11, 1),
        ("gs", 11, 1),
        ("gt", 7, 2),
        ("gs", 7, 2),
        ("gt", 1, 1),
        ("gs", 1, 1),
        ("gt", 9, 2),
        ("gs", 9, 2),
        ("gt", 2, 1),
        ("gs", 2, 1),
        ("gt", 3, 3),
        ("gs", 3, 3),
        ("gt", 0, 3),
        ("gs", 0, 3),
        ("gt", 3, 4),
        ("gt", 0, 4),
        ("gt", 7, 3),
        ("gs", 7, 3),
        ("gt", 5, 3),
    ),
    ("att", 2, 1): (
        ("gs", 5, 3),
        ("gt", 7, 4),
    ),
    ("att", 2, 3): (
        ("gt", 1, 2),
        ("gs", 1, 2),
        ("gt", 2, 2),
        ("gs", 2, 2),
        ("gt", 5, 4),
        ("gt", 8, 2),
        ("gs", 8, 2),
        ("gt", 10, 1),
        ("gs", 10, 1),
    ),
    ("att", 3, 1): (
        ("gt", 8, 3),
        ("gt", 11, 2),
        ("gs", 11, 2),
    ),
    ("feed", 0, 0): (
        ("gt", 4, 1),
        ("gs", 4, 1),
        ("gt", 9, 3),
        ("gs", 9, 3),
    ),
    ("feed", 1, 0): (
        ("gt", 4, 2),
        ("gt", 9, 4),
        ("gt", 10, 2),
        ("gs", 10, 2),
    ),
    ("feed", 1, 1): (
        ("gt", 1, 3),
        ("gs", 1, 3),
        ("gt", 2, 3),
        ("gs", 2, 3),
        ("gt", 6, 1),
        ("gs", 6, 1),
        ("gt", 10, 3),
        ("gt", 11, 3),
        ("gs", 11, 3),
    ),
    ("feed", 3, 0): (
        ("gt", 1, 4),
        ("gt", 2, 4),
        ("gt", 6, 2),
        ("gt", 11, 4),
    ),
    ("fa", 3, 1): (
        ("cs", 0, 3),
    ),
    ("fa", 1, 0): (
        ("ct", 0, 2),
        ("s", 0, 0, "y", 2),
        ("s", 0, 3, 1, 2),
        ("s", 0, 1, 0, 2),
        ("s", 0, 2, 1, 2),
    ),
    ("fa", 1, 1): (
        ("cs", 0, 1),
    ),
    ("fb", 3, 0): (
        ("ct", 0, 0),
        ("s", 0, 3, 1, 0),
        ("s", 0, 1, 0, 0),
        ("s", 0, 2, 1, 0),
    ),
    ("fb", 3, 1): (
        ("cs", 1, 3),
    ),
    ("fb", 1, 0): (
        ("ct", 1, 2),
        ("s", 1, 0, "y", 2),
        ("s", 1, 1, 0, 2),
        ("s", 1, 2, 1, 2),
        ("t", 0, 3, 1, 2),
        ("s", 0, 3, 0, 2),
        ("t", 0, 1, 0, 2),
        ("s", 0, 1, "y", 2),
        ("t", 0, 2, 1, 2),
        ("s", 0, 2, "y", 2),
    ),
    ("fb", 1, 1): (
        ("cs", 1, 1),
    ),
    ("fb", 0, 1): (
        ("t", 0, 0, "y", 2),
        ("s", 0, 0, 0, 0),
        ("t", 0, 3, 1, 0),
        ("s", 0, 3, 0, 0),
        ("ct", 1, 0),
        ("s", 1, 1, 0, 0),
        ("s", 1, 2, 1, 0),
        ("t", 0, 1, 0, 0),
        ("t", 0, 2, 1, 0),
    ),
    ("lnb", 0, 0): (
        ("t", 0, 3, 0, 2),
        ("s", 0, 3, 2, 2),
    ),
    ("ab", 3, 3): (
        ("cs", 2, 3),
        ("t", 1, 1, 0, 2),
        ("s", 1, 1, "y", 2),
    ),
    ("ab", 2, 1): (
        ("t", 0, 3, 0, 0),
        ("s", 0, 3, 2, 0),
        ("t", 0, 1, "y", 2),
        ("s", 0, 1, 1, 0),
        ("t", 1, 0, "y", 2),
        ("s", 1, 0, 2, 0),
        ("t", 0, 3, 2, 2),
        ("s", 0, 3, "y", 2),
        ("t", 1, 2, 1, 2),
        ("s", 1, 2, 0, 2),
    ),
    ("ab", 2, 2): (
        ("t", 0, 2, "y", 2),
        ("s", 0, 2, 0, 0),
    ),
    ("ab", 2, 3): (
        ("ct", 2, 2),
        ("s", 2, 1, 0, 2),
        ("s", 2, 0, "y", 2),
        ("s", 2, 2, 1, 2),
        ("t", 0, 0, 0, 0),
        ("s", 0, 0, 1, 0),
    ),
    ("ab", 1, 1): (
        ("t", 0, 3, 2, 0),
        ("t", 0, 3, "y", 2),
        ("t", 1, 2, 1, 0),
        ("s", 1, 2, 0, 0),
    ),
    ("ab", 1, 2): (
        ("t", 1, 1, 0, 0),
        ("t", 1, 1, "y", 2),
        ("s", 1, 1, 1, 0),
    ),
    ("ab", 1, 3): (
        ("cs", 2, 1),
        ("t", 0, 1, 1, 0),
        ("s", 0, 1, 2, 0),
    ),
    ("ab", 0, 0): (
        ("t", 0, 2, 0, 0),
        ("s", 0, 2, 2, 0),
        ("t", 1, 0, 2, 0),
        ("s", 1, 0, 0, 0),
    ),
    ("ab", 0, 1): (
        ("t", 1, 2, 0, 2),
        ("s", 1, 2, "y", 2),
    ),
    ("ab", 0, 3): (
        ("ms", 0),
        ("ct", 2, 0),
        ("s", 2, 1, 0, 0),
        ("s", 2, 2, 1, 0),
        ("t", 0, 0, 1, 0),
        ("s", 0, 0, 2, 0),
    ),
    ("end", 0, 0): (
        ("mt", 0),
        ("ms", 1),
        ("t", 2, 0, "y", 2),
        ("s", 2, 0, 0, 0),
        ("t", 1, 2, 0, 0),
        ("t", 2, 2, 1, 2),
        ("s", 2, 2, 0, 2),
        ("t", 2, 1, 0, 2),
        ("s", 2, 1, "y", 2),
        ("t", 1, 1, 1, 0),
        ("s", 1, 1, 2, 0),
        ("t", 1, 2, "y", 2),
        ("s", 1, 2, 2, 0),
        ("t", 1, 0, 0, 0),
        ("s", 1, 0, 1, 0),
        ("t", 0, 2, 2, 0),
        ("t", 0, 1, 2, 0),
        ("mt", 1),
        ("ms", 2),
        ("t", 0, 0, 2, 0),
        ("t", 1, 1, 2, 0),
        ("t", 2, 1, 0, 0),
        ("t", 2, 1, "y", 2),
        ("s", 2, 1, 1, 0),
        ("t", 2, 2, 1, 0),
        ("s", 2, 2, 0, 0),
        ("t", 2, 0, 0, 0),
        ("s", 2, 0, 1, 0),
        ("t", 1, 2, 2, 0),
        ("t", 1, 0, 1, 0),
        ("t", 2, 2, 0, 2),
        ("s", 2, 2, "y", 2),
        ("mt", 2),
        ("ms", 3),
        ("t", 2, 1, 1, 0),
        ("s", 2, 1, 2, 0),
        ("t", 2, 2, 0, 0),
        ("t", 2, 0, 1, 0),
        ("s", 2, 0, 2, 0),
        ("t", 2, 2, "y", 2),
        ("s", 2, 2, 2, 0),
        ("mt", 3),
        ("ms", 4),
        ("t", 2, 1, 2, 0),
        ("t", 2, 0, 2, 0),
        ("t", 2, 2, 2, 0),
        ("mt", 4),
    ),
}


def mm(a, b, da, db):
    return lax.dot_general(a, b, (((da,), (db,)), ((), ())), preferred_element_type=F32)


def nn(a, b):
    return mm(a, b, 1, 0)


def nt(a, b):
    return mm(a, b, 1, 1)


def tn(a, b):
    return mm(a, b, 0, 0)


def iota(shape, dim):
    return lax.broadcasted_iota(jnp.int32, shape, dim)


def page_scalars(pages_ref, line, half):
    total = jnp.int32(0)
    begin = jnp.int32(0)
    bounds = []
    for k in range(pages_ref.shape[1]):
        length = pages_ref[line, k]
        begin = begin + jnp.where(length == half, total, 0)
        total = total + length
        bounds.append(total)
    return begin, bounds


def page_numbers(places, bounds):
    number = jnp.zeros(places.shape, jnp.int32)
    for bound in bounds:
        number = number + (places >= bound).astype(jnp.int32)
    return number


def half_lanes(which):
    return ((iota((1, 128), 1) // HEAD_DIM) == which).astype(BF)


def norm_stats(signal):
    mean = jnp.mean(signal, axis=1, keepdims=True)
    center = signal - mean
    spread = jnp.mean(center * center, axis=1, keepdims=True)
    scale = lax.rsqrt(spread + EPSILON)
    return center * scale, scale


def norm_back(grad, hat, scale, gain):
    scaled = grad * gain
    return scale * (
        scaled
        - jnp.mean(scaled, axis=1, keepdims=True)
        - hat * jnp.mean(scaled * hat, axis=1, keepdims=True)
    )


MESH = pl.DeviceIdType.MESH
SMALL_ROWS = 16


class Net:
    def __init__(self, bits):
        t = lax.axis_index("tensor")
        d = lax.axis_index("dp")
        self.t = t
        self.core = {"tensor": t + 1 - 2 * (t % 2)}
        self.y = {"tensor": (t + 2) % 4}
        self.bit = [(d // 2 ** b) % 2 for b in bits]
        self.dp = [{"dp": d + 2 ** b * (1 - 2 * k)} for b, k in zip(bits, self.bit)]


def remote(source, target, sems, index, partner):
    return pltpu.make_async_remote_copy(
        src_ref=source,
        dst_ref=target,
        send_sem=sems.at[0, index],
        recv_sem=sems.at[1, index],
        device_id=partner,
        device_id_type=MESH,
    )


def rows_at(ref, start, count):
    return ref.at[pl.ds(pl.multiple_of(start, 16), count), :]


class Piece:
    def __init__(self, net, own, slots, start, count, axes, sems, first):
        self.net, self.own, self.slots, self.start, self.count = net, own, slots, start, count
        self.axes, self.sems, self.first = axes, sems, first

    def region(self, hop, flip):
        index, weight = 0, 1
        for axis in self.axes[hop - 1 :]:
            bit = self.net.bit[axis]
            index = index + weight * ((1 - bit) if flip and weight == 1 else bit)
            weight *= 2
        rows = self.count // weight
        return self.start + index * rows, rows

    def hop(self, number, arriving=False):
        if number == len(self.axes) + 1:
            here = rows_at(self.slots(2), self.start, self.count)
            there, partner = rows_at(self.slots(3), self.start, self.count), self.net.core
        elif number == 0:
            start, rows = self.region(1, False)
            here, partner = rows_at(self.own, start, rows), self.net.y
            there = rows_at(self.slots(2), start, rows)
        else:
            here = there = rows_at(self.slots(2), *self.region(number, arriving))
            partner = self.net.dp[self.axes[number - 1]]
        return remote(here, there, self.sems, self.first + number, partner)

    def sent(self):
        for number in range(len(self.axes) + 2):
            self.hop(number).wait_send()


SHARED = 9
class Stage:
    def __init__(self, net, axis, slot, fixed, values, room, index, sems, block):
        self.net, self.axis, self.slot, self.fixed, self.values = net, axis, slot, dict(fixed), values
        self.room, self.index, self.sems, self.block = room, index, sems, block
        self.kept = slot if axis != "y" else 0
        self.partner = net.y if axis == "y" else net.dp[axis]

    def runs(self, bits):
        low = 0
        while low < 3 and low not in bits:
            low += 1
        starts = [0]
        for k in range(low, 3):
            choice = [bits[k]] if k in bits else [0, 1]
            starts = [start + value * (2 ** k * self.block) for start in starts for value in choice]
        return [(start, 2 ** low * self.block) for start in starts]

    def theirs(self):
        bits = dict(self.fixed)
        if self.axis != "y":
            bits[self.axis] = 1 - self.net.bit[self.axis]
        return self.runs(bits)

    def ours(self):
        bits = dict(self.fixed)
        if self.axis != "y":
            bits[self.axis] = self.net.bit[self.axis]
        return self.runs(bits)

    def send(self):
        at = 0
        for start, count in self.theirs():
            remote(
                self.values(self.slot, start, count), self.room(at, count),
                self.sems, self.index, self.partner,
            ).start()
            at += count

    def all_of_it(self):
        total = sum(count for _, count in self.ours())
        return remote(self.room(0, total), self.room(0, total), self.sems, self.index, self.partner)

    def take(self):
        self.all_of_it().wait_recv()
        at = 0
        for start, count in self.ours():
            here = self.values(self.kept, start, count)
            here[...] = here[...] + self.room(at, count)[...]
            at += count

    def sent(self):
        self.all_of_it().wait_send()


def chunk_stages(net, order, lanes, slots, got, sems, first, block):
    def values(slot, start, count):
        return slots(slot).at[pl.ds(pl.multiple_of(start, 32), count), lanes]

    stages, fixed, live, at = {}, {}, (2, 0), 0
    for axis in order:
        exchanges = (2,) if axis == "y" else live
        for slot in exchanges:
            count = (8 * block) >> (len(fixed) + (axis != "y"))
            room = lambda start, rows, at=at: got.at[pl.ds(at + start, rows), lanes]
            stages[(axis, slot)] = Stage(
                net, axis, slot, fixed, values, room, first + len(stages), sems, block
            )
            at += count
        if axis == "y":
            live = (0,)
        else:
            fixed[axis] = net.bit[axis]
    return stages


def layer_kernel(
    bits,
    pages_ref, cells_ref, shift_ref, es_ref, tables_ref, ms_ref, rs_ref, gain_ref, nshift_ref,
    aw_hbm, mw_hbm, ew_hbm, rw_hbm, cot_hbm, x_hbm,
    gaw_ref, gmw_ref, both_ref, out_hbm, gin_hbm, gew_hbm, grw_hbm,
    AW, MW, EW, RW, XR, HOT, BACK, Q, K, V, PR, CTX, NB, HAT, SCALE, AS, ACC, GB, GC, DQ, DK, DV, E, DD, SM,
    FROM_CORE, FROM, GRW, GEW, MIX, RESULT, SUMS, SUMS_CORE, SUMS_FAR,
    in_sems, own_sems, small_sems, local_sems,
    unit_sems, stage_sems, total_sems,
):
    net = Net(bits)
    rows, width = x_hbm.shape
    half = rows // 2
    local = aw_hbm.shape[1]
    heads = local // HEAD_DIM
    hidden = ew_hbm.shape[1]

    fetch_x = pltpu.make_async_copy(x_hbm, NB, local_sems.at[5])
    fetch_x.start()

    barrier = pltpu.get_barrier_semaphore()
    greeted = (net.core, net.y, net.dp[0], net.dp[1], net.dp[2])
    for partner in greeted:
        pl.semaphore_signal(barrier, inc=1, device_id=partner, device_id_type=MESH)

    SM[0, 0:2, :local] = shift_ref[...].astype(F32)
    SM[0, 2:3, :] = es_ref[...].reshape(1, hidden).astype(F32)
    for h in range(heads):
        SM[0, 8 + 2 * h : 10 + 2 * h, :BUCKETS] = tables_ref[h].astype(F32)

    whole_of = {
        "aw0": (aw_hbm.at[0], lambda s: AW.at[s, 0]),
        "aw1": (aw_hbm.at[1], lambda s: AW.at[s, 1]),
        "aw2": (aw_hbm.at[2], lambda s: AW.at[s, 2]),
        "mw": (mw_hbm, lambda s: MW.at[s]),
        "ew": (ew_hbm, lambda s: EW.at[s]),
        "rw": (rw_hbm, lambda s: RW.at[s]),
    }
    pieces = [
        Piece(net, *whole_of[name], start, count, axes, in_sems, 4 * n)
        for n, (name, start, count, axes) in enumerate(PIECES)
    ]
    weights = ((aw_hbm, AW), (mw_hbm, MW), (ew_hbm, EW), (rw_hbm, RW))
    keep_own = [
        pltpu.make_async_copy(own, ref.at[0], local_sems.at[n]) for n, (own, ref) in enumerate(weights)
    ]
    give_own = [remote(own, ref.at[1], own_sems, n, net.core) for n, (own, ref) in enumerate(weights)]
    small_core = remote(SM.at[0], SM.at[1], small_sems, 0, net.core)
    small_y = remote(SM.at[0], SM.at[2], small_sems, 1, net.y)
    small_far = remote(SM.at[2], SM.at[3], small_sems, 2, net.core)
    fetch_cot = pltpu.make_async_copy(cot_hbm, GB, local_sems.at[4])

    keep_own[0].start()
    keep_own[1].start()
    pl.semaphore_wait(barrier, len(greeted))
    block = width // 8
    units = (
        (lambda slot: RW.at[slot]),
        (lambda slot: EW.at[slot]),
        (lambda slot: AS.at[slot, pl.ds(0, width), :]),
    )
    flows, first = {}, 0
    for unit, chunks in enumerate(CHUNKS):
        for chunk, (lane, lanes, order) in enumerate(chunks):
            stages = chunk_stages(
                net, order, pl.ds(lane, lanes), units[unit], FROM.at[unit], stage_sems, first, block
            )
            flows[unit, chunk] = stages
            first += len(stages)

    def to_core(unit, slot):
        return remote(
            units[unit](slot), FROM_CORE.at[unit, slot // 2], unit_sems, unit * 2 + slot // 2, net.core
        )

    def add_core(unit, slot):
        to_core(unit, slot + 1).wait_recv()
        here = units[unit](slot)
        here[...] = here[...] + FROM_CORE[unit, slot // 2]

    sums_core = [
        remote(SUMS.at[2 * n + 1], SUMS_CORE.at[n], total_sems, n, net.core) for n in range(2)
    ]
    sums_far = [
        remote(SUMS.at[2 - 2 * (n > 0)], SUMS_FAR.at[n], total_sems, 2 + n, partner)
        for n, partner in enumerate([net.y] + net.dp)
    ]
    shared = slice(SHARED, SHARED + 6)

    def send_totals(k):
        if k == 0:
            for copy in sums_core:
                copy.start()
        else:
            sums_far[k - 1].start()

    def take_totals(k):
        if k == 0:
            for n, copy in enumerate(sums_core):
                copy.wait_recv()
                SUMS[2 * n] = SUMS[2 * n] + SUMS_CORE[n]
            SUMS[2, shared, :] = SUMS[0, shared, :]
        else:
            sums_far[k - 1].wait_recv()
            if k > 1:
                sums_far[k - 1].wait_send()
            SUMS[0] = SUMS[0] + SUMS_FAR[k - 1]

    results = (GRW, GEW, MIX)

    def take(unit, chunk, axis, slot):
        stages = flows[unit, chunk]
        stage = stages[axis, slot]
        if stage is not list(stages.values())[-1]:
            stage.take()
            return
        stage.all_of_it().wait_recv()
        (start, count), = stage.ours()
        lane, lanes, _ = CHUNKS[unit][chunk]
        mine = stage.values(0, start, count)[...].astype(F32)
        results[unit][:, lane : lane + lanes] = mine + stage.room(0, count)[...].astype(F32)

    def act(kind, *what):
        if kind == "gs":
            pieces[what[0]].hop(what[1]).start()
        elif kind == "gt":
            pieces[what[0]].hop(what[1] - 1, True).wait_recv()
        elif kind == "cs":
            to_core(*what).start()
        elif kind == "ct":
            add_core(*what)
        elif kind == "s":
            flows[what[0], what[1]][what[2], what[3]].send()
        elif kind == "t":
            take(*what)
        elif kind == "ms":
            send_totals(*what)
        else:
            take_totals(*what)

    def do(actions):
        for action in actions:
            act(*action)

    def at(phase, point, index=None, before=None):
        if index is None:
            do(PLAN.get((phase, 0, point), ()))
            return
        for r in range(4):
            first = (before or {}).get(r, ())
            actions = PLAN.get((phase, r, point), ())
            if first or actions:

                @pl.when(index == r)
                def _():
                    for wait in first:
                        wait()
                    do(actions)

    small_y.start()
    at("start", 0)
    small_core.start()
    for copy in give_own:
        copy.start()
    keep_own[2].start()
    keep_own[3].start()
    fetch_cot.start()

    begin, bounds = page_scalars(pages_ref, net.t, half)
    perm = (iota((rows, rows), 1) == ((iota((rows, rows), 0) + begin) & (rows - 1))).astype(BF)
    fetch_x.wait()
    XR[...] = nn(perm, NB[...]).astype(BF)
    bucket = iota((BUCKETS, rows), 0)
    mine = pl.ds(pl.multiple_of(net.t * rows, 128), rows)
    one = (cells_ref[0:1, mine] == bucket).astype(BF)
    two = (cells_ref[1:2, mine] == bucket).astype(BF)
    HOT[...] = nt(perm, jnp.concatenate([one, two, one, two], axis=0)).astype(BF)
    one = (cells_ref[0:1, mine] == BUCKETS - 1 - bucket).astype(BF)
    two = (cells_ref[1:2, mine] == BUCKETS - 1 - bucket).astype(BF)
    BACK[...] = nt(perm, jnp.concatenate([one, two], axis=0)).astype(BF)
    ACC[...] = XR[...].astype(F32) + ms_ref[...].reshape(1, width).astype(F32)
    for ref in (Q, K, V):
        for s in range(4):
            ref[s, :, local:] = jnp.zeros((rows, 256 - local), BF)
    GC[:, local:] = jnp.zeros((rows, 256 - local), BF)
    DD[:, :local] = jnp.zeros((rows, local), BF)
    col = page_numbers((iota((half, 1), 0) + (half + begin)) & (rows - 1), bounds)
    row = page_numbers((iota((1, half), 1) + (half + begin)) & (rows - 1), bounds)

    spot = iota((BUCKETS, 128), 1)
    spot = jnp.where(spot < 64, spot, spot - 128)
    fold = (iota((BUCKETS, 128), 0) == jnp.clip(BUCKETS // 2 - spot, 0, BUCKETS - 1)).astype(BF)

    fold_f32 = fold.astype(F32)

    keep_own[0].wait()
    keep_own[1].wait()

    def attend(r, _):
        at(
            "att", 0, r,
            {
                1: [small_core.wait_recv, give_own[0].wait_recv, give_own[1].wait_recv],
                2: [small_y.wait_recv, small_far.start],
                3: [small_far.wait_recv],
            },
        )
        line = nn(SM[r, 8 : 8 + 2 * heads, :BUCKETS].astype(BF), fold)
        lanes_at = iota((BUCKETS, 128), 1)
        tiles = []
        for a in range(2):
            parts = []
            for pair in range(2):
                total = jnp.zeros((BUCKETS, 128), F32)
                for which in range(min(2, heads - 2 * pair)):
                    off = which * HEAD_DIM + a * BUCKETS
                    h = (2 * pair + which) * 2 + a
                    spread = jnp.broadcast_to(line[h : h + 1, :], (BUCKETS, 128))
                    spread = pltpu.roll(spread, off, axis=1, stride=1, stride_axis=0)
                    inside = (lanes_at >= off) & (lanes_at < off + BUCKETS)
                    total = jnp.where(inside, spread, total)
                parts.append(total.astype(BF))
            tiles.append(jnp.concatenate(parts, axis=1))
        pairs = jnp.concatenate(tiles, axis=0)
        left = nn(HOT[:, : 2 * BUCKETS], pairs).astype(BF)

        queries = (nt(XR[...], AW[r, 0]) + SM[r, 0:1, :local]).astype(BF)
        Q[r, :, :local] = queries * jnp.asarray(HEAD_DIM ** -0.5, BF)
        K[r, :, :local] = nt(XR[...], AW[r, 1]).astype(BF)
        V[r, :, :local] = (nt(XR[...], AW[r, 2]) + SM[r, 1:2, :local]).astype(BF)
        at("att", 1, r)
        same = col == row
        for block in range(2):
            span = slice(block * half, (block + 1) * half)
            if block == 1:
                at("att", 2, r)
            for pair in range(2):
                lanes = slice(pair * 128, (pair + 1) * 128)
                key_side = jnp.concatenate([K[r, span, lanes], HOT[span, :]], axis=1)
                total = None
                for which in range(min(2, heads - 2 * pair)):
                    keep = half_lanes(which)
                    query_side = jnp.concatenate(
                        [Q[r, span, lanes] * keep, left[span, lanes] * keep], axis=1
                    )
                    scores = nt(key_side, query_side)
                    if block == 1:
                        scores = jnp.where(same, scores, MASKED)
                    weights = jnp.exp(scores - jnp.max(scores, axis=0, keepdims=True))
                    probs = (weights * (1.0 / jnp.sum(weights, axis=0, keepdims=True))).astype(BF)
                    PR[r, (2 * pair + which) * 2 + block] = probs
                    part = tn(probs, V[r, span, lanes]) * keep.astype(F32)
                    total = part if total is None else total + part
                CTX[r, span, lanes] = total.astype(BF)
        at("att", 3, r)
        ACC[...] += nn(CTX[r, :, :local], MW[r])
        return 0

    lax.fori_loop(0, 4, attend, 0)

    hat, scale = norm_stats(ACC[...])
    HAT[...] = hat
    SCALE[...] = scale
    normed = hat * gain_ref[0:1, :].astype(F32) + nshift_ref[0:1, :].astype(F32)
    NB[...] = normed.astype(BF)
    ACC[...] = normed + rs_ref[...].reshape(1, width).astype(F32)
    keep_own[2].wait()
    keep_own[3].wait()

    def feed(r, _):
        at("feed", 0, r, {1: [give_own[2].wait_recv, give_own[3].wait_recv]})
        pre = nn(NB[...], EW[r]) + SM[r, 2:3, :]
        gate = 0.5 * (1.0 + lax.erf(pre * (0.5 ** 0.5)))
        AS[r, :rows] = (pre * gate).astype(BF)
        AS[r, rows:] = (
            gate + pre * (jnp.exp(-0.5 * (pre * pre)) * (1.0 / math.sqrt(2.0 * math.pi)))
        ).astype(BF)
        at("feed", 1, r)
        ACC[...] += nn(AS[r, :rows], RW[r])
        return 0

    lax.fori_loop(0, 4, feed, 0)

    fetch_cot.wait()
    hat, scale = norm_stats(ACC[...])
    gain = gain_ref[1:2, :].astype(F32)
    result = (hat * gain + nshift_ref[1:2, :].astype(F32)).astype(BF)
    perm = (iota((rows, rows), 1) == ((iota((rows, rows), 0) + begin) & (rows - 1))).astype(BF)
    RESULT[...] = result
    cot = nn(perm, GB[...])
    grad = norm_back(cot, hat, scale, gain)
    ACC[...] = grad
    GB[...] = grad.astype(BF)
    shared_two = (
        jnp.sum(cot * hat, axis=0, keepdims=True),
        jnp.sum(cot, axis=0, keepdims=True),
        jnp.sum(grad, axis=0, keepdims=True),
    )
    for n, line in enumerate(shared_two):
        SUMS[0, SHARED + 3 + n : SHARED + 4 + n, :] = line

    for (name, *_), piece in zip(PIECES, pieces):
        if name in ("ew", "rw"):
            piece.sent()

    def reduce_back(i, _):
        r = 3 - i
        grad_pre = (nt(GB[...], RW[r]) * AS[r, rows:].astype(F32)).astype(BF)
        AS[r, rows:] = grad_pre
        SUMS[r, 0:1, :] = jnp.sum(grad_pre.astype(F32), axis=0, keepdims=True)
        at("fa", 0, r)
        RW[r] = tn(GB[...], AS[r, :rows]).astype(BF)
        at("fa", 1, r)
        return 0

    lax.fori_loop(0, 4, reduce_back, 0)

    def expand_back(i, _):
        r = 3 - i
        ACC[...] += nt(AS[r, rows:], EW[r])
        at("fb", 0, r)
        EW[r] = tn(NB[...], AS[r, rows:]).astype(BF)
        at("fb", 1, r)
        return 0

    lax.fori_loop(0, 4, expand_back, 0)

    grad = ACC[...]
    hat = HAT[...]
    gone = norm_back(grad, hat, SCALE[...], gain_ref[0:1, :].astype(F32))
    ACC[...] = gone
    GB[...] = gone.astype(BF)
    shared_one = (
        jnp.sum(grad * hat, axis=0, keepdims=True),
        jnp.sum(grad, axis=0, keepdims=True),
        jnp.sum(gone, axis=0, keepdims=True),
    )
    for n, line in enumerate(shared_one):
        SUMS[0, SHARED + n : SHARED + 1 + n, :] = line

    at("lnb", 0)

    def attend_back(i, _):
        r = 3 - i

        GC[:, :local] = nt(GB[...], MW[r]).astype(BF)
        at("ab", 0, r)
        for block in range(2):
            span = slice(block * half, (block + 1) * half)
            for pair in range(2):
                lanes = slice(pair * 128, (pair + 1) * 128)
                key_side = jnp.concatenate([K[r, span, lanes], HOT[span, :]], axis=1)
                sums = None
                for which in range(min(2, heads - 2 * pair)):
                    keep = half_lanes(which)
                    wide = keep.astype(F32)
                    probs = PR[r, (2 * pair + which) * 2 + block]
                    grad_probs = nt(V[r, span, lanes] * keep, GC[span, lanes])
                    soft = probs.astype(F32)
                    inner = jnp.sum(soft * grad_probs, axis=0, keepdims=True)
                    grad_scores = (soft * (grad_probs - inner)).astype(BF)
                    both = tn(grad_scores, key_side)
                    parts = (
                        both[:, :128] * wide,
                        both[:, 128:] * wide,
                        nn(grad_scores, Q[r, span, lanes]) * wide,
                        nn(probs, GC[span, lanes]) * wide,
                    )
                    sums = parts if sums is None else tuple(a + b for a, b in zip(sums, parts))
                DQ[span, lanes] = (sums[0] * (HEAD_DIM ** -0.5)).astype(BF)
                E[span, lanes] = sums[1].astype(BF)
                DK[span, lanes] = sums[2].astype(BF)
                DV[span, lanes] = sums[3].astype(BF)
            at("ab", 1 + block, r)
        for m, ref in enumerate((DQ, DK, DV)):
            DD[:, (m + 1) * local : (m + 2) * local] = ref[:, :local]
            ACC[...] += nn(ref[:, :local], AW[r, m])
        weight_grad = tn(XR[...], DD[...])
        AS[r, :width, 256:] = weight_grad[:, 256:].astype(BF)
        AS[r, :width, :256] = (weight_grad[:, :256] + tn(GB[...], CTX[r])).astype(BF)
        SUMS[r, 1:2, :local] = jnp.sum(DQ[:, :local].astype(F32), axis=0, keepdims=True)
        SUMS[r, 2:3, :local] = jnp.sum(DV[:, :local].astype(F32), axis=0, keepdims=True)
        grad_pairs = tn(BACK[...], E[...])
        lanes_at = iota((BUCKETS, 128), 1)
        for h in range(heads):
            for a in range(2):
                off = (h % 2) * HEAD_DIM + a * BUCKETS
                part = grad_pairs[a * BUCKETS : (a + 1) * BUCKETS, (h // 2) * 128 : (h // 2 + 1) * 128]
                part = jnp.where((lanes_at >= off) & (lanes_at < off + BUCKETS), part, 0.0)
                part = pltpu.roll(part, (129 - BUCKETS - off) % 128, axis=1, stride=1, stride_axis=0)
                SUMS[r, 3 + 2 * h + a : 4 + 2 * h + a, :128] = jnp.sum(part, axis=0, keepdims=True)
        at("ab", 3, r)
        return 0

    SUMS[1, shared, :] = SUMS[0, shared, :]
    lax.fori_loop(0, 4, attend_back, 0)

    at("fin", 0)
    perm = (iota((rows, rows), 1) == ((iota((rows, rows), 0) + begin) & (rows - 1))).astype(BF)
    GB[...] = tn(perm, ACC[...].astype(BF)).astype(BF)
    RESULT[...] = tn(perm, RESULT[...]).astype(BF)
    leave = [
        pltpu.make_async_copy(source, target, local_sems.at[6 + n])
        for n, (source, target) in enumerate(
            ((RESULT, out_hbm), (GB, gin_hbm), (GEW, gew_hbm), (GRW, grw_hbm))
        )
    ]
    leave[0].start()
    leave[1].start()
    at("end", 0)
    leave[2].start()
    leave[3].start()
    gmw_ref[...] = jnp.transpose(MIX[:, :256])[:local, :]
    for m in range(3):
        gaw_ref[m] = MIX[:, (m + 1) * local : (m + 2) * local]
    both_ref[...] = SUMS[0]
    for row in range(2 * heads):
        both_ref[3 + row : 4 + row, :BUCKETS] = lax.dot_general(
            both_ref[3 + row : 4 + row, :128], fold_f32, (((1,), (1,)), ((), ())),
            precision=lax.Precision.HIGHEST, preferred_element_type=F32,
        )

    for stages in flows.values():
        for stage in stages.values():
            stage.sent()
    for unit in range(3):
        for slot in (1, 3):
            to_core(unit, slot).wait_send()
    for copy in sums_core + sums_far[:1]:
        copy.wait_send()
    for (name, *_), piece in zip(PIECES, pieces):
        if name not in ("ew", "rw"):
            piece.sent()
    for copy in give_own + [small_core, small_y, small_far]:
        copy.wait_send()
    for copy in leave:
        copy.wait()


def swap(value, axis, size, bit):
    return lax.ppermute(value, axis, [(i, i ^ bit) for i in range(size)])


def finish_rows(value, dp, bits_done):
    me = lax.axis_index("dp")
    left = dp.bit_length() - 1 - bits_done
    rows, cols = value.shape
    value = value.reshape((2,) * left + (rows >> left, cols))
    for bit in range(left):
        axis = value.ndim - 3
        mine = (me >> bit) & 1
        keep = lax.dynamic_index_in_dim(value, mine, axis, keepdims=False)
        send = lax.dynamic_index_in_dim(value, 1 - mine, axis, keepdims=False)
        value = keep + swap(send, "dp", dp, 1 << bit)
    return value


def finish_kernel(*refs):
    sources, both, targets, small = refs[:6], refs[6], refs[7:13], refs[13:20]
    for source, target in zip(sources, targets):
        target[...] = source[...]
    shifts, merge, gains, norm_shift, expand, reduced, tables = small
    shifts[...] = both[1:3, : shifts.shape[1]]
    for target, row in ((merge, SHARED + 2), (expand, 0), (reduced, SHARED + 5)):
        target[...] = both[row : row + 1, :].reshape(target.shape)
    for target, row in ((gains, SHARED), (norm_shift, SHARED + 1)):
        target[0:1, :] = both[row : row + 1, :]
        target[1:2, :] = both[row + 3 : row + 4, :]
    for h in range(tables.shape[0]):
        tables[h] = both[3 + 2 * h : 5 + 2 * h, :BUCKETS]


def on_device(
    dp,
    inputs,
    layout_cells,
    page_lengths,
    attend_weight,
    attend_shift,
    merge_weight,
    merge_shift,
    norm_gains,
    norm_shifts,
    expand_weight,
    expand_shift,
    reduce_weight,
    reduce_shift,
    bias_tables,
    cotangent,
):
    rows, width = inputs.shape
    half = rows // 2
    local = attend_weight.shape[2]
    heads = bias_tables.shape[1]
    hidden = expand_weight.shape[1]
    top = dp.bit_length() - 1
    bits = (top - 3, top - 2, top - 1)

    sds = jax.ShapeDtypeStruct
    smem = pl.BlockSpec(memory_space=pltpu.SMEM)
    vmem = pl.BlockSpec(memory_space=pltpu.VMEM)
    hbm = pl.BlockSpec(memory_space=pl.ANY)

    def kernel(*refs):
        return layer_kernel(bits, *refs)

    dma = pltpu.SemaphoreType.DMA
    count = sum(len(order) + order.index("y") for chunks in CHUNKS for _, _, order in chunks)
    block = width // 8
    gaw, gmw, both, output, input_grad, gew, grw = pl.pallas_call(
        kernel,
        in_specs=[smem] + [vmem] * 8 + [hbm] * 6,
        out_specs=[vmem] * 3 + [hbm] * 4,
        out_shape=[
            sds((3, block, local), F32), sds((local, block), F32), sds((SMALL_ROWS, width), F32),
            sds((rows, width), BF), sds((rows, width), BF), sds((block, hidden), F32),
            sds((block, hidden), F32),
        ],
        scratch_shapes=[
            pltpu.VMEM((4, 3, local, width), BF),
            pltpu.VMEM((4, local, width), BF),
            pltpu.VMEM((4, width, hidden), BF),
            pltpu.VMEM((4, hidden, width), BF),
            pltpu.VMEM((rows, width), BF),
            pltpu.VMEM((rows, 128), BF),
            pltpu.VMEM((rows, 2 * BUCKETS), BF),
            pltpu.VMEM((4, rows, 256), BF),
            pltpu.VMEM((4, rows, 256), BF),
            pltpu.VMEM((4, rows, 256), BF),
            pltpu.VMEM((4, 2 * heads, half, half), BF),
            pltpu.VMEM((4, rows, 256), BF),
            pltpu.VMEM((rows, width), BF),
            pltpu.VMEM((rows, width), F32),
            pltpu.VMEM((rows, 1), F32),
            pltpu.VMEM((4, 2 * rows, hidden), BF),
            pltpu.VMEM((rows, width), F32),
            pltpu.VMEM((rows, width), BF),
            pltpu.VMEM((rows, 256), BF),
            pltpu.VMEM((rows, 256), BF),
            pltpu.VMEM((rows, 256), BF),
            pltpu.VMEM((rows, 256), BF),
            pltpu.VMEM((rows, 256), BF),
            pltpu.VMEM((rows, 4 * local), BF),
            pltpu.VMEM((4, SMALL_ROWS, hidden), F32),
            pltpu.VMEM((3, 2, width, hidden), BF),
            pltpu.VMEM((3, 15 * block, hidden), BF),
            pltpu.VMEM((block, hidden), F32),
            pltpu.VMEM((block, hidden), F32),
            pltpu.VMEM((block, width), F32),
            pltpu.VMEM((rows, width), BF),
            pltpu.VMEM((4, SMALL_ROWS, width), F32),
            pltpu.VMEM((2, SMALL_ROWS, width), F32),
            pltpu.VMEM((4, SMALL_ROWS, width), F32),
            dma((2, 4 * len(PIECES))), dma((2, 4)), dma((2, 3)), dma((10,)),
            dma((2, 6)), dma((2, count)), dma((2, 6)),
        ],
        compiler_params=pltpu.CompilerParams(
            collective_id=0, has_side_effects=True, vmem_limit_bytes=VMEM_LIMIT
        ),
    )(
        page_lengths, layout_cells, attend_shift, expand_shift,
        jnp.transpose(bias_tables, (1, 0, 2)), merge_shift, reduce_shift, norm_gains, norm_shifts,
        jnp.transpose(attend_weight, (0, 2, 1)), merge_weight, expand_weight, reduce_weight, cotangent,
        inputs,
    )

    if top > 3:
        grw = finish_rows(grw, dp, 3)
        gew = finish_rows(gew, dp, 3)
        gmw = finish_rows(gmw.T, dp, 3).T
        gaw = jnp.stack([finish_rows(gaw[m], dp, 3) for m in range(3)])
        for bit in range(top - 3):
            both = both + swap(both, "dp", dp, 1 << bit)
    big = (output, input_grad, gaw, gmw, gew, grw)
    done = pl.pallas_call(
        finish_kernel,
        in_specs=[vmem] * 7,
        out_specs=[vmem] * 13,
        out_shape=[sds(a.shape, a.dtype) for a in big]
        + [
            sds((2, local), F32), sds((width,), F32), sds((2, width), F32), sds((2, width), F32),
            sds((hidden,), F32), sds((width,), F32), sds((heads, 2, BUCKETS), F32),
        ],
    )(*big, both)
    output, input_grad, gaw, gmw, gew, grw, shifts, merge, gains, norm_shift, expand, reduced, tables = done
    return (
        output, input_grad, gaw, shifts, gmw, merge, gains, norm_shift, gew, expand, grw.T, reduced,
        jnp.transpose(tables, (1, 0, 2)),
    )


def solution(mesh):
    in_specs = (
        P(("dp", "tensor"), None),
        P(None, "dp"),
        P("dp", None),
        P(None, None, "tensor"),
        P(None, "tensor"),
        P("tensor", None),
        P(),
        P(),
        P(),
        P(None, "tensor"),
        P("tensor"),
        P("tensor", None),
        P(),
        P(None, "tensor", None),
        P(("dp", "tensor"), None),
    )
    out_specs = (
        P(("dp", "tensor"), None),
        P(("dp", "tensor"), None),
        P(None, "dp", "tensor"),
        P(None, "tensor"),
        P("tensor", "dp"),
        P(),
        P(),
        P(),
        P("dp", "tensor"),
        P("tensor"),
        P("tensor", "dp"),
        P(),
        P(None, "tensor", None),
    )

    def run(*arrays):
        return on_device(mesh.shape["dp"], *arrays)

    return jax.shard_map(
        run, mesh=mesh, in_specs=in_specs, out_specs=out_specs, check_vma=False
    )
```

```python
import math

import jax
import jax.numpy as jnp
from jax import lax
from jax.experimental import pallas as pl
from jax.experimental.pallas import tpu as pltpu
from jax.sharding import PartitionSpec as P

HEAD_DIM = 64
BUCKETS = 32
EPSILON = 1e-05
MASKED = -1000000000.0
BF = jnp.bfloat16
F32 = jnp.float32
VMEM_LIMIT = 60 * 1024 * 1024
PIECES = (
    ("ew", 0, 192, (1, 0)),
    ("ew", 192, 192, (1, 0)),
    ("rw", 0, 192, (1, 0)),
    ("aw0", 0, 192, (0, 1)),
    ("rw", 192, 192, ()),
    ("aw1", 0, 192, (1, 0)),
    ("ew", 384, 192, ()),
    ("aw2", 0, 192, (0, 1)),
    ("mw", 0, 192, (0,)),
    ("rw", 384, 192, (1, 0)),
    ("ew", 576, 192, (1,)),
    ("rw", 576, 192, (0, 1)),
)
CHUNKS = (
    (
        (0, 256, ("y", 0, 1, 2)),
        (256, 256, (0, "y", 1, 2)),
        (512, 128, (1, "y", 0, 2)),
        (640, 128, (1, 0, 2, "y")),
    ),
    (
        (0, 128, ("y", 2, 0, 1)),
        (128, 256, (0, "y", 1, 2)),
        (384, 384, (1, 0, "y", 2)),
    ),
    (
        (0, 256, ("y", 0, 1, 2)),
        (256, 256, (0, "y", 1, 2)),
        (512, 256, (1, 0, "y", 2)),
    ),
)
PLAN = {
    ("start", 0, 0): (
        ("gs", 0, 0),
        ("gs", 3, 0),
        ("gs", 5, 0),
    ),
    ("att", 0, 2): (
        ("gs", 7, 0),
    ),
    ("att", 1, 0): (
        ("gs", 8, 0),
        ("gs", 9, 0),
        ("gs", 11, 0),
        ("gt", 0, 1),
        ("gs", 0, 1),
        ("gt", 3, 1),
        ("gs", 3, 1),
    ),
    ("att", 1, 2): (
        ("gs", 1, 0),
        ("gs", 2, 0),
        ("gs", 10, 0),
    ),
    ("att", 1, 3): (
        ("gt", 5, 1),
        ("gs", 5, 1),
    ),
    ("att", 2, 0): (
        ("gs", 4, 0),
        ("gs", 6, 0),
        ("gt", 7, 1),
        ("gs", 7, 1),
        ("gt", 0, 2),
        ("gs", 0, 2),
        ("gt", 3, 2),
        ("gs", 3, 2),
        ("gt", 9, 1),
        ("gs", 9, 1),
        ("gt", 5, 2),
        ("gs", 5, 2),
        ("gt", 8, 1),
        ("gs", 8, 1),
        ("gt", 11, 1),
        ("gs", 11, 1),
        ("gt", 7, 2),
        ("gs", 7, 2),
        ("gt", 1, 1),
        ("gs", 1, 1),
        ("gt", 9, 2),
        ("gs", 9, 2),
        ("gt", 2, 1),
        ("gs", 2, 1),
        ("gt", 3, 3),
        ("gs", 3, 3),
        ("gt", 0, 3),
        ("gs", 0, 3),
        ("gt", 3, 4),
        ("gt", 0, 4),
        ("gt", 7, 3),
        ("gs", 7, 3),
        ("gt", 5, 3),
    ),
    ("att", 2, 1): (
        ("gs", 5, 3),
        ("gt", 7, 4),
    ),
    ("att", 2, 3): (
        ("gt", 1, 2),
        ("gs", 1, 2),
        ("gt", 2, 2),
        ("gs", 2, 2),
        ("gt", 5, 4),
        ("gt", 8, 2),
        ("gs", 8, 2),
        ("gt", 10, 1),
        ("gs", 10, 1),
    ),
    ("att", 3, 1): (
        ("gt", 8, 3),
        ("gt", 11, 2),
        ("gs", 11, 2),
    ),
    ("feed", 0, 0): (
        ("gt", 4, 1),
        ("gs", 4, 1),
        ("gt", 9, 3),
        ("gs", 9, 3),
    ),
    ("feed", 1, 0): (
        ("gt", 4, 2),
        ("gt", 9, 4),
        ("gt", 10, 2),
        ("gs", 10, 2),
    ),
    ("feed", 1, 1): (
        ("gt", 1, 3),
        ("gs", 1, 3),
        ("gt", 2, 3),
        ("gs", 2, 3),
        ("gt", 6, 1),
        ("gs", 6, 1),
        ("gt", 10, 3),
        ("gt", 11, 3),
        ("gs", 11, 3),
    ),
    ("feed", 3, 0): (
        ("gt", 1, 4),
        ("gt", 2, 4),
        ("gt", 6, 2),
        ("gt", 11, 4),
    ),
    ("fa", 3, 1): (
        ("cs", 0, 3),
    ),
    ("fa", 1, 0): (
        ("ct", 0, 2),
        ("s", 0, 0, "y", 2),
        ("s", 0, 3, 1, 2),
        ("s", 0, 1, 0, 2),
        ("s", 0, 2, 1, 2),
    ),
    ("fa", 1, 1): (
        ("cs", 0, 1),
    ),
    ("fb", 3, 0): (
        ("ct", 0, 0),
        ("s", 0, 3, 1, 0),
        ("s", 0, 1, 0, 0),
        ("s", 0, 2, 1, 0),
    ),
    ("fb", 3, 1): (
        ("cs", 1, 3),
    ),
    ("fb", 1, 0): (
        ("ct", 1, 2),
        ("s", 1, 0, "y", 2),
        ("s", 1, 1, 0, 2),
        ("s", 1, 2, 1, 2),
        ("t", 0, 3, 1, 2),
        ("s", 0, 3, 0, 2),
        ("t", 0, 1, 0, 2),
        ("s", 0, 1, "y", 2),
        ("t", 0, 2, 1, 2),
        ("s", 0, 2, "y", 2),
    ),
    ("fb", 1, 1): (
        ("cs", 1, 1),
    ),
    ("fb", 0, 1): (
        ("t", 0, 0, "y", 2),
        ("s", 0, 0, 0, 0),
        ("t", 0, 3, 1, 0),
        ("s", 0, 3, 0, 0),
        ("ct", 1, 0),
        ("s", 1, 1, 0, 0),
        ("s", 1, 2, 1, 0),
        ("t", 0, 1, 0, 0),
        ("t", 0, 2, 1, 0),
    ),
    ("lnb", 0, 0): (
        ("t", 0, 3, 0, 2),
        ("s", 0, 3, 2, 2),
    ),
    ("ab", 3, 3): (
        ("cs", 2, 3),
        ("t", 1, 1, 0, 2),
        ("s", 1, 1, "y", 2),
    ),
    ("ab", 2, 1): (
        ("t", 0, 3, 0, 0),
        ("s", 0, 3, 2, 0),
        ("t", 0, 1, "y", 2),
        ("s", 0, 1, 1, 0),
        ("t", 1, 0, "y", 2),
        ("s", 1, 0, 2, 0),
        ("t", 0, 3, 2, 2),
        ("s", 0, 3, "y", 2),
        ("t", 1, 2, 1, 2),
        ("s", 1, 2, 0, 2),
    ),
    ("ab", 2, 2): (
        ("t", 0, 2, "y", 2),
        ("s", 0, 2, 0, 0),
    ),
    ("ab", 2, 3): (
        ("ct", 2, 2),
        ("s", 2, 1, 0, 2),
        ("s", 2, 0, "y", 2),
        ("s", 2, 2, 1, 2),
        ("t", 0, 0, 0, 0),
        ("s", 0, 0, 1, 0),
    ),
    ("ab", 1, 1): (
        ("t", 0, 3, 2, 0),
        ("t", 0, 3, "y", 2),
        ("t", 1, 2, 1, 0),
        ("s", 1, 2, 0, 0),
    ),
    ("ab", 1, 2): (
        ("t", 1, 1, 0, 0),
        ("t", 1, 1, "y", 2),
        ("s", 1, 1, 1, 0),
    ),
    ("ab", 1, 3): (
        ("cs", 2, 1),
        ("t", 0, 1, 1, 0),
        ("s", 0, 1, 2, 0),
    ),
    ("ab", 0, 0): (
        ("t", 0, 2, 0, 0),
        ("s", 0, 2, 2, 0),
        ("t", 1, 0, 2, 0),
        ("s", 1, 0, 0, 0),
    ),
    ("ab", 0, 1): (
        ("t", 1, 2, 0, 2),
        ("s", 1, 2, "y", 2),
    ),
    ("ab", 0, 3): (
        ("ms", 0),
        ("ct", 2, 0),
        ("s", 2, 1, 0, 0),
        ("s", 2, 2, 1, 0),
        ("t", 0, 0, 1, 0),
        ("s", 0, 0, 2, 0),
    ),
    ("end", 0, 0): (
        ("mt", 0),
        ("ms", 1),
        ("t", 2, 0, "y", 2),
        ("s", 2, 0, 0, 0),
        ("t", 1, 2, 0, 0),
        ("t", 2, 2, 1, 2),
        ("s", 2, 2, 0, 2),
        ("t", 2, 1, 0, 2),
        ("s", 2, 1, "y", 2),
        ("t", 1, 1, 1, 0),
        ("s", 1, 1, 2, 0),
        ("t", 1, 2, "y", 2),
        ("s", 1, 2, 2, 0),
        ("t", 1, 0, 0, 0),
        ("s", 1, 0, 1, 0),
        ("t", 0, 2, 2, 0),
        ("t", 0, 1, 2, 0),
        ("mt", 1),
        ("ms", 2),
        ("t", 0, 0, 2, 0),
        ("t", 1, 1, 2, 0),
        ("t", 2, 1, 0, 0),
        ("t", 2, 1, "y", 2),
        ("s", 2, 1, 1, 0),
        ("t", 2, 2, 1, 0),
        ("s", 2, 2, 0, 0),
        ("t", 2, 0, 0, 0),
        ("s", 2, 0, 1, 0),
        ("t", 1, 2, 2, 0),
        ("t", 1, 0, 1, 0),
        ("t", 2, 2, 0, 2),
        ("s", 2, 2, "y", 2),
        ("mt", 2),
        ("ms", 3),
        ("t", 2, 1, 1, 0),
        ("s", 2, 1, 2, 0),
        ("t", 2, 2, 0, 0),
        ("t", 2, 0, 1, 0),
        ("s", 2, 0, 2, 0),
        ("t", 2, 2, "y", 2),
        ("s", 2, 2, 2, 0),
        ("mt", 3),
        ("ms", 4),
        ("t", 2, 1, 2, 0),
        ("t", 2, 0, 2, 0),
        ("t", 2, 2, 2, 0),
        ("mt", 4),
    ),
}


def mm(a, b, da, db):
    return lax.dot_general(a, b, (((da,), (db,)), ((), ())), preferred_element_type=F32)


def nn(a, b):
    return mm(a, b, 1, 0)


def nt(a, b):
    return mm(a, b, 1, 1)


def tn(a, b):
    return mm(a, b, 0, 0)


def iota(shape, dim):
    return lax.broadcasted_iota(jnp.int32, shape, dim)


def page_scalars(pages_ref, line, half):
    total = jnp.int32(0)
    begin = jnp.int32(0)
    bounds = []
    for k in range(pages_ref.shape[1]):
        length = pages_ref[line, k]
        begin = begin + jnp.where(length == half, total, 0)
        total = total + length
        bounds.append(total)
    return begin, bounds


def page_numbers(places, bounds):
    number = jnp.zeros(places.shape, jnp.int32)
    for bound in bounds:
        number = number + (places >= bound).astype(jnp.int32)
    return number


def half_lanes(which):
    return ((iota((1, 128), 1) // HEAD_DIM) == which).astype(BF)


def norm_stats(signal):
    mean = jnp.mean(signal, axis=1, keepdims=True)
    center = signal - mean
    spread = jnp.mean(center * center, axis=1, keepdims=True)
    scale = lax.rsqrt(spread + EPSILON)
    return center * scale, scale


def norm_back(grad, hat, scale, gain):
    scaled = grad * gain
    return scale * (
        scaled
        - jnp.mean(scaled, axis=1, keepdims=True)
        - hat * jnp.mean(scaled * hat, axis=1, keepdims=True)
    )


MESH = pl.DeviceIdType.MESH
SMALL_ROWS = 16


class Net:
    def __init__(self, bits):
        t = lax.axis_index("tensor")
        d = lax.axis_index("dp")
        self.t = t
        self.core = {"tensor": t + 1 - 2 * (t % 2)}
        self.y = {"tensor": (t + 2) % 4}
        self.bit = [(d // 2 ** b) % 2 for b in bits]
        self.dp = [{"dp": d + 2 ** b * (1 - 2 * k)} for b, k in zip(bits, self.bit)]


def remote(source, target, sems, index, partner):
    return pltpu.make_async_remote_copy(
        src_ref=source,
        dst_ref=target,
        send_sem=sems.at[0, index],
        recv_sem=sems.at[1, index],
        device_id=partner,
        device_id_type=MESH,
    )


def rows_at(ref, start, count):
    return ref.at[pl.ds(pl.multiple_of(start, 16), count), :]


class Piece:
    def __init__(self, net, own, slots, start, count, axes, sems, first):
        self.net, self.own, self.slots, self.start, self.count = net, own, slots, start, count
        self.axes, self.sems, self.first = axes, sems, first

    def region(self, hop, flip):
        index, weight = 0, 1
        for axis in self.axes[hop - 1 :]:
            bit = self.net.bit[axis]
            index = index + weight * ((1 - bit) if flip and weight == 1 else bit)
            weight *= 2
        rows = self.count // weight
        return self.start + index * rows, rows

    def hop(self, number, arriving=False):
        if number == len(self.axes) + 1:
            here = rows_at(self.slots(2), self.start, self.count)
            there, partner = rows_at(self.slots(3), self.start, self.count), self.net.core
        elif number == 0:
            start, rows = self.region(1, False)
            here, partner = rows_at(self.own, start, rows), self.net.y
            there = rows_at(self.slots(2), start, rows)
        else:
            here = there = rows_at(self.slots(2), *self.region(number, arriving))
            partner = self.net.dp[self.axes[number - 1]]
        return remote(here, there, self.sems, self.first + number, partner)

    def sent(self):
        for number in range(len(self.axes) + 2):
            self.hop(number).wait_send()


SHARED = 9
class Stage:
    def __init__(self, net, axis, slot, fixed, values, room, index, sems, block):
        self.net, self.axis, self.slot, self.fixed, self.values = net, axis, slot, dict(fixed), values
        self.room, self.index, self.sems, self.block = room, index, sems, block
        self.kept = slot if axis != "y" else 0
        self.partner = net.y if axis == "y" else net.dp[axis]

    def runs(self, bits):
        low = 0
        while low < 3 and low not in bits:
            low += 1
        starts = [0]
        for k in range(low, 3):
            choice = [bits[k]] if k in bits else [0, 1]
            starts = [start + value * (2 ** k * self.block) for start in starts for value in choice]
        return [(start, 2 ** low * self.block) for start in starts]

    def theirs(self):
        bits = dict(self.fixed)
        if self.axis != "y":
            bits[self.axis] = 1 - self.net.bit[self.axis]
        return self.runs(bits)

    def ours(self):
        bits = dict(self.fixed)
        if self.axis != "y":
            bits[self.axis] = self.net.bit[self.axis]
        return self.runs(bits)

    def send(self):
        at = 0
        for start, count in self.theirs():
            remote(
                self.values(self.slot, start, count), self.room(at, count),
                self.sems, self.index, self.partner,
            ).start()
            at += count

    def all_of_it(self):
        total = sum(count for _, count in self.ours())
        return remote(self.room(0, total), self.room(0, total), self.sems, self.index, self.partner)

    def take(self):
        self.all_of_it().wait_recv()
        at = 0
        for start, count in self.ours():
            here = self.values(self.kept, start, count)
            here[...] = here[...] + self.room(at, count)[...]
            at += count

    def sent(self):
        self.all_of_it().wait_send()


def chunk_stages(net, order, lanes, slots, got, sems, first, block):
    def values(slot, start, count):
        return slots(slot).at[pl.ds(pl.multiple_of(start, 32), count), lanes]

    stages, fixed, live, at = {}, {}, (2, 0), 0
    for axis in order:
        exchanges = (2,) if axis == "y" else live
        for slot in exchanges:
            count = (8 * block) >> (len(fixed) + (axis != "y"))
            room = lambda start, rows, at=at: got.at[pl.ds(at + start, rows), lanes]
            stages[(axis, slot)] = Stage(
                net, axis, slot, fixed, values, room, first + len(stages), sems, block
            )
            at += count
        if axis == "y":
            live = (0,)
        else:
            fixed[axis] = net.bit[axis]
    return stages


def layer_kernel(
    bits,
    pages_ref, cells_ref, shift_ref, es_ref, tables_ref, ms_ref, rs_ref, gain_ref, nshift_ref,
    aw_hbm, mw_hbm, ew_hbm, rw_hbm, cot_hbm, x_hbm,
    gaw_ref, gmw_ref, both_ref, out_hbm, gin_hbm, gew_hbm, grw_hbm,
    AW, MW, EW, RW, XR, HOT, BACK, Q, K, V, PR, CTX, NB, HAT, SCALE, AS, ACC, GB, GC, DQ, DK, DV, E, DD, SM,
    FROM_CORE, FROM, GRW, GEW, MIX, RESULT, SUMS, SUMS_CORE, SUMS_FAR,
    in_sems, own_sems, small_sems, local_sems,
    unit_sems, stage_sems, total_sems,
):
    net = Net(bits)
    rows, width = x_hbm.shape
    half = rows // 2
    local = aw_hbm.shape[1]
    heads = local // HEAD_DIM
    hidden = ew_hbm.shape[1]

    fetch_x = pltpu.make_async_copy(x_hbm, NB, local_sems.at[5])
    fetch_x.start()

    barrier = pltpu.get_barrier_semaphore()
    greeted = (net.core, net.y, net.dp[0], net.dp[1], net.dp[2])
    for partner in greeted:
        pl.semaphore_signal(barrier, inc=1, device_id=partner, device_id_type=MESH)

    SM[0, 0:2, :local] = shift_ref[...].astype(F32)
    SM[0, 2:3, :] = es_ref[...].reshape(1, hidden).astype(F32)
    for h in range(heads):
        SM[0, 8 + 2 * h : 10 + 2 * h, :BUCKETS] = tables_ref[h].astype(F32)

    whole_of = {
        "aw0": (aw_hbm.at[0], lambda s: AW.at[s, 0]),
        "aw1": (aw_hbm.at[1], lambda s: AW.at[s, 1]),
        "aw2": (aw_hbm.at[2], lambda s: AW.at[s, 2]),
        "mw": (mw_hbm, lambda s: MW.at[s]),
        "ew": (ew_hbm, lambda s: EW.at[s]),
        "rw": (rw_hbm, lambda s: RW.at[s]),
    }
    pieces = [
        Piece(net, *whole_of[name], start, count, axes, in_sems, 4 * n)
        for n, (name, start, count, axes) in enumerate(PIECES)
    ]
    weights = ((aw_hbm, AW), (mw_hbm, MW), (ew_hbm, EW), (rw_hbm, RW))
    keep_own = [
        pltpu.make_async_copy(own, ref.at[0], local_sems.at[n]) for n, (own, ref) in enumerate(weights)
    ]
    give_own = [remote(own, ref.at[1], own_sems, n, net.core) for n, (own, ref) in enumerate(weights)]
    small_core = remote(SM.at[0], SM.at[1], small_sems, 0, net.core)
    small_y = remote(SM.at[0], SM.at[2], small_sems, 1, net.y)
    small_far = remote(SM.at[2], SM.at[3], small_sems, 2, net.core)
    fetch_cot = pltpu.make_async_copy(cot_hbm, GB, local_sems.at[4])

    keep_own[0].start()
    keep_own[1].start()
    pl.semaphore_wait(barrier, len(greeted))
    block = width // 8
    units = (
        (lambda slot: RW.at[slot]),
        (lambda slot: EW.at[slot]),
        (lambda slot: AS.at[slot, pl.ds(0, width), :]),
    )
    flows, first = {}, 0
    for unit, chunks in enumerate(CHUNKS):
        for chunk, (lane, lanes, order) in enumerate(chunks):
            stages = chunk_stages(
                net, order, pl.ds(lane, lanes), units[unit], FROM.at[unit], stage_sems, first, block
            )
            flows[unit, chunk] = stages
            first += len(stages)

    def to_core(unit, slot):
        return remote(
            units[unit](slot), FROM_CORE.at[unit, slot // 2], unit_sems, unit * 2 + slot // 2, net.core
        )

    def add_core(unit, slot):
        to_core(unit, slot + 1).wait_recv()
        here = units[unit](slot)
        here[...] = here[...] + FROM_CORE[unit, slot // 2]

    sums_core = [
        remote(SUMS.at[2 * n + 1], SUMS_CORE.at[n], total_sems, n, net.core) for n in range(2)
    ]
    sums_far = [
        remote(SUMS.at[2 - 2 * (n > 0)], SUMS_FAR.at[n], total_sems, 2 + n, partner)
        for n, partner in enumerate([net.y] + net.dp)
    ]
    shared = slice(SHARED, SHARED + 6)

    def send_totals(k):
        if k == 0:
            for copy in sums_core:
                copy.start()
        else:
            sums_far[k - 1].start()

    def take_totals(k):
        if k == 0:
            for n, copy in enumerate(sums_core):
                copy.wait_recv()
                SUMS[2 * n] = SUMS[2 * n] + SUMS_CORE[n]
            SUMS[2, shared, :] = SUMS[0, shared, :]
        else:
            sums_far[k - 1].wait_recv()
            if k > 1:
                sums_far[k - 1].wait_send()
            SUMS[0] = SUMS[0] + SUMS_FAR[k - 1]

    results = (GRW, GEW, MIX)

    def take(unit, chunk, axis, slot):
        stages = flows[unit, chunk]
        stage = stages[axis, slot]
        if stage is not list(stages.values())[-1]:
            stage.take()
            return
        stage.all_of_it().wait_recv()
        (start, count), = stage.ours()
        lane, lanes, _ = CHUNKS[unit][chunk]
        mine = stage.values(0, start, count)[...].astype(F32)
        results[unit][:, lane : lane + lanes] = mine + stage.room(0, count)[...].astype(F32)

    def act(kind, *what):
        if kind == "gs":
            pieces[what[0]].hop(what[1]).start()
        elif kind == "gt":
            pieces[what[0]].hop(what[1] - 1, True).wait_recv()
        elif kind == "cs":
            to_core(*what).start()
        elif kind == "ct":
            add_core(*what)
        elif kind == "s":
            flows[what[0], what[1]][what[2], what[3]].send()
        elif kind == "t":
            take(*what)
        elif kind == "ms":
            send_totals(*what)
        else:
            take_totals(*what)

    def do(actions):
        for action in actions:
            act(*action)

    def at(phase, point, index=None, before=None):
        if index is None:
            do(PLAN.get((phase, 0, point), ()))
            return
        for r in range(4):
            first = (before or {}).get(r, ())
            actions = PLAN.get((phase, r, point), ())
            if first or actions:

                @pl.when(index == r)
                def _():
                    for wait in first:
                        wait()
                    do(actions)

    small_y.start()
    at("start", 0)
    small_core.start()
    give_own[0].start()
    give_own[1].start()
    not_urgent = give_own[2:] + keep_own[2:] + [fetch_cot]

    begin, bounds = page_scalars(pages_ref, net.t, half)
    perm = (iota((rows, rows), 1) == ((iota((rows, rows), 0) + begin) & (rows - 1))).astype(BF)
    fetch_x.wait()
    XR[...] = nn(perm, NB[...]).astype(BF)
    bucket = iota((BUCKETS, rows), 0)
    mine = pl.ds(pl.multiple_of(net.t * rows, 128), rows)
    one = (cells_ref[0:1, mine] == bucket).astype(BF)
    two = (cells_ref[1:2, mine] == bucket).astype(BF)
    HOT[...] = nt(perm, jnp.concatenate([one, two, one, two], axis=0)).astype(BF)
    one = (cells_ref[0:1, mine] == BUCKETS - 1 - bucket).astype(BF)
    two = (cells_ref[1:2, mine] == BUCKETS - 1 - bucket).astype(BF)
    BACK[...] = nt(perm, jnp.concatenate([one, two], axis=0)).astype(BF)
    ACC[...] = XR[...].astype(F32) + ms_ref[...].reshape(1, width).astype(F32)
    for ref in (Q, K, V):
        for s in range(4):
            ref[s, :, local:] = jnp.zeros((rows, 256 - local), BF)
    GC[:, local:] = jnp.zeros((rows, 256 - local), BF)
    DD[:, :local] = jnp.zeros((rows, local), BF)
    col = page_numbers((iota((half, 1), 0) + (half + begin)) & (rows - 1), bounds)
    row = page_numbers((iota((1, half), 1) + (half + begin)) & (rows - 1), bounds)

    spot = iota((BUCKETS, 128), 1)
    spot = jnp.where(spot < 64, spot, spot - 128)
    fold = (iota((BUCKETS, 128), 0) == jnp.clip(BUCKETS // 2 - spot, 0, BUCKETS - 1)).astype(BF)

    fold_f32 = fold.astype(F32)

    keep_own[0].wait()
    keep_own[1].wait()

    def attend(r, _):
        at(
            "att", 0, r,
            {
                1: [small_core.wait_recv, give_own[0].wait_recv, give_own[1].wait_recv],
                2: [small_y.wait_recv, small_far.start],
                3: [small_far.wait_recv],
            },
        )
        line = nn(SM[r, 8 : 8 + 2 * heads, :BUCKETS].astype(BF), fold)
        lanes_at = iota((BUCKETS, 128), 1)
        tiles = []
        for a in range(2):
            parts = []
            for pair in range(2):
                total = jnp.zeros((BUCKETS, 128), F32)
                for which in range(min(2, heads - 2 * pair)):
                    off = which * HEAD_DIM + a * BUCKETS
                    h = (2 * pair + which) * 2 + a
                    spread = jnp.broadcast_to(line[h : h + 1, :], (BUCKETS, 128))
                    spread = pltpu.roll(spread, off, axis=1, stride=1, stride_axis=0)
                    inside = (lanes_at >= off) & (lanes_at < off + BUCKETS)
                    total = jnp.where(inside, spread, total)
                parts.append(total.astype(BF))
            tiles.append(jnp.concatenate(parts, axis=1))
        pairs = jnp.concatenate(tiles, axis=0)
        left = nn(HOT[:, : 2 * BUCKETS], pairs).astype(BF)

        queries = (nt(XR[...], AW[r, 0]) + SM[r, 0:1, :local]).astype(BF)
        Q[r, :, :local] = queries * jnp.asarray(HEAD_DIM ** -0.5, BF)
        K[r, :, :local] = nt(XR[...], AW[r, 1]).astype(BF)
        V[r, :, :local] = (nt(XR[...], AW[r, 2]) + SM[r, 1:2, :local]).astype(BF)
        at("att", 1, r)
        same = col == row
        for block in range(2):
            span = slice(block * half, (block + 1) * half)
            if block == 1:
                at("att", 2, r)
            for pair in range(2):
                lanes = slice(pair * 128, (pair + 1) * 128)
                key_side = jnp.concatenate([K[r, span, lanes], HOT[span, :]], axis=1)
                total = None
                for which in range(min(2, heads - 2 * pair)):
                    keep = half_lanes(which)
                    query_side = jnp.concatenate(
                        [Q[r, span, lanes] * keep, left[span, lanes] * keep], axis=1
                    )
                    scores = nt(key_side, query_side)
                    if block == 1:
                        scores = jnp.where(same, scores, MASKED)
                    weights = jnp.exp(scores - jnp.max(scores, axis=0, keepdims=True))
                    probs = (weights * (1.0 / jnp.sum(weights, axis=0, keepdims=True))).astype(BF)
                    PR[r, (2 * pair + which) * 2 + block] = probs
                    part = tn(probs, V[r, span, lanes]) * keep.astype(F32)
                    total = part if total is None else total + part
                CTX[r, span, lanes] = total.astype(BF)
        at("att", 3, r, {0: [copy.start for copy in not_urgent]})
        ACC[...] += nn(CTX[r, :, :local], MW[r])
        return 0

    lax.fori_loop(0, 4, attend, 0)

    hat, scale = norm_stats(ACC[...])
    HAT[...] = hat
    SCALE[...] = scale
    normed = hat * gain_ref[0:1, :].astype(F32) + nshift_ref[0:1, :].astype(F32)
    NB[...] = normed.astype(BF)
    ACC[...] = normed + rs_ref[...].reshape(1, width).astype(F32)
    keep_own[2].wait()
    keep_own[3].wait()

    def feed(r, _):
        at("feed", 0, r, {1: [give_own[2].wait_recv, give_own[3].wait_recv]})
        pre = nn(NB[...], EW[r]) + SM[r, 2:3, :]
        gate = 0.5 * (1.0 + lax.erf(pre * (0.5 ** 0.5)))
        AS[r, :rows] = (pre * gate).astype(BF)
        AS[r, rows:] = (
            gate + pre * (jnp.exp(-0.5 * (pre * pre)) * (1.0 / math.sqrt(2.0 * math.pi)))
        ).astype(BF)
        at("feed", 1, r)
        ACC[...] += nn(AS[r, :rows], RW[r])
        return 0

    lax.fori_loop(0, 4, feed, 0)

    fetch_cot.wait()
    hat, scale = norm_stats(ACC[...])
    gain = gain_ref[1:2, :].astype(F32)
    result = (hat * gain + nshift_ref[1:2, :].astype(F32)).astype(BF)
    perm = (iota((rows, rows), 1) == ((iota((rows, rows), 0) + begin) & (rows - 1))).astype(BF)
    RESULT[...] = result
    cot = nn(perm, GB[...])
    grad = norm_back(cot, hat, scale, gain)
    ACC[...] = grad
    GB[...] = grad.astype(BF)
    shared_two = (
        jnp.sum(cot * hat, axis=0, keepdims=True),
        jnp.sum(cot, axis=0, keepdims=True),
        jnp.sum(grad, axis=0, keepdims=True),
    )
    for n, line in enumerate(shared_two):
        SUMS[0, SHARED + 3 + n : SHARED + 4 + n, :] = line

    for (name, *_), piece in zip(PIECES, pieces):
        if name in ("ew", "rw"):
            piece.sent()

    def reduce_back(i, _):
        r = 3 - i
        grad_pre = (nt(GB[...], RW[r]) * AS[r, rows:].astype(F32)).astype(BF)
        AS[r, rows:] = grad_pre
        SUMS[r, 0:1, :] = jnp.sum(grad_pre.astype(F32), axis=0, keepdims=True)
        at("fa", 0, r)
        RW[r] = tn(GB[...], AS[r, :rows]).astype(BF)
        at("fa", 1, r)
        return 0

    lax.fori_loop(0, 4, reduce_back, 0)

    def expand_back(i, _):
        r = 3 - i
        ACC[...] += nt(AS[r, rows:], EW[r])
        at("fb", 0, r)
        EW[r] = tn(NB[...], AS[r, rows:]).astype(BF)
        at("fb", 1, r)
        return 0

    lax.fori_loop(0, 4, expand_back, 0)

    grad = ACC[...]
    hat = HAT[...]
    gone = norm_back(grad, hat, SCALE[...], gain_ref[0:1, :].astype(F32))
    ACC[...] = gone
    GB[...] = gone.astype(BF)
    shared_one = (
        jnp.sum(grad * hat, axis=0, keepdims=True),
        jnp.sum(grad, axis=0, keepdims=True),
        jnp.sum(gone, axis=0, keepdims=True),
    )
    for n, line in enumerate(shared_one):
        SUMS[0, SHARED + n : SHARED + 1 + n, :] = line

    at("lnb", 0)

    def attend_back(i, _):
        r = 3 - i

        GC[:, :local] = nt(GB[...], MW[r]).astype(BF)
        at("ab", 0, r)
        for block in range(2):
            span = slice(block * half, (block + 1) * half)
            for pair in range(2):
                lanes = slice(pair * 128, (pair + 1) * 128)
                key_side = jnp.concatenate([K[r, span, lanes], HOT[span, :]], axis=1)
                sums = None
                for which in range(min(2, heads - 2 * pair)):
                    keep = half_lanes(which)
                    wide = keep.astype(F32)
                    probs = PR[r, (2 * pair + which) * 2 + block]
                    grad_probs = nt(V[r, span, lanes] * keep, GC[span, lanes])
                    soft = probs.astype(F32)
                    inner = jnp.sum(soft * grad_probs, axis=0, keepdims=True)
                    grad_scores = (soft * (grad_probs - inner)).astype(BF)
                    both = tn(grad_scores, key_side)
                    parts = (
                        both[:, :128] * wide,
                        both[:, 128:] * wide,
                        nn(grad_scores, Q[r, span, lanes]) * wide,
                        nn(probs, GC[span, lanes]) * wide,
                    )
                    sums = parts if sums is None else tuple(a + b for a, b in zip(sums, parts))
                DQ[span, lanes] = (sums[0] * (HEAD_DIM ** -0.5)).astype(BF)
                E[span, lanes] = sums[1].astype(BF)
                DK[span, lanes] = sums[2].astype(BF)
                DV[span, lanes] = sums[3].astype(BF)
            at("ab", 1 + block, r)
        for m, ref in enumerate((DQ, DK, DV)):
            DD[:, (m + 1) * local : (m + 2) * local] = ref[:, :local]
            ACC[...] += nn(ref[:, :local], AW[r, m])
        weight_grad = tn(XR[...], DD[...])
        AS[r, :width, 256:] = weight_grad[:, 256:].astype(BF)
        AS[r, :width, :256] = (weight_grad[:, :256] + tn(GB[...], CTX[r])).astype(BF)
        SUMS[r, 1:2, :local] = jnp.sum(DQ[:, :local].astype(F32), axis=0, keepdims=True)
        SUMS[r, 2:3, :local] = jnp.sum(DV[:, :local].astype(F32), axis=0, keepdims=True)
        grad_pairs = tn(BACK[...], E[...])
        lanes_at = iota((BUCKETS, 128), 1)
        for h in range(heads):
            for a in range(2):
                off = (h % 2) * HEAD_DIM + a * BUCKETS
                part = grad_pairs[a * BUCKETS : (a + 1) * BUCKETS, (h // 2) * 128 : (h // 2 + 1) * 128]
                part = jnp.where((lanes_at >= off) & (lanes_at < off + BUCKETS), part, 0.0)
                part = pltpu.roll(part, (129 - BUCKETS - off) % 128, axis=1, stride=1, stride_axis=0)
                SUMS[r, 3 + 2 * h + a : 4 + 2 * h + a, :128] = jnp.sum(part, axis=0, keepdims=True)
        at("ab", 3, r)
        return 0

    SUMS[1, shared, :] = SUMS[0, shared, :]
    lax.fori_loop(0, 4, attend_back, 0)

    at("fin", 0)
    perm = (iota((rows, rows), 1) == ((iota((rows, rows), 0) + begin) & (rows - 1))).astype(BF)
    GB[...] = tn(perm, ACC[...].astype(BF)).astype(BF)
    RESULT[...] = tn(perm, RESULT[...]).astype(BF)
    leave = [
        pltpu.make_async_copy(source, target, local_sems.at[6 + n])
        for n, (source, target) in enumerate(
            ((RESULT, out_hbm), (GB, gin_hbm), (GEW, gew_hbm), (GRW, grw_hbm))
        )
    ]
    leave[0].start()
    leave[1].start()
    at("end", 0)
    leave[2].start()
    leave[3].start()
    gmw_ref[...] = jnp.transpose(MIX[:, :256])[:local, :]
    for m in range(3):
        gaw_ref[m] = MIX[:, (m + 1) * local : (m + 2) * local]
    both_ref[...] = SUMS[0]
    for row in range(2 * heads):
        both_ref[3 + row : 4 + row, :BUCKETS] = lax.dot_general(
            both_ref[3 + row : 4 + row, :128], fold_f32, (((1,), (1,)), ((), ())),
            precision=lax.Precision.HIGHEST, preferred_element_type=F32,
        )

    for stages in flows.values():
        for stage in stages.values():
            stage.sent()
    for unit in range(3):
        for slot in (1, 3):
            to_core(unit, slot).wait_send()
    for copy in sums_core + sums_far[:1]:
        copy.wait_send()
    for (name, *_), piece in zip(PIECES, pieces):
        if name not in ("ew", "rw"):
            piece.sent()
    for copy in give_own + [small_core, small_y, small_far]:
        copy.wait_send()
    for copy in leave:
        copy.wait()


def swap(value, axis, size, bit):
    return lax.ppermute(value, axis, [(i, i ^ bit) for i in range(size)])


def finish_rows(value, dp, bits_done):
    me = lax.axis_index("dp")
    left = dp.bit_length() - 1 - bits_done
    rows, cols = value.shape
    value = value.reshape((2,) * left + (rows >> left, cols))
    for bit in range(left):
        axis = value.ndim - 3
        mine = (me >> bit) & 1
        keep = lax.dynamic_index_in_dim(value, mine, axis, keepdims=False)
        send = lax.dynamic_index_in_dim(value, 1 - mine, axis, keepdims=False)
        value = keep + swap(send, "dp", dp, 1 << bit)
    return value


def finish_kernel(*refs):
    sources, both, targets, small = refs[:6], refs[6], refs[7:13], refs[13:20]
    for source, target in zip(sources, targets):
        target[...] = source[...]
    shifts, merge, gains, norm_shift, expand, reduced, tables = small
    shifts[...] = both[1:3, : shifts.shape[1]]
    for target, row in ((merge, SHARED + 2), (expand, 0), (reduced, SHARED + 5)):
        target[...] = both[row : row + 1, :].reshape(target.shape)
    for target, row in ((gains, SHARED), (norm_shift, SHARED + 1)):
        target[0:1, :] = both[row : row + 1, :]
        target[1:2, :] = both[row + 3 : row + 4, :]
    for h in range(tables.shape[0]):
        tables[h] = both[3 + 2 * h : 5 + 2 * h, :BUCKETS]


def on_device(
    dp,
    inputs,
    layout_cells,
    page_lengths,
    attend_weight,
    attend_shift,
    merge_weight,
    merge_shift,
    norm_gains,
    norm_shifts,
    expand_weight,
    expand_shift,
    reduce_weight,
    reduce_shift,
    bias_tables,
    cotangent,
):
    rows, width = inputs.shape
    half = rows // 2
    local = attend_weight.shape[2]
    heads = bias_tables.shape[1]
    hidden = expand_weight.shape[1]
    top = dp.bit_length() - 1
    bits = (top - 3, top - 2, top - 1)

    sds = jax.ShapeDtypeStruct
    smem = pl.BlockSpec(memory_space=pltpu.SMEM)
    vmem = pl.BlockSpec(memory_space=pltpu.VMEM)
    hbm = pl.BlockSpec(memory_space=pl.ANY)

    def kernel(*refs):
        return layer_kernel(bits, *refs)

    dma = pltpu.SemaphoreType.DMA
    count = sum(len(order) + order.index("y") for chunks in CHUNKS for _, _, order in chunks)
    block = width // 8
    gaw, gmw, both, output, input_grad, gew, grw = pl.pallas_call(
        kernel,
        in_specs=[smem] + [vmem] * 8 + [hbm] * 6,
        out_specs=[vmem] * 3 + [hbm] * 4,
        out_shape=[
            sds((3, block, local), F32), sds((local, block), F32), sds((SMALL_ROWS, width), F32),
            sds((rows, width), BF), sds((rows, width), BF), sds((block, hidden), F32),
            sds((block, hidden), F32),
        ],
        scratch_shapes=[
            pltpu.VMEM((4, 3, local, width), BF),
            pltpu.VMEM((4, local, width), BF),
            pltpu.VMEM((4, width, hidden), BF),
            pltpu.VMEM((4, hidden, width), BF),
            pltpu.VMEM((rows, width), BF),
            pltpu.VMEM((rows, 128), BF),
            pltpu.VMEM((rows, 2 * BUCKETS), BF),
            pltpu.VMEM((4, rows, 256), BF),
            pltpu.VMEM((4, rows, 256), BF),
            pltpu.VMEM((4, rows, 256), BF),
            pltpu.VMEM((4, 2 * heads, half, half), BF),
            pltpu.VMEM((4, rows, 256), BF),
            pltpu.VMEM((rows, width), BF),
            pltpu.VMEM((rows, width), F32),
            pltpu.VMEM((rows, 1), F32),
            pltpu.VMEM((4, 2 * rows, hidden), BF),
            pltpu.VMEM((rows, width), F32),
            pltpu.VMEM((rows, width), BF),
            pltpu.VMEM((rows, 256), BF),
            pltpu.VMEM((rows, 256), BF),
            pltpu.VMEM((rows, 256), BF),
            pltpu.VMEM((rows, 256), BF),
            pltpu.VMEM((rows, 256), BF),
            pltpu.VMEM((rows, 4 * local), BF),
            pltpu.VMEM((4, SMALL_ROWS, hidden), F32),
            pltpu.VMEM((3, 2, width, hidden), BF),
            pltpu.VMEM((3, 15 * block, hidden), BF),
            pltpu.VMEM((block, hidden), F32),
            pltpu.VMEM((block, hidden), F32),
            pltpu.VMEM((block, width), F32),
            pltpu.VMEM((rows, width), BF),
            pltpu.VMEM((4, SMALL_ROWS, width), F32),
            pltpu.VMEM((2, SMALL_ROWS, width), F32),
            pltpu.VMEM((4, SMALL_ROWS, width), F32),
            dma((2, 4 * len(PIECES))), dma((2, 4)), dma((2, 3)), dma((10,)),
            dma((2, 6)), dma((2, count)), dma((2, 6)),
        ],
        compiler_params=pltpu.CompilerParams(
            collective_id=0, has_side_effects=True, vmem_limit_bytes=VMEM_LIMIT
        ),
    )(
        page_lengths, layout_cells, attend_shift, expand_shift,
        jnp.transpose(bias_tables, (1, 0, 2)), merge_shift, reduce_shift, norm_gains, norm_shifts,
        jnp.transpose(attend_weight, (0, 2, 1)), merge_weight, expand_weight, reduce_weight, cotangent,
        inputs,
    )

    if top > 3:
        grw = finish_rows(grw, dp, 3)
        gew = finish_rows(gew, dp, 3)
        gmw = finish_rows(gmw.T, dp, 3).T
        gaw = jnp.stack([finish_rows(gaw[m], dp, 3) for m in range(3)])
        for bit in range(top - 3):
            both = both + swap(both, "dp", dp, 1 << bit)
    big = (output, input_grad, gaw, gmw, gew, grw)
    done = pl.pallas_call(
        finish_kernel,
        in_specs=[vmem] * 7,
        out_specs=[vmem] * 13,
        out_shape=[sds(a.shape, a.dtype) for a in big]
        + [
            sds((2, local), F32), sds((width,), F32), sds((2, width), F32), sds((2, width), F32),
            sds((hidden,), F32), sds((width,), F32), sds((heads, 2, BUCKETS), F32),
        ],
    )(*big, both)
    output, input_grad, gaw, gmw, gew, grw, shifts, merge, gains, norm_shift, expand, reduced, tables = done
    return (
        output, input_grad, gaw, shifts, gmw, merge, gains, norm_shift, gew, expand, grw.T, reduced,
        jnp.transpose(tables, (1, 0, 2)),
    )


def solution(mesh):
    in_specs = (
        P(("dp", "tensor"), None),
        P(None, "dp"),
        P("dp", None),
        P(None, None, "tensor"),
        P(None, "tensor"),
        P("tensor", None),
        P(),
        P(),
        P(),
        P(None, "tensor"),
        P("tensor"),
        P("tensor", None),
        P(),
        P(None, "tensor", None),
        P(("dp", "tensor"), None),
    )
    out_specs = (
        P(("dp", "tensor"), None),
        P(("dp", "tensor"), None),
        P(None, "dp", "tensor"),
        P(None, "tensor"),
        P("tensor", "dp"),
        P(),
        P(),
        P(),
        P("dp", "tensor"),
        P("tensor"),
        P("tensor", "dp"),
        P(),
        P(None, "tensor", None),
    )

    def run(*arrays):
        return on_device(mesh.shape["dp"], *arrays)

    return jax.shard_map(
        run, mesh=mesh, in_specs=in_specs, out_specs=out_specs, check_vma=False
    )
```
